32 devices in a mesh: groups: 2 (over y), cells: 4 (over z), sect: 2 (over x), lev: 2 (over core).
Axes of the slice: x: 2, y: 2, z: 4, core: 2. Of those that a mesh axis runs over, the one named last changes fastest.
Arguments:
- spectrum: bfloat16 [1152, 32, 256], P(('cells', 'lev'), 'groups', 'sect'), parts along dimension 1, may hold values from -6 to 6
- courant_x: float32 [1152], P(('cells', 'lev')), may hold values from -0.45 to 0.45
- courant_y: float32 [1152], P(('cells', 'lev')), may hold values from -0.45 to 0.45
- growth: float32 [1152], replicated, may hold values from 0.5 to 2
- quartet: bfloat16 [1152, 1152], replicated, may hold values from -0.1875 to 0.1875
- coupler: bfloat16 [128, 1152], replicated, may hold values from -0.1875 to 0.1875
- atmosphere: float32 [64, 32, 256], P('lev', ('groups', 'cells'), 'sect'), parts along dimension 1, may hold values from -6 to 6
- ocean_state: float32 [64, 32, 256], P('lev', ('groups', 'cells'), 'sect'), parts along dimension 1, may hold values from -6 to 6
- sea_mask: int32 [32, 256], P(('groups', 'cells'), 'sect'), parts along dimension 0, may hold values 0 or 1
Outputs:
- spectrum_out: bfloat16 [1152, 32, 256], P(('cells', 'lev'), 'groups', 'sect'), parts along dimension 1
- atmosphere_out: float32 [64, 32, 256], P('lev', ('groups', 'cells'), 'sect'), parts along dimension 1
- ocean_out: float32 [64, 32, 256], P('lev', ('groups', 'cells'), 'sect'), parts along dimension 1
The draws below stay inside these ranges and needn't reach their ends.
There are 2 independent parts, one for each index of `groups`. The reference program is written for one: setup_inputs(seed, part) draws one part's arguments, and reference() takes and returns one part's arrays. A program takes and returns all parts, laid end to end along the dimension named above; an argument that names none is the same for every part. Nothing has to cross between parts.
Inputs may be any that keep to these rules, and one draw needn't show every extreme that they name: `sea_mask`: 1 marks a sea cell, 0 a land cell.
All inputs are finite; a program needn't handle non-finite values. No bound on the sum of `sea_mask` on one device may be relied on, other than what follows from the above.
Results may differ from the reference program's by a relative error of at most 0.0062.
Values may be sent and summed in bfloat16 or wider, within the bound.
A program may use at most 64 MiB of HBM per device.

```python
import math
import jax
import jax.numpy as jnp
from jax import lax

COMPS = 1152
LEVELS = 64
NSTEP = 2
GRID_Y = 16
GRID_X = 256


def place_ends(entries, stream_key, low, largest):
    shape = entries.shape
    spot = [jax.random.randint(jax.random.fold_in(stream_key, axis), (), 0, shape[axis]) for axis in range(len(shape))]
    entries = entries.at[tuple(spot)].set(low)
    longest = shape.index(max(shape))
    spot[longest] = (spot[longest] + 1) % shape[longest]
    return entries.at[tuple(spot)].set(largest)


def level_of(own_key, extent, split, smallest, high):
    def one(position, parts):
        draws = jax.random.uniform(jax.random.fold_in(jax.random.fold_in(own_key, 6), position), (parts,), jnp.float32, smallest / len(split), high / len(split))
        return jnp.repeat(jnp.exp(draws), extent[position] // parts).reshape((-1,) + (1,) * (len(extent) - position - 1))

    level = one(*split[0])
    for cut in split[1:]:
        level = level * one(*cut)
    return level


def centred(key, dims, deviation, reach, pieces=(), kind=jnp.bfloat16):
    values = deviation * jax.random.normal(key, dims, jnp.float32)
    if pieces:
        values = values * level_of(key, dims, pieces, -0.22, 0.18)
    return jnp.clip(values, -reach, reach).astype(kind)


def setup_inputs(seed: int = 0, part: int = 0) -> dict:
    arg_keys = jax.random.split(jax.random.key(seed), 10)
    own_keys = jax.random.split(jax.random.fold_in(arg_keys[9], part), 10)
    spectrum = centred(own_keys[0], (COMPS, GRID_Y, GRID_X), 1.0, 6.0, ((0, 8), (2, 2)))
    courant_x = jnp.clip(jax.random.uniform(arg_keys[1], (COMPS,), jnp.float32, -0.45, 0.45) * level_of(arg_keys[1], (COMPS,), ((0, 8),), -0.4, 0.0), -0.45, 0.45)
    courant_y = jnp.clip(jax.random.uniform(arg_keys[2], (COMPS,), jnp.float32, -0.45, 0.45) * level_of(arg_keys[2], (COMPS,), ((0, 8),), -0.4, 0.0), -0.45, 0.45)
    growth = jnp.clip(jnp.exp(jax.random.uniform(arg_keys[3], (COMPS,), jnp.float32, math.log(0.5), math.log(2.0))), 0.5, 2.0)
    quartet = centred(arg_keys[4], (COMPS, COMPS), COMPS ** -0.5, 0.1875)
    coupler = centred(arg_keys[5], (2 * LEVELS, COMPS), COMPS ** -0.5, 0.1875)
    atmosphere = centred(own_keys[6], (LEVELS, GRID_Y, GRID_X), 1.0, 6.0, ((0, 2), (1, 4), (2, 2)), jnp.float32)
    ocean_state = centred(own_keys[7], (LEVELS, GRID_Y, GRID_X), 1.0, 6.0, ((0, 2), (1, 4), (2, 2)), jnp.float32)
    sea_mask = place_ends((jax.random.randint(own_keys[8], (GRID_Y, GRID_X), 0, 4) < 3).astype(jnp.int32), jax.random.fold_in(own_keys[8], 1), 0, 1)
    return {"spectrum": spectrum, "courant_x": courant_x, "courant_y": courant_y, "growth": growth, "quartet": quartet, "coupler": coupler, "atmosphere": atmosphere, "ocean_state": ocean_state, "sea_mask": sea_mask}


def upwind(values, courant, before, after):
    return jnp.maximum(courant, 0.0) * (values - before) + jnp.minimum(courant, 0.0) * (after - values)


def column_update(state, forcing, factor):
    padded = jnp.pad(state, 1)
    middle = padded[1:-1, 1:-1, 1:-1]
    lateral = padded[1:-1, 2:, 1:-1] + padded[1:-1, :-2, 1:-1] + padded[1:-1, 1:-1, 2:] + padded[1:-1, 1:-1, :-2] - 4.0 * middle
    upright = padded[2:, 1:-1, 1:-1] + padded[:-2, 1:-1, 1:-1] - 2.0 * middle
    return middle + 0.1 * lateral + 0.1 * upright + factor * forcing


def reference(spectrum, courant_x, courant_y, growth, quartet, coupler, atmosphere, ocean_state, sea_mask):
    highest = lax.Precision.HIGHEST
    weights = quartet.astype(jnp.float32)
    couple_full = coupler.astype(jnp.float32)
    shift_x = courant_x[:, None, None]
    shift_y = courant_y[:, None, None]
    sea_float = sea_mask.astype(jnp.float32).reshape(1, GRID_Y * GRID_X)
    energy = spectrum
    for counter in range(NSTEP):
        surface_wind = atmosphere[0] - ocean_state[0]
        wind_input = (surface_wind * surface_wind).reshape(1, GRID_Y * GRID_X)
        values = energy.astype(jnp.float32)
        moved = values - upwind(values, shift_x, jnp.roll(values, 1, axis=2), jnp.roll(values, -1, axis=2))
        moved = moved - upwind(values, shift_y, jnp.roll(values, 1, axis=1), jnp.roll(values, -1, axis=1))
        advected = lax.optimization_barrier(moved.astype(jnp.bfloat16)).astype(jnp.float32)
        advected = advected.reshape(COMPS, GRID_Y * GRID_X)
        paired = jnp.dot(weights, advected, precision=highest)
        squared = lax.optimization_barrier((advected * advected).astype(jnp.bfloat16)).astype(jnp.float32)
        quad_square = jnp.dot(weights, squared, precision=highest)
        fresh = (advected + 0.3 * (advected * paired - quad_square) + 0.1 * growth[:, None] * wind_input) / (1.0 + 0.1 * advected * advected)
        fresh = (fresh * sea_float).astype(jnp.bfloat16)
        fresh_float = lax.optimization_barrier(fresh).astype(jnp.float32)
        profile = jnp.dot(couple_full, fresh_float, precision=highest).reshape(2, LEVELS, GRID_Y, GRID_X)
        atmosphere = column_update(atmosphere, profile[0], -0.3)
        ocean_state = column_update(ocean_state, profile[1], 0.3)
        energy = fresh.reshape(COMPS, GRID_Y, GRID_X)
    return energy, atmosphere, ocean_state
```

```python
import functools

import jax
import jax.numpy as jnp
from jax import lax
from jax.experimental import pallas as pl
from jax.experimental.pallas import tpu as pltpu
from jax.sharding import PartitionSpec as P

NSTEP = 2
LANES = 128
F32 = jnp.float32
BF16 = jnp.bfloat16


def from_root(block, axis, source):
    block = jnp.where(lax.axis_index(axis) == source, block, jnp.zeros_like(block))
    return lax.psum(block, axis)


def extended_2(block, sides, width, periodic):
    for axis, dim in sides:
        count = lax.axis_size(axis)
        forward = [(i, i + 1) for i in range(count - 1)]
        if periodic:
            forward.append((count - 1, 0))
        backward = [(target, source) for source, target in forward]
        low = lax.ppermute(
            lax.slice_in_dim(block, block.shape[dim] - width, None, axis=dim), axis, forward
        )
        high = lax.ppermute(lax.slice_in_dim(block, 0, width, axis=dim), axis, backward)
        block = jnp.concatenate([low, block, high], axis=dim)
    return block


def upwind(values, courant, before, after):
    return jnp.maximum(courant, 0.0) * (values - before) + jnp.minimum(courant, 0.0) * (
        after - values
    )


def on_device(
    spectrum, courant_x, courant_y, growth, quartet, coupler, atmosphere, ocean_state, sea_mask
):
    cell_tiles = lax.axis_size("cells")
    lev_parts = lax.axis_size("lev")
    blocks = cell_tiles * lev_parts
    comps_own, rows_all, row_width = spectrum.shape
    total_comps = comps_own * blocks
    cell_rows = rows_all // blocks
    level_count = coupler.shape[0] // 2
    row_start = lax.axis_index("lev") * cell_rows
    shift_x = courant_x[:, None, None]
    shift_y = courant_y[:, None, None]
    sea_rows = (
        lax.dynamic_slice_in_dim(sea_mask, row_start, cell_rows, 0)
        .astype(jnp.float32)
        .reshape(1, cell_rows * row_width)
    )
    growth_column = growth[:, None]
    forcing_sign = jnp.array([-0.3, 0.3], jnp.float32)[:, None, None, None]
    state = jnp.stack([atmosphere, ocean_state])
    energy = spectrum
    for counter in range(NSTEP):
        surface = from_root(state[:, 0], "lev", 0)
        surface_wind = surface[0] - surface[1]
        wind_rows = lax.dynamic_slice_in_dim(
            surface_wind * surface_wind, row_start, cell_rows, 0
        ).reshape(1, cell_rows * row_width)
        padded = extended_2(energy, (("sect", 2),), 1, True)
        values = padded[:, :, 1:-1].astype(jnp.float32)
        west_side = padded[:, :, :-2].astype(jnp.float32)
        east_side = padded[:, :, 2:].astype(jnp.float32)
        moved = values - upwind(values, shift_x, west_side, east_side)
        moved = moved - upwind(
            values, shift_y, jnp.roll(values, 1, axis=1), jnp.roll(values, -1, axis=1)
        )
        advected = moved.astype(jnp.bfloat16)
        pieces = advected.reshape(1, comps_own, blocks, cell_rows, row_width)
        on_cells = lax.all_to_all(pieces, ("cells", "lev"), split_axis=2, concat_axis=0, tiled=True)
        on_cells = on_cells.reshape(total_comps, cell_rows * row_width)
        cell_values = on_cells.astype(jnp.float32)
        paired = jnp.dot(quartet, on_cells, preferred_element_type=jnp.float32)
        squared = (cell_values * cell_values).astype(jnp.bfloat16)
        quad_square = jnp.dot(quartet, squared, preferred_element_type=jnp.float32)
        fresh = (
            cell_values
            + 0.3 * (cell_values * paired - quad_square)
            + 0.1 * growth_column * wind_rows
        ) / (1.0 + 0.1 * cell_values * cell_values)
        fresh = (fresh * sea_rows).astype(jnp.bfloat16)
        profile = jnp.dot(coupler, fresh, preferred_element_type=jnp.float32).reshape(
            2, level_count, cell_rows, row_width
        )
        forcing = lax.all_to_all(profile, "lev", split_axis=1, concat_axis=2, tiled=True)
        returned = fresh.reshape(blocks, comps_own, 1, cell_rows, row_width)
        returned = lax.all_to_all(
            returned, ("cells", "lev"), split_axis=0, concat_axis=2, tiled=True
        )
        energy = returned.reshape(comps_own, rows_all, row_width)
        extended = extended_2(state, (("lev", 1), ("cells", 2), ("sect", 3)), 1, False)
        middle = extended[:, 1:-1, 1:-1, 1:-1]
        lateral = (
            extended[:, 1:-1, 2:, 1:-1]
            + extended[:, 1:-1, :-2, 1:-1]
            + extended[:, 1:-1, 1:-1, 2:]
            + extended[:, 1:-1, 1:-1, :-2]
            - 4.0 * middle
        )
        upright = extended[:, 2:, 1:-1, 1:-1] + extended[:, :-2, 1:-1, 1:-1] - 2.0 * middle
        state = middle + 0.1 * lateral + 0.1 * upright + forcing_sign * forcing
    return (energy, state[0], state[1])


def column_of(row):
    n = row.shape[1]
    down = lax.broadcasted_iota(jnp.int32, (n, n), 0)
    across = lax.broadcasted_iota(jnp.int32, (n, n), 1)
    return jnp.sum(jnp.where(down == across, row, 0.0), axis=1, keepdims=True)


def swap_groups(vectors, seg):
    count = len(vectors)
    width = vectors[0].shape[1]
    group = lax.broadcasted_iota(jnp.int32, vectors[0].shape, 1) // seg
    dist = count // 2
    vectors = list(vectors)
    while dist:
        even = (group // dist) % 2 == 0
        for i in range(count):
            if (i // dist) % 2 == 0:
                x, y = vectors[i], vectors[i + dist]
                vectors[i] = jnp.where(even, x, pltpu.roll(y, dist * seg, 1))
                vectors[i + dist] = jnp.where(even, pltpu.roll(x, width - dist * seg, 1), y)
        dist //= 2
    return vectors


def fused_kernel(
    cell_tiles, lev_parts, sect_tiles,
    spec_hbm, cx_hbm, cy_hbm, growth_hbm, quartet_hbm, coupler_hbm, atm_hbm, oce_hbm, sea_hbm,
    ret, fin,
    spec_v, cx_v, cy_v, growth_v, quartet_v, coupler_v, col_in, sea_v,
    flat, rows_v, send_f, cell_f, cell_s, cx_all, cy_all, cxb, cyb, grow_b,
    edge_send, edge_recv, e1, rim, halo_n, halo_s, e2,
    swap_send, st_in, sea_send, sea_in, outer, inner, st0, st1, st2, st_edge_send, st_edge_recv, st_halo, st_back,
    in_sem, out_sem, own_sem, f_send, f_recv, c_send, c_recv,
    edge_ss, edge_rs, row_ss, row_rs, swap_ss, swap_rs, back_ss, back_rs, ste_ss, ste_rs, sth_ss, sth_rs,
    ret_ss, ret_rs,
):
    blocks = cell_tiles * lev_parts
    comps, rows, width = spec_v.shape
    cell_rows = rows // blocks
    lown = col_in.shape[1]
    levels = lown * lev_parts
    seg = width // cell_tiles
    mine_c = lax.axis_index("cells")
    mine_l = lax.axis_index("lev")
    mine_x = lax.axis_index("sect")
    me = mine_c * lev_parts + mine_l
    turned = lax.rem(mine_x, 2) == 1

    def swapped(c):
        return jnp.where(turned, cell_tiles - 1 - c, c)

    mine_t = swapped(mine_c)
    spot_t = mine_t * lev_parts + mine_l
    half = cell_tiles // 2
    side = lax.div(mine_c, half)
    west = {"sect": lax.rem(mine_x + sect_tiles - 1, sect_tiles)}
    east = {"sect": lax.rem(mine_x + 1, sect_tiles)}
    partner = {"lev": 1 - mine_l}
    near_west = {
        "cells": jnp.where(mine_t == 0, mine_c, swapped(mine_t - 1)),
        "sect": jnp.where(mine_t == 0, west["sect"], mine_x),
    }
    near_east = {
        "cells": jnp.where(mine_t == cell_tiles - 1, mine_c, swapped(mine_t + 1)),
        "sect": jnp.where(mine_t == cell_tiles - 1, east["sect"], mine_x),
    }

    def block_id(b):
        return {"cells": lax.div(b, lev_parts), "lev": lax.rem(b, lev_parts)}

    def peer(d):
        return lax.rem(me + d, blocks)

    def part(b):
        return pl.ds(pl.multiple_of(b * comps, 16), comps)

    def remote(src, dst, ss, rs, where):
        return pltpu.make_async_remote_copy(
            src_ref=src, dst_ref=dst, send_sem=ss, recv_sem=rs,
            device_id=where, device_id_type=pl.DeviceIdType.MESH,
        )

    across = [jnp.where(side == 0, cell_tiles - 1 - i, i) for i in range(half)]
    mates = [side * half + lax.rem(mine_c - side * half + i, half) for i in range(1, half)]
    order = [c * lev_parts + lax.rem(mine_l + k, lev_parts)
             for c in across + mates for k in range(lev_parts)]
    order.extend(c for k in range(1, lev_parts) for c in [mine_c * lev_parts + lax.rem(mine_l + k, lev_parts)])

    loads = [
        pltpu.make_async_copy(a, b, in_sem.at[i])
        for i, (a, b) in enumerate([
            (spec_hbm, spec_v), (cx_hbm, cx_v), (cy_hbm, cy_v),
            (atm_hbm, col_in.at[0]), (oce_hbm, col_in.at[1]), (sea_hbm, sea_v),
            (growth_hbm, growth_v), (coupler_hbm, coupler_v), (quartet_hbm, quartet_v),
        ])
    ]
    for load in loads:
        load.start()

    barrier = pltpu.get_barrier_semaphore()
    for d in range(1, blocks):
        pl.semaphore_signal(barrier, inc=1, device_id=block_id(peer(d)),
                            device_id_type=pl.DeviceIdType.MESH)
    for side in (west, east, near_west, near_east):
        pl.semaphore_signal(barrier, inc=1, device_id=side,
                            device_id_type=pl.DeviceIdType.MESH)

    lane = lax.broadcasted_iota(jnp.int32, (comps, width), 1)
    loads[0].wait()
    flat[...] = spec_v[...].astype(F32).reshape(comps * rows, width)
    first = jnp.zeros((comps, width), F32)
    last = jnp.zeros((comps, width), F32)
    for r in range(rows):
        v = flat[pl.ds(r, comps, stride=rows), :]
        rows_v[r] = v
        spot = (r % cell_tiles) * seg + r // cell_tiles
        first = jnp.where(lane == spot, pltpu.roll(v, spot, 1), first)
        last = jnp.where(lane == spot, pltpu.roll(v, (spot + 1) % width, 1), last)
    edge_send[0, 0] = first.astype(BF16)
    edge_send[0, 1] = last.astype(BF16)

    pl.semaphore_wait(barrier, blocks + 3)
    pending = []

    def send_edges(step):
        copies = [
            remote(edge_send.at[step, i], edge_recv.at[step, i],
                   edge_ss.at[step, i], edge_rs.at[step, i], side)
            for i, side in enumerate((west, east) if step == 0 else (near_west, near_east))
        ]
        for copy in copies:
            copy.start()
        pending.extend(copies)
        return copies

    edges = send_edges(0)

    loads[1].wait()
    loads[2].wait()
    for d, b in enumerate(order):
        to = block_id(b)
        for i, (src, dst) in enumerate(((cx_v, cx_all), (cy_v, cy_all))):
            copy = remote(src, dst.at[me], c_send.at[i, d], c_recv.at[i, me], to)
            copy.start()
            pending.append(copy)

    home = lax.div(mine_c, cell_rows)
    slot_h = lax.rem(mine_c, cell_rows)
    my_levels = pl.ds(pl.multiple_of(mine_l * lown, 16), lown)

    def state_in(dc):
        c = lax.rem(mine_c + dc, cell_tiles)
        return remote(swap_send.at[swapped(c)], st_in.at[:, slot_h, my_levels, :], swap_ss.at[0, dc],
                      swap_rs.at[0, slot_h, mine_l], {"cells": c, "lev": home})

    def sea_over(dc):
        c = lax.rem(mine_c + dc, cell_tiles)
        return remote(sea_send.at[swapped(c)], sea_in.at[slot_h], swap_ss.at[1, dc],
                      swap_rs.at[1, slot_h, 0], {"cells": c, "lev": home})

    def send_state_in():
        loads[3].wait()
        loads[4].wait()
        loads[5].wait()
        for f in range(2):
            lines = [col_in[f, :, r, :] for r in range(cell_tiles)]
            for c, line in enumerate(swap_groups(lines, seg)):
                swap_send[c, f] = line.astype(BF16)
        lines = [jnp.broadcast_to(sea_v[r:r + 1, :].astype(F32), (8, width)) for r in range(cell_tiles)]
        for c, line in enumerate(swap_groups(lines, seg)):
            sea_send[c] = line[0:1]
        for dc in range(1, cell_tiles):
            copy = state_in(dc)
            copy.start()
            pending.append(copy)

        @pl.when(home == mine_l)
        def _():
            for dc in range(1, cell_tiles):
                sea_over(dc).start()
            for f in range(2):
                st_in[f, slot_h, my_levels, :] = swap_send[mine_t, f]
            sea_in[slot_h] = sea_send[mine_t]

        @pl.when(home != mine_l)
        def _():
            state_in(0).start()

    def halves(c):
        return jnp.maximum(c, 0.0), jnp.maximum(-c, 0.0)

    cx = jnp.broadcast_to(column_of(cx_v[...]), (comps, width))
    cy = jnp.broadcast_to(column_of(cy_v[...]), (comps, width))
    cxb[part(me), :] = cx
    cyb[part(me), :] = cy
    px, mx = halves(cx)
    py, my = halves(cy)
    keep = 1.0 - jnp.abs(cx) - jnp.abs(cy)

    far = sorted(range(cell_tiles), key=lambda d: abs(d - cell_tiles // 2))

    def send_piece(c, core):
        b = c * lev_parts + core
        t = swapped(c) * lev_parts + core

        @pl.when(b != me)
        def _():
            remote(send_f.at[t], cell_f.at[part(me), :], f_send.at[b], f_recv.at[me], block_id(b)).start()

        @pl.when(b == me)
        def _():
            cell_f[part(me), :] = send_f[spot_t]

    at_rim = (mine_c == 0) | (mine_c == cell_tiles - 1)
    middle = [jnp.where(side == 0, c, cell_tiles - 1 - c) for c in range(cell_tiles - 2, 0, -1)]
    ends = [jnp.where(side == 0, cell_tiles - 1, 0), jnp.where(side == 0, 0, cell_tiles - 1)]

    for k in (1, 0):
        core = lax.rem(mine_l + k, lev_parts)
        for h in range(cell_rows):
            lines = []
            for g in range(cell_tiles):
                row = (core * cell_rows + h) * cell_tiles + g
                v = rows_v[row]
                to_west = jnp.where(lane == 0, 0.0, pltpu.roll(v, 1, 1))
                to_east = jnp.where(lane == width - 1, 0.0, pltpu.roll(v, width - 1, 1))
                lines.append(
                    v * keep + px * to_west + mx * to_east
                    + py * rows_v[lax.rem(row + rows - 1, rows)] + my * rows_v[lax.rem(row + 1, rows)]
                )
            for c, line in enumerate(swap_groups(lines, seg)):
                if 0 < c < cell_tiles - 1:
                    send_f[c * lev_parts + core, :, h * width:(h + 1) * width] = line.astype(BF16)
                else:
                    outer[min(c, 1), core * cell_rows + h] = line
        send_piece(middle[0], core)

        @pl.when(jnp.logical_not(at_rim))
        def _():
            send_piece(middle[1], core)
    send_state_in()
    for copy in edges:
        copy.wait_recv()
    from_east = edge_recv[0, 0].astype(F32)
    from_west = edge_recv[0, 1].astype(F32)
    place_c = lane % seg
    for k in (1, 0):
        core = lax.rem(mine_l + k, lev_parts)
        for h in range(cell_rows):
            band = core * cell_rows + h
            cut = slice(h * width, (h + 1) * width)
            west_part = jnp.where(place_c == 0, pltpu.roll(from_west, lax.rem(width - band, width), 1), 0.0)
            east_part = jnp.where(place_c == seg - 1, pltpu.roll(from_east, seg - 1 - band, 1), 0.0)
            send_f[core, :, cut] = (outer[0, band] + px * west_part).astype(BF16)
            send_f[(cell_tiles - 1) * lev_parts + core, :, cut] = (
                outer[1, band] + mx * east_part
            ).astype(BF16)
        send_piece(ends[0], core)

    @pl.when(at_rim)
    def _():
        for k in (1, 0):
            send_piece(middle[1], lax.rem(mine_l + k, lev_parts))
    for k in (1, 0):
        send_piece(ends[1], lax.rem(mine_l + k, lev_parts))

    level_id = lax.broadcasted_iota(jnp.int32, (levels, width), 0)
    level_lane = lax.broadcasted_iota(jnp.int32, (levels, width), 1)

    place = level_lane % seg

    def send_state(state, step):
        west_pack = jnp.zeros((levels, width), F32)
        east_pack = jnp.zeros((levels, width), F32)
        for f in range(2):
            for r in range(cell_rows):
                slot = f * cell_rows + r
                v = state[f, r]
                west_pack = jnp.where(place == slot, pltpu.roll(v, slot, 1), west_pack)
                east_pack = jnp.where(place == slot, pltpu.roll(v, (slot + 1 - seg) % width, 1), east_pack)
        st_edge_send[step, 0] = west_pack
        st_edge_send[step, 1] = east_pack
        copies = []
        for i, side in enumerate((near_west, near_east)):
            copies.append(remote(st_edge_send.at[step, i], st_edge_recv.at[step, i],
                                 ste_ss.at[step, i], ste_rs.at[step, i], side))
        for i, row in enumerate((0, cell_rows - 1)):
            copies.append(remote(state.at[0:2, row], st_halo.at[step, i],
                                 sth_ss.at[step, i], sth_rs.at[step, i], partner))
        for copy in copies:
            copy.start()
        pending.extend(copies)
        return copies

    def update(state, new, step, profile):
        rim_west = (mine_x == 0) & (mine_t == 0)
        rim_east = (mine_x == sect_tiles - 1) & (mine_t == cell_tiles - 1)
        west_pack = jnp.where(rim_west, 0.0, st_edge_recv[step, 1])
        east_pack = jnp.where(rim_east, 0.0, st_edge_recv[step, 0])
        for f in range(2):
            factor = -0.3 if f == 0 else 0.3
            south_row = jnp.where(mine_l == lev_parts - 1, 0.0, st_halo[step, 0, f])
            north_row = jnp.where(mine_l == 0, 0.0, st_halo[step, 1, f])
            for r in range(cell_rows):
                slot = f * cell_rows + r
                v = state[f, r]
                w = jnp.where(place == 0, pltpu.roll(west_pack, (width - slot) % width, 1), pltpu.roll(v, 1, 1))
                e = jnp.where(place == seg - 1, pltpu.roll(east_pack, (width + seg - 1 - slot) % width, 1),
                              pltpu.roll(v, width - 1, 1))
                n = north_row if r == 0 else state[f, r - 1]
                s = south_row if r == cell_rows - 1 else state[f, r + 1]
                n = pltpu.roll(jnp.where(level_lane >= width - seg, n, v), seg, 1)
                s = pltpu.roll(jnp.where(level_lane < seg, s, v), width - seg, 1)
                below = jnp.where(level_id == 0, 0.0, pltpu.roll(v, 1, 0))
                above = jnp.where(level_id == levels - 1, 0.0, pltpu.roll(v, levels - 1, 0))
                g = profile[f * levels:(f + 1) * levels, r * width:(r + 1) * width]
                new[f, r] = (v + 0.1 * (n + s + w + e - 4.0 * v)
                             + 0.1 * (above + below - 2.0 * v) + factor * g)

    loads[6].wait()
    for t in range(growth_v.shape[0] // LANES):
        column = column_of(growth_v[t * LANES:(t + 1) * LANES].reshape(1, LANES))
        grow_b[t * LANES:(t + 1) * LANES, :] = jnp.broadcast_to(0.1 * column, (LANES, width))
    def wind(state):
        out = []
        for r in range(cell_rows):
            diff = state[0, r, 0:1, :] - state[1, r, 0:1, :]
            out.append(diff * diff)
        return out

    def fresh_part(b, wind_rows, target):
        weights = quartet_v[part(b), :]
        pair = jnp.dot(weights, cell_f[...], preferred_element_type=F32)
        quad = jnp.dot(weights, cell_s[...], preferred_element_type=F32)
        outs = []
        for r in range(cell_rows):
            cut = slice(r * width, (r + 1) * width)
            f = cell_f[part(b), cut].astype(F32)
            top = f + 0.3 * (f * pair[:, cut] - quad[:, cut]) + grow_b[part(b), :] * wind_rows[r]
            out = (sea[r] * (top / (1.0 + 0.1 * (f * f)))).astype(BF16)
            target[part(b), cut] = out
            outs.append(out)
        return outs

    def square(b):
        f = cell_f[part(b), :].astype(F32)
        cell_s[part(b), :] = (f * f).astype(BF16)

    square(me)
    for b in order[::-1]:
        for i, dst in enumerate((cx_all, cy_all)):
            remote(dst.at[b], dst.at[b], c_send.at[i, 0], c_recv.at[i, b], block_id(b)).wait_recv()
        cxb[part(b), :] = jnp.broadcast_to(column_of(cx_all[b]), (comps, width))
        cyb[part(b), :] = jnp.broadcast_to(column_of(cy_all[b]), (comps, width))
    for i in range(cell_rows):
        for core in range(lev_parts):
            source = mine_l * cell_rows + i

            @pl.when((source != mine_c) | (mine_l != core))
            def _():
                there = st_in.at[:, i, pl.ds(core * lown, lown), :]
                remote(there, there, swap_ss.at[0, 0], swap_rs.at[0, i, core], partner).wait_recv()

        @pl.when(mine_l * cell_rows + i != mine_c)
        def _():
            there = sea_in.at[i]
            remote(there, there, swap_ss.at[1, 0], swap_rs.at[1, i, 0], partner).wait_recv()

    @pl.when(home != mine_l)
    def _():
        state_in(0).wait_send()

    @pl.when(home == mine_l)
    def _():
        for dc in range(1, cell_tiles):
            sea_over(dc).wait_send()

    st0[...] = st_in[...].astype(F32)
    state_copies = send_state(st0, 0)

    sea = [sea_in[r] for r in range(cell_rows)]

    loads[7].wait()
    loads[8].wait()
    for b in order[::-1]:
        remote(cell_f.at[part(b), :], cell_f.at[part(b), :], f_send.at[0], f_recv.at[b],
               block_id(b)).wait_recv()
        square(b)

    wind_rows = wind(st0)
    first = jnp.zeros((comps, width), F32)
    last = jnp.zeros((comps, width), F32)
    rim_copies = []
    group = max(blocks // 2, 1)
    for b in range(blocks):
        outs = fresh_part(b, wind_rows, e1)
        rim[0, part(b), :] = outs[0]
        rim[1, part(b), :] = outs[cell_rows - 1]
        if (b + 1) % group == 0:
            run = pl.ds((b + 1 - group) * comps, group * comps)
            for i, dst in enumerate((halo_s, halo_n)):
                copy = remote(rim.at[i, run, :], dst.at[run, :], row_ss.at[i, b], row_rs.at[i, b], partner)
                copy.start()
                rim_copies.append(copy)
        for r in range(cell_rows):
            slot = b * cell_rows + r
            v = outs[r].astype(F32)
            first = jnp.where(lane % seg == slot, pltpu.roll(v, slot, 1), first)
            last = jnp.where(lane % seg == slot, pltpu.roll(v, (slot + 1 - seg) % width, 1), last)
    pending.extend(rim_copies)
    edge_send[1, 0] = first.astype(BF16)
    edge_send[1, 1] = last.astype(BF16)
    edges = send_edges(1)

    west_rim = lane % seg == 0
    east_rim = lane % seg == seg - 1
    for b in range(blocks):
        if b % group == 0:
            rim_copies[2 * (b // group)].wait_recv()
            rim_copies[2 * (b // group) + 1].wait_recv()
        cx = cxb[part(b), :]
        cy = cyb[part(b), :]
        px, mx = halves(cx)
        py, my = halves(cy)
        keep = 1.0 - jnp.abs(cx) - jnp.abs(cy)
        field = [e1[part(b), r * width:(r + 1) * width].astype(F32) for r in range(cell_rows)]
        field = [halo_n[part(b), :].astype(F32)] + field + [halo_s[part(b), :].astype(F32)]
        for r in range(cell_rows):
            v = field[r + 1]
            north = pltpu.roll(jnp.where(lane >= width - seg, field[r], v), seg, 1)
            south = pltpu.roll(jnp.where(lane < seg, field[r + 2], v), width - seg, 1)
            to_west = jnp.where(west_rim, 0.0, pltpu.roll(v, 1, 1))
            to_east = jnp.where(east_rim, 0.0, pltpu.roll(v, width - 1, 1))
            inner[part(b), r * width:(r + 1) * width] = (
                v * keep + px * to_west + mx * to_east + py * north + my * south
            )

    for copy in state_copies:
        copy.wait_recv()
    update(st0, st1, 0, jnp.dot(coupler_v[...], e1[...], preferred_element_type=F32))
    state_copies = send_state(st1, 1)
    wind_rows = wind(st1)

    for copy in edges:
        copy.wait_recv()
    from_east = edge_recv[1, 0].astype(F32)
    from_west = edge_recv[1, 1].astype(F32)
    for b in range(blocks):
        px, mx = halves(cxb[part(b), :])
        for r in range(cell_rows):
            slot = b * cell_rows + r
            cut = slice(r * width, (r + 1) * width)
            side = jnp.where(
                west_rim, px * pltpu.roll(from_west, (width - slot) % width, 1),
                mx * pltpu.roll(from_east, (width + seg - 1 - slot) % width, 1),
            )
            out = (inner[part(b), cut] + jnp.where(west_rim | east_rim, side, 0.0)).astype(BF16)
            cell_f[part(b), cut] = out
            wide = out.astype(F32)
            cell_s[part(b), cut] = (wide * wide).astype(BF16)

    for d, b in enumerate(order + [me]):
        fresh_part(b, wind_rows, e2)
        if d < blocks - 1:
            copy = remote(e2.at[part(b), :], ret.at[spot_t], ret_ss.at[d], ret_rs.at[spot_t], block_id(b))
            copy.start()
            pending.append(copy)

    for copy in state_copies:
        copy.wait_recv()
    update(st1, st2, 1, jnp.dot(coupler_v[...], e2[...], preferred_element_type=F32))
    st_back[...] = st2[...].astype(BF16)

    def state_back(h, core):
        owner = mine_l * cell_rows + h
        return (owner != mine_c) | (mine_l != core), remote(
            st_back.at[:, h, pl.ds(core * lown, lown), :], fin.at[mine_t], back_ss.at[h, core],
            back_rs.at[mine_t], {"cells": owner, "lev": core},
        )

    for h in range(cell_rows):
        for core in range(lev_parts):
            away, copy = state_back(h, core)

            @pl.when(away)
            def _():
                copy.start()

            @pl.when(jnp.logical_not(away))
            def _():
                pltpu.make_async_copy(
                    st_back.at[:, h, pl.ds(core * lown, lown), :], fin.at[mine_t], own_sem.at[0]
                ).start()

    stores = []
    stores.append(pltpu.make_async_copy(e2.at[part(me), :], ret.at[spot_t], out_sem.at[2]))
    stores[-1].start()
    for b in order[::-1]:
        t = swapped(lax.div(b, lev_parts)) * lev_parts + lax.rem(b, lev_parts)
        remote(e2.at[part(b), :], ret.at[t], ret_ss.at[0], ret_rs.at[t], block_id(b)).wait_recv()
    for c in range(cell_tiles):
        @pl.when((c != mine_t) | (home != mine_l))
        def _():
            remote(fin.at[c], fin.at[c], back_ss.at[0, 0], back_rs.at[c], partner).wait_recv()

    @pl.when(home == mine_l)
    def _():
        pltpu.make_async_copy(st_back.at[:, 0, pl.ds(0, lown), :], fin.at[mine_t], own_sem.at[0]).wait()

    for h in range(cell_rows):
        for core in range(lev_parts):
            away, copy = state_back(h, core)

            @pl.when(away)
            def _():
                copy.wait_send()

    for b in range(blocks):
        @pl.when(b != me)
        def _():
            remote(send_f.at[b], send_f.at[b], f_send.at[b], f_recv.at[0], partner).wait_send()

    for copy in pending:
        copy.wait_send()
    for store in stores:
        store.wait()


def unpack_kernel(lev_parts, ret, fin, spec_out, atm_out, oce_out, ret_v, fin_v, atm_v, oce_v, flat, spec_v, in_sem, out_sem):
    blocks, comps, cells = ret_v.shape
    rows, width = spec_v.shape[1:]
    cell_rows = rows // blocks
    loads = [pltpu.make_async_copy(ret.at[b], ret_v.at[b], in_sem.at[b]) for b in range(blocks)]
    loads.append(pltpu.make_async_copy(fin, fin_v, in_sem.at[blocks]))
    for load in loads:
        load.start()
    tiles = blocks // lev_parts
    for core in range(lev_parts):
        for c in range(tiles):
            loads[c * lev_parts + core].wait()
        for h in range(cell_rows):
            lines = swap_groups([
                ret_v[c * lev_parts + core, :, h * width:(h + 1) * width].astype(F32) for c in range(tiles)
            ], width // tiles)
            for g, line in enumerate(lines):
                flat[pl.ds((core * cell_rows + h) * tiles + g, comps, stride=rows), :] = line
    loads[-1].wait()
    for f, target in enumerate((atm_v, oce_v)):
        lines = swap_groups([fin_v[c, f].astype(F32) for c in range(tiles)], width // tiles)
        for r, line in enumerate(lines):
            target[:, r, :] = line
    stores = [
        pltpu.make_async_copy(atm_v, atm_out, out_sem.at[0]),
        pltpu.make_async_copy(oce_v, oce_out, out_sem.at[1]),
    ]
    for store in stores:
        store.start()
    pieces = 3 if comps % 3 == 0 else 1
    size = comps // pieces
    for p in range(pieces):
        cut = pl.ds(p * size, size)
        spec_v[cut] = flat[pl.ds(p * size * rows, size * rows), :].reshape(size, rows, width).astype(BF16)
        stores.append(pltpu.make_async_copy(spec_v.at[cut], spec_out.at[cut], out_sem.at[2 + p]))
        stores[-1].start()
    for store in stores:
        store.wait()


def fused(
    spectrum, courant_x, courant_y, growth, quartet, coupler, atmosphere, ocean_state, sea_mask
):
    cell_tiles = lax.axis_size("cells")
    lev_parts = lax.axis_size("lev")
    sect_tiles = lax.axis_size("sect")
    blocks = cell_tiles * lev_parts
    comps, rows, width = spectrum.shape
    total = comps * blocks
    cell_rows = rows // blocks
    lown, tile_rows, _ = atmosphere.shape
    levels = lown * lev_parts
    cells = cell_rows * width
    v = pltpu.VMEM
    dma = pltpu.SemaphoreType.DMA
    scratch = [
        v((comps, rows, width), BF16), v((1, comps), F32), v((1, comps), F32),
        v((total,), F32), v((total, total), BF16), v(coupler.shape, BF16),
        v((2, lown, tile_rows, width), F32), v(sea_mask.shape, jnp.int32),
        v((comps * rows, width), F32), v((rows, comps, width), F32),
        v((blocks, comps, cells), BF16), v((total, cells), BF16), v((total, cells), BF16),
        v((blocks, 1, comps), F32), v((blocks, 1, comps), F32),
        v((total, width), F32), v((total, width), F32), v((total, width), F32),
        v((NSTEP, 2, comps, width), BF16), v((NSTEP, 2, comps, width), BF16),
        v((total, cells), BF16), v((2, total, width), BF16), v((total, width), BF16), v((total, width), BF16),
        v((total, cells), BF16),
        v((cell_tiles, 2, lown, width), BF16), v((2, cell_rows, levels, width), BF16),
        v((cell_tiles, 1, width), F32), v((cell_rows, 1, width), F32),
        v((2, lev_parts * cell_rows, comps, width), F32), v((total, cells), F32),
        v((2, cell_rows, levels, width), F32), v((2, cell_rows, levels, width), F32),
        v((2, cell_rows, levels, width), F32),
        v((NSTEP, 2, levels, width), F32), v((NSTEP, 2, levels, width), F32),
        v((NSTEP, 2, 2, levels, width), F32),
        v((2, cell_rows, levels, width), BF16), dma((9,)), dma((3,)), dma((1,)), dma((blocks,)), dma((blocks,)),
        dma((2, blocks)), dma((2, blocks)),
        dma((NSTEP, 2)), dma((NSTEP, 2)), dma((2, blocks)), dma((2, blocks)),
        dma((2, cell_tiles)), dma((2, cell_rows, lev_parts)), dma((cell_rows, lev_parts)), dma((cell_tiles,)),
        dma((NSTEP, 2)), dma((NSTEP, 2)), dma((NSTEP, 2)), dma((NSTEP, 2)),
        dma((blocks,)), dma((blocks,)),
    ]
    anywhere = pl.BlockSpec(memory_space=pltpu.HBM)
    column = jax.ShapeDtypeStruct(atmosphere.shape, F32)
    packed = pl.pallas_call(
        functools.partial(fused_kernel, cell_tiles, lev_parts, sect_tiles),
        out_shape=(
            jax.ShapeDtypeStruct((blocks, comps, cells), BF16),
            jax.ShapeDtypeStruct((cell_tiles, 2, lown, width), BF16),
        ),
        in_specs=[anywhere] * 9,
        out_specs=(anywhere,) * 2,
        scratch_shapes=scratch,
        compiler_params=pltpu.CompilerParams(
            collective_id=0, has_side_effects=True, vmem_limit_bytes=67043328
        ),
    )(
        spectrum, courant_x.reshape(1, comps), courant_y.reshape(1, comps),
        growth, quartet, coupler, atmosphere, ocean_state, sea_mask,
    )
    return pl.pallas_call(
        functools.partial(unpack_kernel, lev_parts),
        out_shape=(jax.ShapeDtypeStruct(spectrum.shape, BF16), column, column),
        in_specs=[anywhere] * 2,
        out_specs=(anywhere,) * 3,
        scratch_shapes=[
            v((blocks, comps, cells), BF16), v((cell_tiles, 2, lown, width), BF16), v(atmosphere.shape, F32), v(atmosphere.shape, F32),
            v((comps * rows, width), F32), v(spectrum.shape, BF16), dma((blocks + 1,)), dma((5,)),
        ],
        compiler_params=pltpu.CompilerParams(vmem_limit_bytes=67043328),
    )(*packed)


def fits_fused(mesh, spectrum, coupler, atmosphere):
    lev_parts = lax.axis_size("lev")
    blocks = lax.axis_size("cells") * lev_parts
    comps, rows, width = spectrum.shape
    return (
        lev_parts == 2 and lax.axis_size("sect") % 2 == 0 and lax.axis_size("cells") == 4 and width == LANES
        and comps % 16 == 0 and rows % blocks == 0 and rows <= LANES and rows % 16 == 0
        and (comps * blocks) % LANES == 0 and atmosphere.shape[0] % 16 == 0
        and atmosphere.shape[1] == lax.axis_size("cells") == lev_parts * (rows // blocks)
        and width % lax.axis_size("cells") == 0
        and blocks * (rows // blocks) <= width // lax.axis_size("cells")
    )


def solution(mesh):
    in_specs = (
        P(("cells", "lev"), "groups", "sect"),
        P(("cells", "lev")),
        P(("cells", "lev")),
        P(),
        P(),
        P(),
        P("lev", ("groups", "cells"), "sect"),
        P("lev", ("groups", "cells"), "sect"),
        P(("groups", "cells"), "sect"),
    )
    out_specs = (
        P(("cells", "lev"), "groups", "sect"),
        P("lev", ("groups", "cells"), "sect"),
        P("lev", ("groups", "cells"), "sect"),
    )

    def body(*args):
        if fits_fused(mesh, args[0], args[5], args[6]):
            return fused(*args)
        return on_device(*args)

    return jax.shard_map(
        body, mesh=mesh, in_specs=in_specs, out_specs=out_specs, check_vma=False
    )
```

```python
import functools

import jax
import jax.numpy as jnp
from jax import lax
from jax.experimental import pallas as pl
from jax.experimental.pallas import tpu as pltpu
from jax.sharding import PartitionSpec as P

NSTEP = 2
LANES = 128
F32 = jnp.float32
BF16 = jnp.bfloat16


def from_root(block, axis, source):
    block = jnp.where(lax.axis_index(axis) == source, block, jnp.zeros_like(block))
    return lax.psum(block, axis)


def extended_2(block, sides, width, periodic):
    for axis, dim in sides:
        count = lax.axis_size(axis)
        forward = [(i, i + 1) for i in range(count - 1)]
        if periodic:
            forward.append((count - 1, 0))
        backward = [(target, source) for source, target in forward]
        low = lax.ppermute(
            lax.slice_in_dim(block, block.shape[dim] - width, None, axis=dim), axis, forward
        )
        high = lax.ppermute(lax.slice_in_dim(block, 0, width, axis=dim), axis, backward)
        block = jnp.concatenate([low, block, high], axis=dim)
    return block


def upwind(values, courant, before, after):
    return jnp.maximum(courant, 0.0) * (values - before) + jnp.minimum(courant, 0.0) * (
        after - values
    )


def on_device(
    spectrum, courant_x, courant_y, growth, quartet, coupler, atmosphere, ocean_state, sea_mask
):
    cell_tiles = lax.axis_size("cells")
    lev_parts = lax.axis_size("lev")
    blocks = cell_tiles * lev_parts
    comps_own, rows_all, row_width = spectrum.shape
    total_comps = comps_own * blocks
    cell_rows = rows_all // blocks
    level_count = coupler.shape[0] // 2
    row_start = lax.axis_index("lev") * cell_rows
    shift_x = courant_x[:, None, None]
    shift_y = courant_y[:, None, None]
    sea_rows = (
        lax.dynamic_slice_in_dim(sea_mask, row_start, cell_rows, 0)
        .astype(jnp.float32)
        .reshape(1, cell_rows * row_width)
    )
    growth_column = growth[:, None]
    forcing_sign = jnp.array([-0.3, 0.3], jnp.float32)[:, None, None, None]
    state = jnp.stack([atmosphere, ocean_state])
    energy = spectrum
    for counter in range(NSTEP):
        surface = from_root(state[:, 0], "lev", 0)
        surface_wind = surface[0] - surface[1]
        wind_rows = lax.dynamic_slice_in_dim(
            surface_wind * surface_wind, row_start, cell_rows, 0
        ).reshape(1, cell_rows * row_width)
        padded = extended_2(energy, (("sect", 2),), 1, True)
        values = padded[:, :, 1:-1].astype(jnp.float32)
        west_side = padded[:, :, :-2].astype(jnp.float32)
        east_side = padded[:, :, 2:].astype(jnp.float32)
        moved = values - upwind(values, shift_x, west_side, east_side)
        moved = moved - upwind(
            values, shift_y, jnp.roll(values, 1, axis=1), jnp.roll(values, -1, axis=1)
        )
        advected = moved.astype(jnp.bfloat16)
        pieces = advected.reshape(1, comps_own, blocks, cell_rows, row_width)
        on_cells = lax.all_to_all(pieces, ("cells", "lev"), split_axis=2, concat_axis=0, tiled=True)
        on_cells = on_cells.reshape(total_comps, cell_rows * row_width)
        cell_values = on_cells.astype(jnp.float32)
        paired = jnp.dot(quartet, on_cells, preferred_element_type=jnp.float32)
        squared = (cell_values * cell_values).astype(jnp.bfloat16)
        quad_square = jnp.dot(quartet, squared, preferred_element_type=jnp.float32)
        fresh = (
            cell_values
            + 0.3 * (cell_values * paired - quad_square)
            + 0.1 * growth_column * wind_rows
        ) / (1.0 + 0.1 * cell_values * cell_values)
        fresh = (fresh * sea_rows).astype(jnp.bfloat16)
        profile = jnp.dot(coupler, fresh, preferred_element_type=jnp.float32).reshape(
            2, level_count, cell_rows, row_width
        )
        forcing = lax.all_to_all(profile, "lev", split_axis=1, concat_axis=2, tiled=True)
        returned = fresh.reshape(blocks, comps_own, 1, cell_rows, row_width)
        returned = lax.all_to_all(
            returned, ("cells", "lev"), split_axis=0, concat_axis=2, tiled=True
        )
        energy = returned.reshape(comps_own, rows_all, row_width)
        extended = extended_2(state, (("lev", 1), ("cells", 2), ("sect", 3)), 1, False)
        middle = extended[:, 1:-1, 1:-1, 1:-1]
        lateral = (
            extended[:, 1:-1, 2:, 1:-1]
            + extended[:, 1:-1, :-2, 1:-1]
            + extended[:, 1:-1, 1:-1, 2:]
            + extended[:, 1:-1, 1:-1, :-2]
            - 4.0 * middle
        )
        upright = extended[:, 2:, 1:-1, 1:-1] + extended[:, :-2, 1:-1, 1:-1] - 2.0 * middle
        state = middle + 0.1 * lateral + 0.1 * upright + forcing_sign * forcing
    return (energy, state[0], state[1])


def column_of(row):
    n = row.shape[1]
    down = lax.broadcasted_iota(jnp.int32, (n, n), 0)
    across = lax.broadcasted_iota(jnp.int32, (n, n), 1)
    return jnp.sum(jnp.where(down == across, row, 0.0), axis=1, keepdims=True)


def swap_groups(vectors, seg):
    count = len(vectors)
    width = vectors[0].shape[1]
    group = lax.broadcasted_iota(jnp.int32, vectors[0].shape, 1) // seg
    dist = count // 2
    vectors = list(vectors)
    while dist:
        even = (group // dist) % 2 == 0
        for i in range(count):
            if (i // dist) % 2 == 0:
                x, y = vectors[i], vectors[i + dist]
                if 2 * dist * seg == width:
                    moved = pltpu.roll(jnp.where(even, y, x), dist * seg, 1)
                    vectors[i], vectors[i + dist] = jnp.where(even, x, moved), jnp.where(even, moved, y)
                else:
                    vectors[i] = jnp.where(even, x, pltpu.roll(y, dist * seg, 1))
                    vectors[i + dist] = jnp.where(even, pltpu.roll(x, width - dist * seg, 1), y)
        dist //= 2
    return vectors


def fused_kernel(
    cell_tiles, lev_parts, sect_tiles,
    spec_hbm, cx_hbm, cy_hbm, growth_hbm, quartet_hbm, coupler_hbm, atm_hbm, oce_hbm, sea_hbm,
    ret, fin,
    spec_v, cx_v, cy_v, growth_v, quartet_v, coupler_v, col_in, sea_v,
    flat, rows_v, send_f, cell_f, cell_s, cx_all, cy_all, cxb, cyb, grow_b,
    edge_send, edge_recv, e1, e2,
    swap_send, st_in, sea_send, sea_in, outer, inner, st0, st1, st2, st_edge_send, st_edge_recv, st_back,
    in_sem, own_sem, f_send, f_recv, c_send, c_recv,
    edge_ss, edge_rs, swap_ss, swap_rs, sea_ss, sea_rs, back_ss, back_rs, ste_ss, ste_rs,
    ret_ss, ret_rs,
):
    blocks = cell_tiles * lev_parts
    comps, rows, width = spec_v.shape
    lines = rows // blocks
    lown = col_in.shape[1]
    tile_rows = col_in.shape[2]
    levels = lown * lev_parts
    seg = width // blocks
    mid = width // 2
    mine_c = lax.axis_index("cells")
    mine_l = lax.axis_index("lev")
    mine_x = lax.axis_index("sect")
    me = mine_c * lev_parts + mine_l
    turned = lax.rem(mine_x, 2) == 1
    side = lax.div(mine_c, cell_tiles // 2)

    def tile_of(b):
        return jnp.where(turned, blocks - 1 - b, b)

    def mirrored(b):
        return jnp.where(side == 1, blocks - 1 - b, b)

    def block_id(b):
        return {"cells": lax.div(b, lev_parts), "lev": lax.rem(b, lev_parts)}

    spot = tile_of(me)
    inside = mirrored(me)
    west = {"sect": lax.rem(mine_x + sect_tiles - 1, sect_tiles)}
    east = {"sect": lax.rem(mine_x + 1, sect_tiles)}
    near_west = {
        **block_id(jnp.where(spot == 0, me, tile_of(spot - 1))),
        "sect": jnp.where(spot == 0, west["sect"], mine_x),
    }
    near_east = {
        **block_id(jnp.where(spot == blocks - 1, me, tile_of(spot + 1))),
        "sect": jnp.where(spot == blocks - 1, east["sect"], mine_x),
    }
    half = blocks // 2
    odd = lax.rem(inside, 2)
    across = [mirrored(blocks - 1 - i + (1 - 2 * (i % 2)) * -odd) for i in range(half)]
    mate = (1 - lax.div(inside, lev_parts)) * lev_parts
    mates = [mirrored(mate + k) for k in range(lev_parts)]
    order = across + mates + [mirrored(inside + 1 - 2 * odd)]

    def part(b):
        return pl.ds(pl.multiple_of(b * comps, 16), comps)

    def remote(src, dst, ss, rs, where):
        return pltpu.make_async_remote_copy(
            src_ref=src, dst_ref=dst, send_sem=ss, recv_sem=rs,
            device_id=where, device_id_type=pl.DeviceIdType.MESH,
        )

    loads = [
        pltpu.make_async_copy(a, b, in_sem.at[i])
        for i, (a, b) in enumerate([
            (spec_hbm, spec_v), (cx_hbm, cx_v), (cy_hbm, cy_v),
            (atm_hbm, col_in.at[0]), (oce_hbm, col_in.at[1]), (sea_hbm, sea_v),
            (growth_hbm, growth_v), (coupler_hbm, coupler_v), (quartet_hbm, quartet_v),
        ])
    ]
    for load in loads:
        load.start()

    barrier = pltpu.get_barrier_semaphore()
    for d in range(1, blocks):
        pl.semaphore_signal(barrier, inc=1, device_id=block_id(lax.rem(me + d, blocks)),
                            device_id_type=pl.DeviceIdType.MESH)
    for side_id in (west, east, near_west, near_east):
        pl.semaphore_signal(barrier, inc=1, device_id=side_id,
                            device_id_type=pl.DeviceIdType.MESH)

    lane = lax.broadcasted_iota(jnp.int32, (comps, width), 1)
    loads[0].wait()
    flat[...] = spec_v[...].astype(F32).reshape(comps * rows, width)
    first = jnp.zeros((comps, width), F32)
    last = jnp.zeros((comps, width), F32)
    for r in range(rows):
        v = flat[pl.ds(r, comps, stride=rows), :]
        rows_v[r] = v
        place = (r % blocks) * seg + r // blocks
        first = jnp.where(lane == place, pltpu.roll(v, place, 1), first)
        last = jnp.where(lane == place, pltpu.roll(v, (place + 1) % width, 1), last)
    edge_send[0, 0] = first.astype(BF16)
    edge_send[0, 1] = last.astype(BF16)

    pl.semaphore_wait(barrier, blocks + 3)
    pending = []

    def send_edges(step):
        copies = [
            remote(edge_send.at[step, i], edge_recv.at[step, i],
                   edge_ss.at[step, i], edge_rs.at[step, i], where)
            for i, where in enumerate((west, east) if step == 0 else (near_west, near_east))
        ]
        for copy in copies:
            copy.start()
        pending.extend(copies)
        return copies

    edges = send_edges(0)

    loads[1].wait()
    loads[2].wait()
    for d, b in enumerate(order):
        for i, (src, dst) in enumerate(((cx_v, cx_all), (cy_v, cy_all))):
            copy = remote(src, dst.at[me], c_send.at[i, d], c_recv.at[i, me], block_id(b))
            copy.start()
            pending.append(copy)

    my_levels = pl.ds(pl.multiple_of(mine_l * lown, 16), lown)

    def state_in(b):
        return remote(swap_send.at[tile_of(b)], st_in.at[mine_c, my_levels, :], swap_ss.at[b],
                      swap_rs.at[mine_c, mine_l], block_id(b))

    def sea_over(c):
        return remote(sea_send.at[tile_of(c * lev_parts + mine_l)], sea_in.at[mine_c], sea_ss.at[c],
                      sea_rs.at[mine_c], {"cells": c})

    def send_state_in():
        loads[3].wait()
        loads[4].wait()
        loads[5].wait()
        groups = [col_in[f, :, r, :] for f in range(2) for r in range(tile_rows)]
        for t, line in enumerate(swap_groups(groups, seg)):
            swap_send[t] = line.astype(BF16)
        groups = [jnp.broadcast_to(sea_v[r:r + 1, :].astype(F32), (8, width)) for r in range(tile_rows)]
        for t, line in enumerate(swap_groups(groups + [jnp.zeros((8, width), F32)] * tile_rows, seg)):
            sea_send[t] = line[0:1]
        for b in order:
            state_in(b).start()
        for dc in range(1, cell_tiles):
            sea_over(lax.rem(mine_c + dc, cell_tiles)).start()
        st_in[mine_c, my_levels, :] = swap_send[spot]
        sea_in[mine_c] = sea_send[spot]

    def halves(c):
        return jnp.maximum(c, 0.0), jnp.maximum(-c, 0.0)

    cxb[part(me), :] = jnp.broadcast_to(column_of(cx_v[...]), (comps, width))
    cyb[part(me), :] = jnp.broadcast_to(column_of(cy_v[...]), (comps, width))

    def send_line(b, h):
        t = tile_of(b)
        cut = slice(h * width, (h + 1) * width)

        @pl.when(b != me)
        def _():
            remote(send_f.at[t, h], cell_f.at[part(me), cut], f_send.at[b, h], f_recv.at[me, h],
                   block_id(b)).start()

        @pl.when(b == me)
        def _():
            cell_f[part(me), cut] = send_f[spot, h]

    chunk = 16
    small = lax.broadcasted_iota(jnp.int32, (chunk, width), 1)
    at_rim = inside < lev_parts

    for h in range(lines):
        for k in range(0, comps, chunk):
            own = pl.ds(pl.multiple_of(me * comps + k, 16), chunk)
            cx = cxb[own, :]
            cy = cyb[own, :]
            px, mx = halves(cx)
            py, my = halves(cy)
            keep = 1.0 - jnp.abs(cx) - jnp.abs(cy)
            groups = []
            for g in range(blocks):
                row = h * blocks + g
                v = rows_v[row, k:k + chunk]
                to_west = jnp.where(small == 0, 0.0, pltpu.roll(v, 1, 1))
                to_east = jnp.where(small == width - 1, 0.0, pltpu.roll(v, width - 1, 1))
                groups.append(
                    v * keep + px * to_west + mx * to_east
                    + py * rows_v[(row + rows - 1) % rows, k:k + chunk] + my * rows_v[(row + 1) % rows, k:k + chunk]
                )
            for t, line in enumerate(swap_groups(groups, seg)):
                if 0 < t < blocks - 1:
                    send_f[t, h, k:k + chunk] = line.astype(BF16)
                else:
                    outer[min(t, 1), h, k:k + chunk] = line
        for i in range(blocks - 2, half - 1, -1):
            send_line(mirrored(i), h)
        send_line(mirrored(1), h)

        @pl.when(jnp.logical_not(at_rim))
        def _():
            for i in range(2, half):
                send_line(mirrored(i), h)
    send_state_in()
    for copy in edges:
        copy.wait_recv()
    for k in range(0, comps, chunk):
        cx = cxb[pl.ds(pl.multiple_of(me * comps + k, 16), chunk), :]
        px, mx = halves(cx)
        from_east = edge_recv[0, 0, k:k + chunk].astype(F32)
        from_west = edge_recv[0, 1, k:k + chunk].astype(F32)
        for h in range(lines):
            west_part = jnp.where(small % seg == 0, pltpu.roll(from_west, (width - h) % width, 1), 0.0)
            east_part = jnp.where(small % seg == seg - 1, pltpu.roll(from_east, seg - 1 - h, 1), 0.0)
            send_f[0, h, k:k + chunk] = (outer[0, h, k:k + chunk] + px * west_part).astype(BF16)
            send_f[blocks - 1, h, k:k + chunk] = (outer[1, h, k:k + chunk] + mx * east_part).astype(BF16)
    for i in (blocks - 1, 0):
        for h in range(lines):
            send_line(mirrored(i), h)

    @pl.when(at_rim)
    def _():
        for i in range(2, half):
            for h in range(lines):
                send_line(mirrored(i), h)

    level_id = lax.broadcasted_iota(jnp.int32, (levels, width), 0)
    level_lane = lax.broadcasted_iota(jnp.int32, (levels, width), 1)
    place = level_lane % seg
    folds = seg // (2 * lines)
    depth = levels // folds
    fold_place = place[:depth]

    def fold_slots():
        for f in range(2):
            for r in range(lines):
                for q in range(folds):
                    yield f, r, slice(q * depth, (q + 1) * depth), (q * 2 + f) * lines + r

    def send_state(state, step):
        west_pack = jnp.zeros((depth, width), F32)
        east_pack = jnp.zeros((depth, width), F32)
        for f, r, cut, slot in fold_slots():
            v = state[f, r, cut]
            west_pack = jnp.where(fold_place == slot, pltpu.roll(v, slot, 1), west_pack)
            east_pack = jnp.where(fold_place == slot, pltpu.roll(v, (slot + 1 - seg) % width, 1), east_pack)
        st_edge_send[step, 0] = west_pack
        st_edge_send[step, 1] = east_pack
        copies = []
        for i, where in enumerate((near_west, near_east)):
            copies.append(remote(st_edge_send.at[step, i], st_edge_recv.at[step, i],
                                 ste_ss.at[step, i], ste_rs.at[step, i], where))
        for copy in copies:
            copy.start()
        pending.extend(copies)
        return copies

    def update(state, new, step, profile):
        rim_west = (mine_x == 0) & (spot == 0)
        rim_east = (mine_x == sect_tiles - 1) & (spot == blocks - 1)
        west_pack = jnp.where(rim_west, 0.0, st_edge_recv[step, 1])
        east_pack = jnp.where(rim_east, 0.0, st_edge_recv[step, 0])
        sides = {}
        for f, r, cut, slot in fold_slots():
            sides.setdefault((f, r), []).append((
                pltpu.roll(west_pack, (width - slot) % width, 1),
                pltpu.roll(east_pack, (width + seg - 1 - slot) % width, 1),
            ))
        for f in range(2):
            factor = -0.3 if f == 0 else 0.3
            for r in range(lines):
                v = state[f, r]
                w = jnp.where(place == 0, jnp.concatenate([x for x, _ in sides[f, r]]), pltpu.roll(v, 1, 1))
                e = jnp.where(place == seg - 1, jnp.concatenate([x for _, x in sides[f, r]]),
                              pltpu.roll(v, width - 1, 1))
                n = 0.0 if r == 0 else state[f, r - 1]
                s = 0.0 if r == lines - 1 else state[f, r + 1]
                n = pltpu.roll(jnp.where(level_lane >= width - seg, n, v), seg, 1)
                s = pltpu.roll(jnp.where(level_lane < seg, s, v), width - seg, 1)
                below = jnp.where(level_id == 0, 0.0, pltpu.roll(v, 1, 0))
                above = jnp.where(level_id == levels - 1, 0.0, pltpu.roll(v, levels - 1, 0))
                g = profile[f * levels:(f + 1) * levels, r * width:(r + 1) * width]
                new[f, r] = (v + 0.1 * (n + s + w + e - 4.0 * v)
                             + 0.1 * (above + below - 2.0 * v) + factor * g)

    loads[6].wait()
    for t in range(growth_v.shape[0] // LANES):
        column = column_of(growth_v[t * LANES:(t + 1) * LANES].reshape(1, LANES))
        grow_b[t * LANES:(t + 1) * LANES, :] = jnp.broadcast_to(0.1 * column, (LANES, width))

    def wind(state):
        out = []
        for r in range(lines):
            diff = state[0, r, 0:1, :] - state[1, r, 0:1, :]
            out.append(diff * diff)
        return out

    def fresh_part(b, wind_rows, target):
        weights = quartet_v[part(b), :]
        pair = jnp.dot(weights, cell_f[...], preferred_element_type=F32)
        quad = jnp.dot(weights, cell_s[...], preferred_element_type=F32)
        outs = []
        for r in range(lines):
            cut = slice(r * width, (r + 1) * width)
            f = cell_f[part(b), cut].astype(F32)
            top = f + 0.3 * (f * pair[:, cut] - quad[:, cut]) + grow_b[part(b), :] * wind_rows[r]
            out = (sea[r] * (top / (1.0 + 0.1 * (f * f)))).astype(BF16)
            target[part(b), cut] = out
            outs.append(out)
        return outs

    def square(b):
        f = cell_f[part(b), :].astype(F32)
        cell_s[part(b), :] = (f * f).astype(BF16)

    square(me)
    for b in order[::-1]:
        for i, dst in enumerate((cx_all, cy_all)):
            remote(dst.at[b], dst.at[b], c_send.at[i, 0], c_recv.at[i, b], block_id(b)).wait_recv()
        cxb[part(b), :] = jnp.broadcast_to(column_of(cx_all[b]), (comps, width))
        cyb[part(b), :] = jnp.broadcast_to(column_of(cy_all[b]), (comps, width))
    for b in order[::-1]:
        c = lax.div(b, lev_parts)
        core = lax.rem(b, lev_parts)
        there = st_in.at[c, pl.ds(pl.multiple_of(core * lown, 16), lown), :]
        remote(there, there, swap_ss.at[0], swap_rs.at[c, core], block_id(b)).wait_recv()
    for dc in range(1, cell_tiles):
        c = lax.rem(mine_c + dc, cell_tiles)
        remote(sea_in.at[c], sea_in.at[c], sea_ss.at[0], sea_rs.at[c], {"cells": c}).wait_recv()

    wide_lane = lax.broadcasted_iota(jnp.int32, (8, width), 1)
    sea = []
    for h in range(lines):
        low = st_in[2 * h].astype(F32)
        high = st_in[2 * h + 1].astype(F32)
        st0[0, h] = jnp.where(level_lane < mid, low, pltpu.roll(high, mid, 1))
        st0[1, h] = jnp.where(level_lane < mid, pltpu.roll(low, mid, 1), high)
        low = jnp.broadcast_to(sea_in[2 * h], (8, width))
        high = jnp.broadcast_to(sea_in[2 * h + 1], (8, width))
        sea.append(jnp.where(wide_lane < mid, low, pltpu.roll(high, mid, 1))[0:1])
    state_copies = send_state(st0, 0)

    loads[7].wait()
    loads[8].wait()
    for b in order[::-1]:
        for h in range(lines):
            cut = slice(h * width, (h + 1) * width)
            remote(cell_f.at[part(b), cut], cell_f.at[part(b), cut], f_send.at[0, 0], f_recv.at[b, h],
                   block_id(b)).wait_recv()
        square(b)

    wind_rows = wind(st0)
    first = jnp.zeros((comps, width), F32)
    last = jnp.zeros((comps, width), F32)
    for b in range(blocks):
        outs = fresh_part(b, wind_rows, e1)
        for r in range(lines):
            slot = b * lines + r
            v = outs[r].astype(F32)
            first = jnp.where(lane % seg == slot, pltpu.roll(v, slot, 1), first)
            last = jnp.where(lane % seg == slot, pltpu.roll(v, (slot + 1 - seg) % width, 1), last)
    edge_send[1, 0] = first.astype(BF16)
    edge_send[1, 1] = last.astype(BF16)
    edges = send_edges(1)

    west_rim = lane % seg == 0
    east_rim = lane % seg == seg - 1
    for b in range(blocks):
        cx = cxb[part(b), :]
        cy = cyb[part(b), :]
        px, mx = halves(cx)
        py, my = halves(cy)
        keep = 1.0 - jnp.abs(cx) - jnp.abs(cy)
        field = [e1[part(b), r * width:(r + 1) * width].astype(F32) for r in range(lines)]
        for r in range(lines):
            v = field[r]
            north = pltpu.roll(jnp.where(lane >= width - seg, field[r - 1], v), seg, 1)
            south = pltpu.roll(jnp.where(lane < seg, field[(r + 1) % lines], v), width - seg, 1)
            to_west = jnp.where(west_rim, 0.0, pltpu.roll(v, 1, 1))
            to_east = jnp.where(east_rim, 0.0, pltpu.roll(v, width - 1, 1))
            inner[part(b), r * width:(r + 1) * width] = (
                v * keep + px * to_west + mx * to_east + py * north + my * south
            )

    for copy in state_copies:
        copy.wait_recv()
    update(st0, st1, 0, jnp.dot(coupler_v[...], e1[...], preferred_element_type=F32))
    state_copies = send_state(st1, 1)
    wind_rows = wind(st1)

    for copy in edges:
        copy.wait_recv()
    from_east = edge_recv[1, 0].astype(F32)
    from_west = edge_recv[1, 1].astype(F32)
    for b in range(blocks):
        px, mx = halves(cxb[part(b), :])
        for r in range(lines):
            slot = b * lines + r
            cut = slice(r * width, (r + 1) * width)
            beside = jnp.where(
                west_rim, px * pltpu.roll(from_west, (width - slot) % width, 1),
                mx * pltpu.roll(from_east, (width + seg - 1 - slot) % width, 1),
            )
            out = (inner[part(b), cut] + jnp.where(west_rim | east_rim, beside, 0.0)).astype(BF16)
            cell_f[part(b), cut] = out
            wide = out.astype(F32)
            cell_s[part(b), cut] = (wide * wide).astype(BF16)

    for d, b in enumerate(order + [me]):
        fresh_part(b, wind_rows, e2)
        if d < blocks - 1:
            copy = remote(e2.at[part(b), :], ret.at[spot], ret_ss.at[d], ret_rs.at[spot], block_id(b))
            copy.start()
            pending.append(copy)

    for copy in state_copies:
        copy.wait_recv()
    update(st1, st2, 1, jnp.dot(coupler_v[...], e2[...], preferred_element_type=F32))
    for h in range(lines):
        atm = st2[0, h]
        oce = st2[1, h]
        st_back[2 * h] = jnp.where(level_lane < mid, atm, pltpu.roll(oce, mid, 1)).astype(BF16)
        st_back[2 * h + 1] = jnp.where(level_lane < mid, pltpu.roll(atm, mid, 1), oce).astype(BF16)

    for d, b in enumerate(order):
        c = lax.div(b, lev_parts)
        core = lax.rem(b, lev_parts)
        copy = remote(st_back.at[c, pl.ds(pl.multiple_of(core * lown, 16), lown), :], fin.at[spot], back_ss.at[d],
                      back_rs.at[spot], block_id(b))
        copy.start()
        pending.append(copy)
    stores = [
        pltpu.make_async_copy(st_back.at[mine_c, my_levels, :], fin.at[spot], own_sem.at[0]),
        pltpu.make_async_copy(e2.at[part(me), :], ret.at[spot], own_sem.at[1]),
    ]
    for store in stores:
        store.start()
    for b in order[::-1]:
        t = tile_of(b)
        remote(e2.at[part(b), :], ret.at[t], ret_ss.at[0], ret_rs.at[t], block_id(b)).wait_recv()
    for b in order[::-1]:
        t = tile_of(b)
        remote(fin.at[t], fin.at[t], back_ss.at[0], back_rs.at[t], block_id(b)).wait_recv()

    for b in order:
        state_in(b).wait_send()
        for h in range(lines):
            remote(send_f.at[tile_of(b), h], send_f.at[tile_of(b), h], f_send.at[b, h], f_recv.at[0, 0],
                   block_id(b)).wait_send()
    for dc in range(1, cell_tiles):
        sea_over(lax.rem(mine_c + dc, cell_tiles)).wait_send()
    for copy in pending:
        copy.wait_send()
    for store in stores:
        store.wait()


def unpack_kernel(ret, fin, spec_out, atm_out, oce_out, ret_v, fin_v, atm_v, oce_v, flat, spec_v, in_sem, out_sem):
    blocks, comps, cells = ret_v.shape
    rows, width = spec_v.shape[1:]
    lines = cells // width
    seg = width // blocks
    tile_rows = atm_v.shape[1]
    loads = [pltpu.make_async_copy(ret.at[b], ret_v.at[b], in_sem.at[b]) for b in range(blocks)]
    loads.append(pltpu.make_async_copy(fin, fin_v, in_sem.at[blocks]))
    for load in loads:
        load.start()
    loads[-1].wait()
    stores = []
    groups = swap_groups([fin_v[t].astype(F32) for t in range(blocks)], seg)
    for f, (target, out) in enumerate(((atm_v, atm_out), (oce_v, oce_out))):
        for r in range(tile_rows):
            target[:, r, :] = groups[f * tile_rows + r]
        stores.append(pltpu.make_async_copy(target, out, out_sem.at[f]))
        stores[-1].start()
    for load in loads[:-1]:
        load.wait()
    pieces = 3 if comps % 48 == 0 else 1
    size = comps // pieces
    for p in range(pieces):
        for k in range(p * size, (p + 1) * size, 16):
            for h in range(lines):
                groups = swap_groups([
                    ret_v[t, k:k + 16, h * width:(h + 1) * width].astype(F32) for t in range(blocks)
                ], seg)
                for g, line in enumerate(groups):
                    flat[pl.ds(k * rows + h * blocks + g, 16, stride=rows), :] = line
            spec_v[k:k + 16] = flat[k * rows:(k + 16) * rows, :].reshape(16, rows, width).astype(BF16)
        cut = pl.ds(p * size, size)
        stores.append(pltpu.make_async_copy(spec_v.at[cut], spec_out.at[cut], out_sem.at[2 + p]))
        stores[-1].start()
    for store in stores:
        store.wait()


def fused(
    spectrum, courant_x, courant_y, growth, quartet, coupler, atmosphere, ocean_state, sea_mask
):
    cell_tiles = lax.axis_size("cells")
    lev_parts = lax.axis_size("lev")
    sect_tiles = lax.axis_size("sect")
    blocks = cell_tiles * lev_parts
    comps, rows, width = spectrum.shape
    total = comps * blocks
    lines = rows // blocks
    lown, tile_rows, _ = atmosphere.shape
    levels = lown * lev_parts
    cells = lines * width
    depth = levels // (width // blocks // (2 * lines))
    v = pltpu.VMEM
    dma = pltpu.SemaphoreType.DMA
    scratch = [
        v((comps, rows, width), BF16), v((1, comps), F32), v((1, comps), F32),
        v((total,), F32), v((total, total), BF16), v(coupler.shape, BF16),
        v((2, lown, tile_rows, width), F32), v(sea_mask.shape, jnp.int32),
        v((comps * rows, width), F32), v((rows, comps, width), F32),
        v((blocks, lines, comps, width), BF16), v((total, cells), BF16), v((total, cells), BF16),
        v((blocks, 1, comps), F32), v((blocks, 1, comps), F32),
        v((total, width), F32), v((total, width), F32), v((total, width), F32),
        v((NSTEP, 2, comps, width), BF16), v((NSTEP, 2, comps, width), BF16),
        v((total, cells), BF16), v((total, cells), BF16),
        v((blocks, lown, width), BF16), v((cell_tiles, levels, width), BF16),
        v((blocks, 1, width), F32), v((cell_tiles, 1, width), F32),
        v((2, lines, comps, width), F32), v((total, cells), F32),
        v((2, lines, levels, width), F32), v((2, lines, levels, width), F32),
        v((2, lines, levels, width), F32),
        v((NSTEP, 2, depth, width), F32), v((NSTEP, 2, depth, width), F32),
        v((cell_tiles, levels, width), BF16),
        dma((9,)), dma((2,)), dma((blocks, lines)), dma((blocks, lines)),
        dma((2, blocks)), dma((2, blocks)),
        dma((NSTEP, 2)), dma((NSTEP, 2)),
        dma((blocks,)), dma((cell_tiles, lev_parts)), dma((cell_tiles,)), dma((cell_tiles,)),
        dma((blocks,)), dma((blocks,)),
        dma((NSTEP, 2)), dma((NSTEP, 2)),
        dma((blocks,)), dma((blocks,)),
    ]
    anywhere = pl.BlockSpec(memory_space=pltpu.HBM)
    column = jax.ShapeDtypeStruct(atmosphere.shape, F32)
    packed = pl.pallas_call(
        functools.partial(fused_kernel, cell_tiles, lev_parts, sect_tiles),
        out_shape=(
            jax.ShapeDtypeStruct((blocks, comps, cells), BF16),
            jax.ShapeDtypeStruct((blocks, lown, width), BF16),
        ),
        in_specs=[anywhere] * 9,
        out_specs=(anywhere,) * 2,
        scratch_shapes=scratch,
        compiler_params=pltpu.CompilerParams(
            collective_id=0, has_side_effects=True, vmem_limit_bytes=67043328
        ),
    )(
        spectrum, courant_x.reshape(1, comps), courant_y.reshape(1, comps),
        growth, quartet, coupler, atmosphere, ocean_state, sea_mask,
    )
    return pl.pallas_call(
        unpack_kernel,
        out_shape=(jax.ShapeDtypeStruct(spectrum.shape, BF16), column, column),
        in_specs=[anywhere] * 2,
        out_specs=(anywhere,) * 3,
        scratch_shapes=[
            v((blocks, comps, cells), BF16), v((blocks, lown, width), BF16), v(atmosphere.shape, F32), v(atmosphere.shape, F32),
            v((comps * rows, width), F32), v(spectrum.shape, BF16), dma((blocks + 1,)), dma((5,)),
        ],
        compiler_params=pltpu.CompilerParams(vmem_limit_bytes=67043328),
    )(*packed)


def fits_fused(mesh, spectrum, coupler, atmosphere):
    lev_parts = lax.axis_size("lev")
    cells = lax.axis_size("cells")
    blocks = cells * lev_parts
    comps, rows, width = spectrum.shape
    return (
        lev_parts == 2 and cells == 4 and lax.axis_size("sect") % 2 == 0 and width == LANES
        and comps % 16 == 0 and rows == 2 * blocks and (comps * blocks) % LANES == 0
        and atmosphere.shape[0] % 16 == 0 and 2 * atmosphere.shape[1] == blocks
    )


def solution(mesh):
    in_specs = (
        P(("cells", "lev"), "groups", "sect"),
        P(("cells", "lev")),
        P(("cells", "lev")),
        P(),
        P(),
        P(),
        P("lev", ("groups", "cells"), "sect"),
        P("lev", ("groups", "cells"), "sect"),
        P(("groups", "cells"), "sect"),
    )
    out_specs = (
        P(("cells", "lev"), "groups", "sect"),
        P("lev", ("groups", "cells"), "sect"),
        P("lev", ("groups", "cells"), "sect"),
    )

    def body(*args):
        if fits_fused(mesh, args[0], args[5], args[6]):
            return fused(*args)
        return on_device(*args)

    return jax.shard_map(
        body, mesh=mesh, in_specs=in_specs, out_specs=out_specs, check_vma=False
    )
```

```python
import functools

import jax
import jax.numpy as jnp
from jax import lax
from jax.experimental import pallas as pl
from jax.experimental.pallas import tpu as pltpu
from jax.sharding import PartitionSpec as P

NSTEP = 2
LANES = 128
F32 = jnp.float32
BF16 = jnp.bfloat16


def from_root(block, axis, source):
    block = jnp.where(lax.axis_index(axis) == source, block, jnp.zeros_like(block))
    return lax.psum(block, axis)


def extended_2(block, sides, width, periodic):
    for axis, dim in sides:
        count = lax.axis_size(axis)
        forward = [(i, i + 1) for i in range(count - 1)]
        if periodic:
            forward.append((count - 1, 0))
        backward = [(target, source) for source, target in forward]
        low = lax.ppermute(
            lax.slice_in_dim(block, block.shape[dim] - width, None, axis=dim), axis, forward
        )
        high = lax.ppermute(lax.slice_in_dim(block, 0, width, axis=dim), axis, backward)
        block = jnp.concatenate([low, block, high], axis=dim)
    return block


def upwind(values, courant, before, after):
    return jnp.maximum(courant, 0.0) * (values - before) + jnp.minimum(courant, 0.0) * (
        after - values
    )


def on_device(
    spectrum, courant_x, courant_y, growth, quartet, coupler, atmosphere, ocean_state, sea_mask
):
    cell_tiles = lax.axis_size("cells")
    lev_parts = lax.axis_size("lev")
    blocks = cell_tiles * lev_parts
    comps_own, rows_all, row_width = spectrum.shape
    total_comps = comps_own * blocks
    cell_rows = rows_all // blocks
    level_count = coupler.shape[0] // 2
    row_start = lax.axis_index("lev") * cell_rows
    shift_x = courant_x[:, None, None]
    shift_y = courant_y[:, None, None]
    sea_rows = (
        lax.dynamic_slice_in_dim(sea_mask, row_start, cell_rows, 0)
        .astype(jnp.float32)
        .reshape(1, cell_rows * row_width)
    )
    growth_column = growth[:, None]
    forcing_sign = jnp.array([-0.3, 0.3], jnp.float32)[:, None, None, None]
    state = jnp.stack([atmosphere, ocean_state])
    energy = spectrum
    for counter in range(NSTEP):
        surface = from_root(state[:, 0], "lev", 0)
        surface_wind = surface[0] - surface[1]
        wind_rows = lax.dynamic_slice_in_dim(
            surface_wind * surface_wind, row_start, cell_rows, 0
        ).reshape(1, cell_rows * row_width)
        padded = extended_2(energy, (("sect", 2),), 1, True)
        values = padded[:, :, 1:-1].astype(jnp.float32)
        west_side = padded[:, :, :-2].astype(jnp.float32)
        east_side = padded[:, :, 2:].astype(jnp.float32)
        moved = values - upwind(values, shift_x, west_side, east_side)
        moved = moved - upwind(
            values, shift_y, jnp.roll(values, 1, axis=1), jnp.roll(values, -1, axis=1)
        )
        advected = moved.astype(jnp.bfloat16)
        pieces = advected.reshape(1, comps_own, blocks, cell_rows, row_width)
        on_cells = lax.all_to_all(pieces, ("cells", "lev"), split_axis=2, concat_axis=0, tiled=True)
        on_cells = on_cells.reshape(total_comps, cell_rows * row_width)
        cell_values = on_cells.astype(jnp.float32)
        paired = jnp.dot(quartet, on_cells, preferred_element_type=jnp.float32)
        squared = (cell_values * cell_values).astype(jnp.bfloat16)
        quad_square = jnp.dot(quartet, squared, preferred_element_type=jnp.float32)
        fresh = (
            cell_values
            + 0.3 * (cell_values * paired - quad_square)
            + 0.1 * growth_column * wind_rows
        ) / (1.0 + 0.1 * cell_values * cell_values)
        fresh = (fresh * sea_rows).astype(jnp.bfloat16)
        profile = jnp.dot(coupler, fresh, preferred_element_type=jnp.float32).reshape(
            2, level_count, cell_rows, row_width
        )
        forcing = lax.all_to_all(profile, "lev", split_axis=1, concat_axis=2, tiled=True)
        returned = fresh.reshape(blocks, comps_own, 1, cell_rows, row_width)
        returned = lax.all_to_all(
            returned, ("cells", "lev"), split_axis=0, concat_axis=2, tiled=True
        )
        energy = returned.reshape(comps_own, rows_all, row_width)
        extended = extended_2(state, (("lev", 1), ("cells", 2), ("sect", 3)), 1, False)
        middle = extended[:, 1:-1, 1:-1, 1:-1]
        lateral = (
            extended[:, 1:-1, 2:, 1:-1]
            + extended[:, 1:-1, :-2, 1:-1]
            + extended[:, 1:-1, 1:-1, 2:]
            + extended[:, 1:-1, 1:-1, :-2]
            - 4.0 * middle
        )
        upright = extended[:, 2:, 1:-1, 1:-1] + extended[:, :-2, 1:-1, 1:-1] - 2.0 * middle
        state = middle + 0.1 * lateral + 0.1 * upright + forcing_sign * forcing
    return (energy, state[0], state[1])


def column_of(row):
    n = row.shape[1]
    down = lax.broadcasted_iota(jnp.int32, (n, n), 0)
    across = lax.broadcasted_iota(jnp.int32, (n, n), 1)
    return jnp.sum(jnp.where(down == across, row, 0.0), axis=1, keepdims=True)


def swap_groups(vectors, seg):
    count = len(vectors)
    width = vectors[0].shape[1]
    group = lax.broadcasted_iota(jnp.int32, vectors[0].shape, 1) // seg
    dist = count // 2
    vectors = list(vectors)
    while dist:
        even = (group // dist) % 2 == 0
        for i in range(count):
            if (i // dist) % 2 == 0:
                x, y = vectors[i], vectors[i + dist]
                if 2 * dist * seg == width:
                    moved = pltpu.roll(jnp.where(even, y, x), dist * seg, 1)
                    vectors[i], vectors[i + dist] = jnp.where(even, x, moved), jnp.where(even, moved, y)
                else:
                    vectors[i] = jnp.where(even, x, pltpu.roll(y, dist * seg, 1))
                    vectors[i + dist] = jnp.where(even, pltpu.roll(x, width - dist * seg, 1), y)
        dist //= 2
    return vectors


def fused_kernel(
    cell_tiles, lev_parts, sect_tiles,
    spec_hbm, cx_hbm, cy_hbm, growth_hbm, quartet_hbm, coupler_hbm, atm_hbm, oce_hbm, sea_hbm,
    ret, fin,
    spec_v, cx_v, cy_v, growth_v, quartet_v, coupler_v, col_in, sea_v,
    flat, rows_v, send_f, cell_f, cell_s, cx_all, cy_all, cxb, cyb, grow_b,
    edge_send, edge_recv, e1, e2,
    swap_send, st_in, sea_send, sea_in, outer, inner, st0, st1, st2, st_edge_send, st_edge_recv, st_back,
    in_sem, own_sem, f_send, f_recv, c_send, c_recv,
    edge_ss, edge_rs, swap_ss, swap_rs, sea_ss, sea_rs, back_ss, back_rs, ste_ss, ste_rs,
    ret_ss, ret_rs,
):
    blocks = cell_tiles * lev_parts
    comps, rows, width = spec_v.shape
    lines = rows // blocks
    lown = col_in.shape[1]
    tile_rows = col_in.shape[2]
    levels = lown * lev_parts
    seg = width // blocks
    mid = width // 2
    mine_c = lax.axis_index("cells")
    mine_l = lax.axis_index("lev")
    mine_x = lax.axis_index("sect")
    me = mine_c * lev_parts + mine_l
    turned = lax.rem(mine_x, 2) == 1
    side = lax.div(mine_c, cell_tiles // 2)

    def tile_of(b):
        return jnp.where(turned, blocks - 1 - b, b)

    def mirrored(b):
        return jnp.where(side == 1, blocks - 1 - b, b)

    def block_id(b):
        return {"cells": lax.div(b, lev_parts), "lev": lax.rem(b, lev_parts)}

    spot = tile_of(me)
    inside = mirrored(me)
    west = {"sect": lax.rem(mine_x + sect_tiles - 1, sect_tiles)}
    east = {"sect": lax.rem(mine_x + 1, sect_tiles)}
    near_west = {
        **block_id(jnp.where(spot == 0, me, tile_of(spot - 1))),
        "sect": jnp.where(spot == 0, west["sect"], mine_x),
    }
    near_east = {
        **block_id(jnp.where(spot == blocks - 1, me, tile_of(spot + 1))),
        "sect": jnp.where(spot == blocks - 1, east["sect"], mine_x),
    }
    half = blocks // 2
    odd = lax.rem(inside, 2)
    across = [mirrored(blocks - 1 - i + (1 - 2 * (i % 2)) * -odd) for i in range(half)]
    mate = (1 - lax.div(inside, lev_parts)) * lev_parts
    mates = [mirrored(mate + k) for k in range(lev_parts)]
    order = across + mates + [mirrored(inside + 1 - 2 * odd)]

    def part(b):
        return pl.ds(pl.multiple_of(b * comps, 16), comps)

    def remote(src, dst, ss, rs, where):
        return pltpu.make_async_remote_copy(
            src_ref=src, dst_ref=dst, send_sem=ss, recv_sem=rs,
            device_id=where, device_id_type=pl.DeviceIdType.MESH,
        )

    loads = [
        pltpu.make_async_copy(a, b, in_sem.at[i])
        for i, (a, b) in enumerate([
            (spec_hbm, spec_v), (cx_hbm, cx_v), (cy_hbm, cy_v),
            (atm_hbm, col_in.at[0]), (oce_hbm, col_in.at[1]), (sea_hbm, sea_v),
            (growth_hbm, growth_v), (coupler_hbm, coupler_v), (quartet_hbm, quartet_v),
        ])
    ]
    for load in loads:
        load.start()

    barrier = pltpu.get_barrier_semaphore()
    for d in range(1, blocks):
        pl.semaphore_signal(barrier, inc=1, device_id=block_id(lax.rem(me + d, blocks)),
                            device_id_type=pl.DeviceIdType.MESH)
    for side_id in (west, east, near_west, near_east):
        pl.semaphore_signal(barrier, inc=1, device_id=side_id,
                            device_id_type=pl.DeviceIdType.MESH)

    lane = lax.broadcasted_iota(jnp.int32, (comps, width), 1)
    loads[0].wait()
    flat[...] = spec_v[...].astype(F32).reshape(comps * rows, width)
    first = jnp.zeros((comps, width), F32)
    last = jnp.zeros((comps, width), F32)
    for r in range(rows):
        v = flat[pl.ds(r, comps, stride=rows), :]
        rows_v[r] = v
        place = (r % blocks) * seg + r // blocks
        first = jnp.where(lane == place, pltpu.roll(v, place, 1), first)
        last = jnp.where(lane == place, pltpu.roll(v, (place + 1) % width, 1), last)
    edge_send[0, 0] = first.astype(BF16)
    edge_send[0, 1] = last.astype(BF16)

    pl.semaphore_wait(barrier, blocks + 3)
    pending = []

    def send_edges(step):
        copies = [
            remote(edge_send.at[step, i], edge_recv.at[step, i],
                   edge_ss.at[step, i], edge_rs.at[step, i], where)
            for i, where in enumerate((west, east) if step == 0 else (near_west, near_east))
        ]
        for copy in copies:
            copy.start()
        pending.extend(copies)
        return copies

    edges = send_edges(0)

    loads[1].wait()
    loads[2].wait()
    for d, b in enumerate(order):
        for i, (src, dst) in enumerate(((cx_v, cx_all), (cy_v, cy_all))):
            copy = remote(src, dst.at[me], c_send.at[i, d], c_recv.at[i, me], block_id(b))
            copy.start()
            pending.append(copy)

    my_levels = pl.ds(pl.multiple_of(mine_l * lown, 16), lown)

    def state_in(b):
        return remote(swap_send.at[tile_of(b)], st_in.at[mine_c, my_levels, :], swap_ss.at[b],
                      swap_rs.at[mine_c, mine_l], block_id(b))

    def sea_over(c):
        return remote(sea_send.at[tile_of(c * lev_parts + mine_l)], sea_in.at[mine_c], sea_ss.at[c],
                      sea_rs.at[mine_c], {"cells": c})

    def send_state_in():
        loads[3].wait()
        loads[4].wait()
        loads[5].wait()
        groups = [col_in[f, :, r, :] for f in range(2) for r in range(tile_rows)]
        for t, line in enumerate(swap_groups(groups, seg)):
            swap_send[t] = line.astype(BF16)
        groups = [jnp.broadcast_to(sea_v[r:r + 1, :].astype(F32), (8, width)) for r in range(tile_rows)]
        for t, line in enumerate(swap_groups(groups + [jnp.zeros((8, width), F32)] * tile_rows, seg)):
            sea_send[t] = line[0:1]
        for b in order:
            state_in(b).start()
        for dc in range(1, cell_tiles):
            sea_over(lax.rem(mine_c + dc, cell_tiles)).start()
        st_in[mine_c, my_levels, :] = swap_send[spot]
        sea_in[mine_c] = sea_send[spot]

    def halves(c):
        return jnp.maximum(c, 0.0), jnp.maximum(-c, 0.0)

    cxb[part(me), :] = jnp.broadcast_to(column_of(cx_v[...]), (comps, width))
    cyb[part(me), :] = jnp.broadcast_to(column_of(cy_v[...]), (comps, width))

    def send_line(b, h):
        t = tile_of(b)
        cut = slice(h * width, (h + 1) * width)

        @pl.when(b != me)
        def _():
            remote(send_f.at[t, h], cell_f.at[part(me), cut], f_send.at[b, h], f_recv.at[me, h],
                   block_id(b)).start()

        @pl.when(b == me)
        def _():
            cell_f[part(me), cut] = send_f[spot, h]

    chunk = comps
    small = lax.broadcasted_iota(jnp.int32, (chunk, width), 1)
    at_rim = inside < lev_parts

    for h in range(lines):
        for k in range(0, comps, chunk):
            own = pl.ds(pl.multiple_of(me * comps + k, 16), chunk)
            cx = cxb[own, :]
            cy = cyb[own, :]
            px, mx = halves(cx)
            py, my = halves(cy)
            keep = 1.0 - jnp.abs(cx) - jnp.abs(cy)
            groups = []
            for g in range(blocks):
                row = h * blocks + g
                v = rows_v[row, k:k + chunk]
                to_west = jnp.where(small == 0, 0.0, pltpu.roll(v, 1, 1))
                to_east = jnp.where(small == width - 1, 0.0, pltpu.roll(v, width - 1, 1))
                groups.append(
                    v * keep + px * to_west + mx * to_east
                    + py * rows_v[(row + rows - 1) % rows, k:k + chunk] + my * rows_v[(row + 1) % rows, k:k + chunk]
                )
            for t, line in enumerate(swap_groups(groups, seg)):
                if 0 < t < blocks - 1:
                    send_f[t, h, k:k + chunk] = line.astype(BF16)
                else:
                    outer[min(t, 1), h, k:k + chunk] = line
        for i in range(blocks - 2, half - 1, -1):
            send_line(mirrored(i), h)
        send_line(mirrored(1), h)

        @pl.when(jnp.logical_not(at_rim))
        def _():
            for i in range(2, half):
                send_line(mirrored(i), h)
    send_state_in()
    for copy in edges:
        copy.wait_recv()
    for k in range(0, comps, chunk):
        cx = cxb[pl.ds(pl.multiple_of(me * comps + k, 16), chunk), :]
        px, mx = halves(cx)
        from_east = edge_recv[0, 0, k:k + chunk].astype(F32)
        from_west = edge_recv[0, 1, k:k + chunk].astype(F32)
        for h in range(lines):
            west_part = jnp.where(small % seg == 0, pltpu.roll(from_west, (width - h) % width, 1), 0.0)
            east_part = jnp.where(small % seg == seg - 1, pltpu.roll(from_east, seg - 1 - h, 1), 0.0)
            send_f[0, h, k:k + chunk] = (outer[0, h, k:k + chunk] + px * west_part).astype(BF16)
            send_f[blocks - 1, h, k:k + chunk] = (outer[1, h, k:k + chunk] + mx * east_part).astype(BF16)
    for i in (blocks - 1, 0):
        for h in range(lines):
            send_line(mirrored(i), h)

    @pl.when(at_rim)
    def _():
        for i in range(2, half):
            for h in range(lines):
                send_line(mirrored(i), h)

    level_id = lax.broadcasted_iota(jnp.int32, (levels, width), 0)
    level_lane = lax.broadcasted_iota(jnp.int32, (levels, width), 1)
    place = level_lane % seg
    folds = seg // (2 * lines)
    depth = levels // folds
    fold_place = place[:depth]

    def fold_slots():
        for f in range(2):
            for r in range(lines):
                for q in range(folds):
                    yield f, r, slice(q * depth, (q + 1) * depth), (q * 2 + f) * lines + r

    def send_state(state, step):
        west_pack = jnp.zeros((depth, width), F32)
        east_pack = jnp.zeros((depth, width), F32)
        for f, r, cut, slot in fold_slots():
            v = state[f, r, cut]
            west_pack = jnp.where(fold_place == slot, pltpu.roll(v, slot, 1), west_pack)
            east_pack = jnp.where(fold_place == slot, pltpu.roll(v, (slot + 1 - seg) % width, 1), east_pack)
        st_edge_send[step, 0] = west_pack
        st_edge_send[step, 1] = east_pack
        copies = []
        for i, where in enumerate((near_west, near_east)):
            copies.append(remote(st_edge_send.at[step, i], st_edge_recv.at[step, i],
                                 ste_ss.at[step, i], ste_rs.at[step, i], where))
        for copy in copies:
            copy.start()
        pending.extend(copies)
        return copies

    def update(state, new, step, profile):
        rim_west = (mine_x == 0) & (spot == 0)
        rim_east = (mine_x == sect_tiles - 1) & (spot == blocks - 1)
        west_pack = jnp.where(rim_west, 0.0, st_edge_recv[step, 1])
        east_pack = jnp.where(rim_east, 0.0, st_edge_recv[step, 0])
        sides = {}
        for f, r, cut, slot in fold_slots():
            sides.setdefault((f, r), []).append((
                pltpu.roll(west_pack, (width - slot) % width, 1),
                pltpu.roll(east_pack, (width + seg - 1 - slot) % width, 1),
            ))
        for f in range(2):
            factor = -0.3 if f == 0 else 0.3
            for r in range(lines):
                v = state[f, r]
                w = jnp.where(place == 0, jnp.concatenate([x for x, _ in sides[f, r]]), pltpu.roll(v, 1, 1))
                e = jnp.where(place == seg - 1, jnp.concatenate([x for _, x in sides[f, r]]),
                              pltpu.roll(v, width - 1, 1))
                n = 0.0 if r == 0 else state[f, r - 1]
                s = 0.0 if r == lines - 1 else state[f, r + 1]
                n = pltpu.roll(jnp.where(level_lane >= width - seg, n, v), seg, 1)
                s = pltpu.roll(jnp.where(level_lane < seg, s, v), width - seg, 1)
                below = jnp.where(level_id == 0, 0.0, pltpu.roll(v, 1, 0))
                above = jnp.where(level_id == levels - 1, 0.0, pltpu.roll(v, levels - 1, 0))
                g = profile[f * levels:(f + 1) * levels, r * width:(r + 1) * width]
                new[f, r] = (v + 0.1 * (n + s + w + e - 4.0 * v)
                             + 0.1 * (above + below - 2.0 * v) + factor * g)

    loads[6].wait()
    for t in range(growth_v.shape[0] // LANES):
        column = column_of(growth_v[t * LANES:(t + 1) * LANES].reshape(1, LANES))
        grow_b[t * LANES:(t + 1) * LANES, :] = jnp.broadcast_to(0.1 * column, (LANES, width))

    def wind(state):
        out = []
        for r in range(lines):
            diff = state[0, r, 0:1, :] - state[1, r, 0:1, :]
            out.append(diff * diff)
        return out

    def fresh_part(b, wind_rows, target):
        weights = quartet_v[part(b), :]
        pair = jnp.dot(weights, cell_f[...], preferred_element_type=F32)
        quad = jnp.dot(weights, cell_s[...], preferred_element_type=F32)
        outs = []
        for r in range(lines):
            cut = slice(r * width, (r + 1) * width)
            f = cell_f[part(b), cut].astype(F32)
            top = f + 0.3 * (f * pair[:, cut] - quad[:, cut]) + grow_b[part(b), :] * wind_rows[r]
            out = (sea[r] * (top / (1.0 + 0.1 * (f * f)))).astype(BF16)
            target[part(b), cut] = out
            outs.append(out)
        return outs

    def square(b):
        f = cell_f[part(b), :].astype(F32)
        cell_s[part(b), :] = (f * f).astype(BF16)

    square(me)
    for b in order[::-1]:
        for i, dst in enumerate((cx_all, cy_all)):
            remote(dst.at[b], dst.at[b], c_send.at[i, 0], c_recv.at[i, b], block_id(b)).wait_recv()
        cxb[part(b), :] = jnp.broadcast_to(column_of(cx_all[b]), (comps, width))
        cyb[part(b), :] = jnp.broadcast_to(column_of(cy_all[b]), (comps, width))
    for b in order[::-1]:
        c = lax.div(b, lev_parts)
        core = lax.rem(b, lev_parts)
        there = st_in.at[c, pl.ds(pl.multiple_of(core * lown, 16), lown), :]
        remote(there, there, swap_ss.at[0], swap_rs.at[c, core], block_id(b)).wait_recv()
    for dc in range(1, cell_tiles):
        c = lax.rem(mine_c + dc, cell_tiles)
        remote(sea_in.at[c], sea_in.at[c], sea_ss.at[0], sea_rs.at[c], {"cells": c}).wait_recv()

    wide_lane = lax.broadcasted_iota(jnp.int32, (8, width), 1)
    sea = []
    for h in range(lines):
        low = st_in[2 * h].astype(F32)
        high = st_in[2 * h + 1].astype(F32)
        st0[0, h] = jnp.where(level_lane < mid, low, pltpu.roll(high, mid, 1))
        st0[1, h] = jnp.where(level_lane < mid, pltpu.roll(low, mid, 1), high)
        low = jnp.broadcast_to(sea_in[2 * h], (8, width))
        high = jnp.broadcast_to(sea_in[2 * h + 1], (8, width))
        sea.append(jnp.where(wide_lane < mid, low, pltpu.roll(high, mid, 1))[0:1])
    state_copies = send_state(st0, 0)

    loads[7].wait()
    loads[8].wait()
    for b in order[::-1]:
        for h in range(lines):
            cut = slice(h * width, (h + 1) * width)
            remote(cell_f.at[part(b), cut], cell_f.at[part(b), cut], f_send.at[0, 0], f_recv.at[b, h],
                   block_id(b)).wait_recv()
        square(b)

    wind_rows = wind(st0)
    first = jnp.zeros((comps, width), F32)
    last = jnp.zeros((comps, width), F32)
    for b in range(blocks):
        outs = fresh_part(b, wind_rows, e1)
        for r in range(lines):
            slot = b * lines + r
            v = outs[r].astype(F32)
            first = jnp.where(lane % seg == slot, pltpu.roll(v, slot, 1), first)
            last = jnp.where(lane % seg == slot, pltpu.roll(v, (slot + 1 - seg) % width, 1), last)
    edge_send[1, 0] = first.astype(BF16)
    edge_send[1, 1] = last.astype(BF16)
    edges = send_edges(1)

    west_rim = lane % seg == 0
    east_rim = lane % seg == seg - 1
    for b in range(blocks):
        cx = cxb[part(b), :]
        cy = cyb[part(b), :]
        px, mx = halves(cx)
        py, my = halves(cy)
        keep = 1.0 - jnp.abs(cx) - jnp.abs(cy)
        field = [e1[part(b), r * width:(r + 1) * width].astype(F32) for r in range(lines)]
        for r in range(lines):
            v = field[r]
            north = pltpu.roll(jnp.where(lane >= width - seg, field[r - 1], v), seg, 1)
            south = pltpu.roll(jnp.where(lane < seg, field[(r + 1) % lines], v), width - seg, 1)
            to_west = jnp.where(west_rim, 0.0, pltpu.roll(v, 1, 1))
            to_east = jnp.where(east_rim, 0.0, pltpu.roll(v, width - 1, 1))
            inner[part(b), r * width:(r + 1) * width] = (
                v * keep + px * to_west + mx * to_east + py * north + my * south
            )

    for copy in state_copies:
        copy.wait_recv()
    update(st0, st1, 0, jnp.dot(coupler_v[...], e1[...], preferred_element_type=F32))
    state_copies = send_state(st1, 1)
    wind_rows = wind(st1)

    for copy in edges:
        copy.wait_recv()
    from_east = edge_recv[1, 0].astype(F32)
    from_west = edge_recv[1, 1].astype(F32)
    for b in range(blocks):
        px, mx = halves(cxb[part(b), :])
        for r in range(lines):
            slot = b * lines + r
            cut = slice(r * width, (r + 1) * width)
            beside = jnp.where(
                west_rim, px * pltpu.roll(from_west, (width - slot) % width, 1),
                mx * pltpu.roll(from_east, (width + seg - 1 - slot) % width, 1),
            )
            out = (inner[part(b), cut] + jnp.where(west_rim | east_rim, beside, 0.0)).astype(BF16)
            cell_f[part(b), cut] = out
            wide = out.astype(F32)
            cell_s[part(b), cut] = (wide * wide).astype(BF16)

    for d, b in enumerate(order + [me]):
        fresh_part(b, wind_rows, e2)
        if d < blocks - 1:
            copy = remote(e2.at[part(b), :], ret.at[spot], ret_ss.at[d], ret_rs.at[spot], block_id(b))
            copy.start()
            pending.append(copy)

    for copy in state_copies:
        copy.wait_recv()
    update(st1, st2, 1, jnp.dot(coupler_v[...], e2[...], preferred_element_type=F32))
    for h in range(lines):
        atm = st2[0, h]
        oce = st2[1, h]
        st_back[2 * h] = jnp.where(level_lane < mid, atm, pltpu.roll(oce, mid, 1)).astype(BF16)
        st_back[2 * h + 1] = jnp.where(level_lane < mid, pltpu.roll(atm, mid, 1), oce).astype(BF16)

    for d, b in enumerate(order):
        c = lax.div(b, lev_parts)
        core = lax.rem(b, lev_parts)
        copy = remote(st_back.at[c, pl.ds(pl.multiple_of(core * lown, 16), lown), :], fin.at[spot], back_ss.at[d],
                      back_rs.at[spot], block_id(b))
        copy.start()
        pending.append(copy)
    stores = [
        pltpu.make_async_copy(st_back.at[mine_c, my_levels, :], fin.at[spot], own_sem.at[0]),
        pltpu.make_async_copy(e2.at[part(me), :], ret.at[spot], own_sem.at[1]),
    ]
    for store in stores:
        store.start()
    for b in order[::-1]:
        t = tile_of(b)
        remote(e2.at[part(b), :], ret.at[t], ret_ss.at[0], ret_rs.at[t], block_id(b)).wait_recv()
    for b in order[::-1]:
        t = tile_of(b)
        remote(fin.at[t], fin.at[t], back_ss.at[0], back_rs.at[t], block_id(b)).wait_recv()

    for b in order:
        state_in(b).wait_send()
        for h in range(lines):
            remote(send_f.at[tile_of(b), h], send_f.at[tile_of(b), h], f_send.at[b, h], f_recv.at[0, 0],
                   block_id(b)).wait_send()
    for dc in range(1, cell_tiles):
        sea_over(lax.rem(mine_c + dc, cell_tiles)).wait_send()
    for copy in pending:
        copy.wait_send()
    for store in stores:
        store.wait()


def unpack_kernel(ret, fin, spec_out, atm_out, oce_out, atm_v, oce_v, flat, spec_v, out_sem):
    blocks, comps, cells = ret.shape
    rows, width = spec_v.shape[1:]
    lines = cells // width
    seg = width // blocks
    tile_rows = atm_v.shape[1]
    stores = []
    for h in range(lines):
        groups = swap_groups([ret[t, :, h * width:(h + 1) * width].astype(F32) for t in range(blocks)], seg)
        for g, line in enumerate(groups):
            flat[pl.ds(h * blocks + g, comps, stride=rows), :] = line
    pieces = 3 if comps % 3 == 0 else 1
    size = comps // pieces
    for p in range(pieces):
        cut = pl.ds(p * size, size)
        spec_v[cut] = flat[pl.ds(p * size * rows, size * rows), :].reshape(size, rows, width).astype(BF16)
        stores.append(pltpu.make_async_copy(spec_v.at[cut], spec_out.at[cut], out_sem.at[2 + p]))
        stores[-1].start()
    groups = swap_groups([fin[t].astype(F32) for t in range(blocks)], seg)
    for f, (target, out) in enumerate(((atm_v, atm_out), (oce_v, oce_out))):
        for r in range(tile_rows):
            target[:, r, :] = groups[f * tile_rows + r]
        stores.append(pltpu.make_async_copy(target, out, out_sem.at[f]))
        stores[-1].start()
    for store in stores:
        store.wait()


def fused(
    spectrum, courant_x, courant_y, growth, quartet, coupler, atmosphere, ocean_state, sea_mask
):
    cell_tiles = lax.axis_size("cells")
    lev_parts = lax.axis_size("lev")
    sect_tiles = lax.axis_size("sect")
    blocks = cell_tiles * lev_parts
    comps, rows, width = spectrum.shape
    total = comps * blocks
    lines = rows // blocks
    lown, tile_rows, _ = atmosphere.shape
    levels = lown * lev_parts
    cells = lines * width
    depth = levels // (width // blocks // (2 * lines))
    v = pltpu.VMEM
    dma = pltpu.SemaphoreType.DMA
    scratch = [
        v((comps, rows, width), BF16), v((1, comps), F32), v((1, comps), F32),
        v((total,), F32), v((total, total), BF16), v(coupler.shape, BF16),
        v((2, lown, tile_rows, width), F32), v(sea_mask.shape, jnp.int32),
        v((comps * rows, width), F32), v((rows, comps, width), F32),
        v((blocks, lines, comps, width), BF16), v((total, cells), BF16), v((total, cells), BF16),
        v((blocks, 1, comps), F32), v((blocks, 1, comps), F32),
        v((total, width), F32), v((total, width), F32), v((total, width), F32),
        v((NSTEP, 2, comps, width), BF16), v((NSTEP, 2, comps, width), BF16),
        v((total, cells), BF16), v((total, cells), BF16),
        v((blocks, lown, width), BF16), v((cell_tiles, levels, width), BF16),
        v((blocks, 1, width), F32), v((cell_tiles, 1, width), F32),
        v((2, lines, comps, width), F32), v((total, cells), F32),
        v((2, lines, levels, width), F32), v((2, lines, levels, width), F32),
        v((2, lines, levels, width), F32),
        v((NSTEP, 2, depth, width), F32), v((NSTEP, 2, depth, width), F32),
        v((cell_tiles, levels, width), BF16),
        dma((9,)), dma((2,)), dma((blocks, lines)), dma((blocks, lines)),
        dma((2, blocks)), dma((2, blocks)),
        dma((NSTEP, 2)), dma((NSTEP, 2)),
        dma((blocks,)), dma((cell_tiles, lev_parts)), dma((cell_tiles,)), dma((cell_tiles,)),
        dma((blocks,)), dma((blocks,)),
        dma((NSTEP, 2)), dma((NSTEP, 2)),
        dma((blocks,)), dma((blocks,)),
    ]
    anywhere = pl.BlockSpec(memory_space=pltpu.HBM)
    here = pl.BlockSpec(memory_space=pltpu.VMEM)
    column = jax.ShapeDtypeStruct(atmosphere.shape, F32)
    packed = pl.pallas_call(
        functools.partial(fused_kernel, cell_tiles, lev_parts, sect_tiles),
        out_shape=(v((blocks, comps, cells), BF16), v((blocks, lown, width), BF16)),
        in_specs=[anywhere] * 9,
        out_specs=(here,) * 2,
        scratch_shapes=scratch,
        compiler_params=pltpu.CompilerParams(
            collective_id=0, has_side_effects=True, vmem_limit_bytes=33554432
        ),
    )(*(
        pltpu.with_memory_space_constraint(x, pltpu.HBM)
        for x in (spectrum, courant_x.reshape(1, comps), courant_y.reshape(1, comps),
                  growth, quartet, coupler, atmosphere, ocean_state, sea_mask)
    ))
    return pl.pallas_call(
        unpack_kernel,
        out_shape=(jax.ShapeDtypeStruct(spectrum.shape, BF16), column, column),
        in_specs=[here] * 2,
        out_specs=(anywhere,) * 3,
        scratch_shapes=[
            v(atmosphere.shape, F32), v(atmosphere.shape, F32),
            v((comps * rows, width), F32), v(spectrum.shape, BF16), dma((5,)),
        ],
        compiler_params=pltpu.CompilerParams(vmem_limit_bytes=33554432),
    )(*packed)


def fits_fused(mesh, spectrum, coupler, atmosphere):
    lev_parts = lax.axis_size("lev")
    cells = lax.axis_size("cells")
    blocks = cells * lev_parts
    comps, rows, width = spectrum.shape
    return (
        lev_parts == 2 and cells == 4 and lax.axis_size("sect") % 2 == 0 and width == LANES
        and comps % 16 == 0 and rows == 2 * blocks and (comps * blocks) % LANES == 0
        and atmosphere.shape[0] % 16 == 0 and 2 * atmosphere.shape[1] == blocks
    )


def solution(mesh):
    in_specs = (
        P(("cells", "lev"), "groups", "sect"),
        P(("cells", "lev")),
        P(("cells", "lev")),
        P(),
        P(),
        P(),
        P("lev", ("groups", "cells"), "sect"),
        P("lev", ("groups", "cells"), "sect"),
        P(("groups", "cells"), "sect"),
    )
    out_specs = (
        P(("cells", "lev"), "groups", "sect"),
        P("lev", ("groups", "cells"), "sect"),
        P("lev", ("groups", "cells"), "sect"),
    )

    def body(*args):
        if fits_fused(mesh, args[0], args[5], args[6]):
            return fused(*args)
        return on_device(*args)

    return jax.shard_map(
        body, mesh=mesh, in_specs=in_specs, out_specs=out_specs, check_vma=False
    )
```

```python
import functools

import jax
import jax.numpy as jnp
from jax import lax
from jax.experimental import pallas as pl
from jax.experimental.pallas import tpu as pltpu
from jax.sharding import PartitionSpec as P

NSTEP = 2
LANES = 128
F32 = jnp.float32
BF16 = jnp.bfloat16


def from_root(block, axis, source):
    block = jnp.where(lax.axis_index(axis) == source, block, jnp.zeros_like(block))
    return lax.psum(block, axis)


def extended_2(block, sides, width, periodic):
    for axis, dim in sides:
        count = lax.axis_size(axis)
        forward = [(i, i + 1) for i in range(count - 1)]
        if periodic:
            forward.append((count - 1, 0))
        backward = [(target, source) for source, target in forward]
        low = lax.ppermute(
            lax.slice_in_dim(block, block.shape[dim] - width, None, axis=dim), axis, forward
        )
        high = lax.ppermute(lax.slice_in_dim(block, 0, width, axis=dim), axis, backward)
        block = jnp.concatenate([low, block, high], axis=dim)
    return block


def upwind(values, courant, before, after):
    return jnp.maximum(courant, 0.0) * (values - before) + jnp.minimum(courant, 0.0) * (
        after - values
    )


def on_device(
    spectrum, courant_x, courant_y, growth, quartet, coupler, atmosphere, ocean_state, sea_mask
):
    cell_tiles = lax.axis_size("cells")
    lev_parts = lax.axis_size("lev")
    blocks = cell_tiles * lev_parts
    comps_own, rows_all, row_width = spectrum.shape
    total_comps = comps_own * blocks
    cell_rows = rows_all // blocks
    level_count = coupler.shape[0] // 2
    row_start = lax.axis_index("lev") * cell_rows
    shift_x = courant_x[:, None, None]
    shift_y = courant_y[:, None, None]
    sea_rows = (
        lax.dynamic_slice_in_dim(sea_mask, row_start, cell_rows, 0)
        .astype(jnp.float32)
        .reshape(1, cell_rows * row_width)
    )
    growth_column = growth[:, None]
    forcing_sign = jnp.array([-0.3, 0.3], jnp.float32)[:, None, None, None]
    state = jnp.stack([atmosphere, ocean_state])
    energy = spectrum
    for counter in range(NSTEP):
        surface = from_root(state[:, 0], "lev", 0)
        surface_wind = surface[0] - surface[1]
        wind_rows = lax.dynamic_slice_in_dim(
            surface_wind * surface_wind, row_start, cell_rows, 0
        ).reshape(1, cell_rows * row_width)
        padded = extended_2(energy, (("sect", 2),), 1, True)
        values = padded[:, :, 1:-1].astype(jnp.float32)
        west_side = padded[:, :, :-2].astype(jnp.float32)
        east_side = padded[:, :, 2:].astype(jnp.float32)
        moved = values - upwind(values, shift_x, west_side, east_side)
        moved = moved - upwind(
            values, shift_y, jnp.roll(values, 1, axis=1), jnp.roll(values, -1, axis=1)
        )
        advected = moved.astype(jnp.bfloat16)
        pieces = advected.reshape(1, comps_own, blocks, cell_rows, row_width)
        on_cells = lax.all_to_all(pieces, ("cells", "lev"), split_axis=2, concat_axis=0, tiled=True)
        on_cells = on_cells.reshape(total_comps, cell_rows * row_width)
        cell_values = on_cells.astype(jnp.float32)
        paired = jnp.dot(quartet, on_cells, preferred_element_type=jnp.float32)
        squared = (cell_values * cell_values).astype(jnp.bfloat16)
        quad_square = jnp.dot(quartet, squared, preferred_element_type=jnp.float32)
        fresh = (
            cell_values
            + 0.3 * (cell_values * paired - quad_square)
            + 0.1 * growth_column * wind_rows
        ) / (1.0 + 0.1 * cell_values * cell_values)
        fresh = (fresh * sea_rows).astype(jnp.bfloat16)
        profile = jnp.dot(coupler, fresh, preferred_element_type=jnp.float32).reshape(
            2, level_count, cell_rows, row_width
        )
        forcing = lax.all_to_all(profile, "lev", split_axis=1, concat_axis=2, tiled=True)
        returned = fresh.reshape(blocks, comps_own, 1, cell_rows, row_width)
        returned = lax.all_to_all(
            returned, ("cells", "lev"), split_axis=0, concat_axis=2, tiled=True
        )
        energy = returned.reshape(comps_own, rows_all, row_width)
        extended = extended_2(state, (("lev", 1), ("cells", 2), ("sect", 3)), 1, False)
        middle = extended[:, 1:-1, 1:-1, 1:-1]
        lateral = (
            extended[:, 1:-1, 2:, 1:-1]
            + extended[:, 1:-1, :-2, 1:-1]
            + extended[:, 1:-1, 1:-1, 2:]
            + extended[:, 1:-1, 1:-1, :-2]
            - 4.0 * middle
        )
        upright = extended[:, 2:, 1:-1, 1:-1] + extended[:, :-2, 1:-1, 1:-1] - 2.0 * middle
        state = middle + 0.1 * lateral + 0.1 * upright + forcing_sign * forcing
    return (energy, state[0], state[1])


def column_of(row):
    n = row.shape[1]
    down = lax.broadcasted_iota(jnp.int32, (n, n), 0)
    across = lax.broadcasted_iota(jnp.int32, (n, n), 1)
    return jnp.sum(jnp.where(down == across, row, 0.0), axis=1, keepdims=True)


def swap_groups(vectors, seg):
    count = len(vectors)
    width = vectors[0].shape[1]
    group = lax.broadcasted_iota(jnp.int32, vectors[0].shape, 1) // seg
    dist = count // 2
    vectors = list(vectors)
    while dist:
        even = (group // dist) % 2 == 0
        for i in range(count):
            if (i // dist) % 2 == 0:
                x, y = vectors[i], vectors[i + dist]
                if 2 * dist * seg == width:
                    moved = pltpu.roll(jnp.where(even, y, x), dist * seg, 1)
                    vectors[i], vectors[i + dist] = jnp.where(even, x, moved), jnp.where(even, moved, y)
                else:
                    vectors[i] = jnp.where(even, x, pltpu.roll(y, dist * seg, 1))
                    vectors[i + dist] = jnp.where(even, pltpu.roll(x, width - dist * seg, 1), y)
        dist //= 2
    return vectors


def fused_kernel(
    cell_tiles, lev_parts, sect_tiles,
    spec_hbm, cx_hbm, cy_hbm, growth_hbm, quartet_hbm, coupler_hbm, atm_hbm, oce_hbm, sea_hbm,
    ret, fin,
    spec_v, cx_v, cy_v, growth_v, quartet_v, coupler_v, col_in, sea_v,
    flat, rows_v, send_f, cell_f, cell_s, cx_all, cy_all, cxb, cyb, grow_b,
    edge_send, edge_recv, e1, e2,
    swap_send, st_in, sea_send, sea_in, outer, inner, st0, st1, st2, st_edge_send, st_edge_recv, st_back,
    in_sem, own_sem, f_send, f_recv, c_send, c_recv,
    edge_ss, edge_rs, swap_ss, swap_rs, sea_ss, sea_rs, back_ss, back_rs, ste_ss, ste_rs,
    ret_ss, ret_rs,
):
    blocks = cell_tiles * lev_parts
    comps, rows, width = spec_v.shape
    lines = rows // blocks
    lown = col_in.shape[1]
    tile_rows = col_in.shape[2]
    levels = lown * lev_parts
    seg = width // blocks
    mid = width // 2
    mine_c = lax.axis_index("cells")
    mine_l = lax.axis_index("lev")
    mine_x = lax.axis_index("sect")
    me = mine_c * lev_parts + mine_l
    turned = lax.rem(mine_x, 2) == 1
    side = lax.div(mine_c, cell_tiles // 2)

    def tile_of(b):
        return jnp.where(turned, blocks - 1 - b, b)

    def mirrored(b):
        return jnp.where(side == 1, blocks - 1 - b, b)

    def block_id(b):
        return {"cells": lax.div(b, lev_parts), "lev": lax.rem(b, lev_parts)}

    spot = tile_of(me)
    inside = mirrored(me)
    west = {"sect": lax.rem(mine_x + sect_tiles - 1, sect_tiles)}
    east = {"sect": lax.rem(mine_x + 1, sect_tiles)}
    near_west = {
        **block_id(jnp.where(spot == 0, me, tile_of(spot - 1))),
        "sect": jnp.where(spot == 0, west["sect"], mine_x),
    }
    near_east = {
        **block_id(jnp.where(spot == blocks - 1, me, tile_of(spot + 1))),
        "sect": jnp.where(spot == blocks - 1, east["sect"], mine_x),
    }
    half = blocks // 2
    odd = lax.rem(inside, 2)
    across = [mirrored(blocks - 1 - i + (1 - 2 * (i % 2)) * -odd) for i in range(half)]
    mate = (1 - lax.div(inside, lev_parts)) * lev_parts
    mates = [mirrored(mate + k) for k in range(lev_parts)]
    order = across + mates + [mirrored(inside + 1 - 2 * odd)]

    def part(b):
        return pl.ds(pl.multiple_of(b * comps, 16), comps)

    def remote(src, dst, ss, rs, where):
        return pltpu.make_async_remote_copy(
            src_ref=src, dst_ref=dst, send_sem=ss, recv_sem=rs,
            device_id=where, device_id_type=pl.DeviceIdType.MESH,
        )

    loads = [
        pltpu.make_async_copy(a, b, in_sem.at[i])
        for i, (a, b) in enumerate([
            (spec_hbm, spec_v), (cx_hbm, cx_v), (cy_hbm, cy_v),
            (atm_hbm, col_in.at[0]), (oce_hbm, col_in.at[1]), (sea_hbm, sea_v),
            (growth_hbm, growth_v), (coupler_hbm, coupler_v), (quartet_hbm, quartet_v),
        ])
    ]
    for load in loads:
        load.start()

    barrier = pltpu.get_barrier_semaphore()
    for d in range(1, blocks):
        pl.semaphore_signal(barrier, inc=1, device_id=block_id(lax.rem(me + d, blocks)),
                            device_id_type=pl.DeviceIdType.MESH)
    for side_id in (west, east, near_west, near_east):
        pl.semaphore_signal(barrier, inc=1, device_id=side_id,
                            device_id_type=pl.DeviceIdType.MESH)

    my_levels = pl.ds(pl.multiple_of(mine_l * lown, 16), lown)

    def state_in(b):
        return remote(swap_send.at[tile_of(b)], st_in.at[mine_c, my_levels, :], swap_ss.at[b],
                      swap_rs.at[mine_c, mine_l], block_id(b))

    def sea_over(c):
        return remote(sea_send.at[tile_of(c * lev_parts + mine_l)], sea_in.at[mine_c], sea_ss.at[c],
                      sea_rs.at[mine_c], {"cells": c})

    loads[3].wait()
    loads[4].wait()
    loads[5].wait()
    groups = [col_in[f, :, r, :] for f in range(2) for r in range(tile_rows)]
    for t, line in enumerate(swap_groups(groups, seg)):
        swap_send[t] = line.astype(BF16)
    groups = [jnp.broadcast_to(sea_v[r:r + 1, :].astype(F32), (8, width)) for r in range(tile_rows)]
    for t, line in enumerate(swap_groups(groups + [jnp.zeros((8, width), F32)] * tile_rows, seg)):
        sea_send[t] = line[0:1]
    st_in[mine_c, my_levels, :] = swap_send[spot]
    sea_in[mine_c] = sea_send[spot]

    lane = lax.broadcasted_iota(jnp.int32, (comps, width), 1)
    loads[0].wait()
    flat[...] = spec_v[...].astype(F32).reshape(comps * rows, width)
    first = jnp.zeros((comps, width), F32)
    last = jnp.zeros((comps, width), F32)
    for r in range(rows):
        v = flat[pl.ds(r, comps, stride=rows), :]
        rows_v[r] = v
        place = (r % blocks) * seg + r // blocks
        first = jnp.where(lane == place, pltpu.roll(v, place, 1), first)
        last = jnp.where(lane == place, pltpu.roll(v, (place + 1) % width, 1), last)
    edge_send[0, 0] = first.astype(BF16)
    edge_send[0, 1] = last.astype(BF16)

    pl.semaphore_wait(barrier, blocks + 3)
    pending = []

    def send_edges(step):
        copies = [
            remote(edge_send.at[step, i], edge_recv.at[step, i],
                   edge_ss.at[step, i], edge_rs.at[step, i], where)
            for i, where in enumerate((west, east) if step == 0 else (near_west, near_east))
        ]
        for copy in copies:
            copy.start()
        pending.extend(copies)
        return copies

    edges = send_edges(0)
    wave = [mirrored(i) for i in sorted(range(blocks), key=lambda i: (abs(2 * i + 1 - blocks), -i))]

    for b in wave:
        @pl.when(b != me)
        def _():
            state_in(b).start()
    for dc in range(1, cell_tiles):
        sea_over(lax.rem(mine_c + dc, cell_tiles)).start()
    loads[1].wait()
    loads[2].wait()
    for d, b in enumerate(order):
        for i, (src, dst) in enumerate(((cx_v, cx_all), (cy_v, cy_all))):
            copy = remote(src, dst.at[me], c_send.at[i, d], c_recv.at[i, me], block_id(b))
            copy.start()
            pending.append(copy)

    def halves(c):
        return jnp.maximum(c, 0.0), jnp.maximum(-c, 0.0)

    cxb[part(me), :] = jnp.broadcast_to(column_of(cx_v[...]), (comps, width))
    cyb[part(me), :] = jnp.broadcast_to(column_of(cy_v[...]), (comps, width))

    def send_line(b, h):
        t = tile_of(b)
        cut = slice(h * width, (h + 1) * width)

        @pl.when(b != me)
        def _():
            remote(send_f.at[t, h], cell_f.at[part(me), cut], f_send.at[b, h], f_recv.at[me, h],
                   block_id(b)).start()

        @pl.when(b == me)
        def _():
            cell_f[part(me), cut] = send_f[spot, h]

    chunk = comps
    small = lax.broadcasted_iota(jnp.int32, (chunk, width), 1)

    for h in range(lines):
        for k in range(0, comps, chunk):
            own = pl.ds(pl.multiple_of(me * comps + k, 16), chunk)
            cx = cxb[own, :]
            cy = cyb[own, :]
            px, mx = halves(cx)
            py, my = halves(cy)
            keep = 1.0 - jnp.abs(cx) - jnp.abs(cy)
            groups = []
            for g in range(blocks):
                row = h * blocks + g
                v = rows_v[row, k:k + chunk]
                to_west = jnp.where(small == 0, 0.0, pltpu.roll(v, 1, 1))
                to_east = jnp.where(small == width - 1, 0.0, pltpu.roll(v, width - 1, 1))
                groups.append(
                    v * keep + px * to_west + mx * to_east
                    + py * rows_v[(row + rows - 1) % rows, k:k + chunk] + my * rows_v[(row + 1) % rows, k:k + chunk]
                )
            for t, line in enumerate(swap_groups(groups, seg)):
                if 0 < t < blocks - 1:
                    send_f[t, h, k:k + chunk] = line.astype(BF16)
                else:
                    outer[min(t, 1), h, k:k + chunk] = line
        for b in wave[:2]:
            send_line(b, h)
    for b in wave[2:4]:
        for h in range(lines):
            send_line(b, h)

    @pl.when(inside != half - 1)
    def _():
        for h in range(lines):
            send_line(wave[4], h)
    for h in range(lines):
        send_line(wave[5], h)
    for copy in edges:
        copy.wait_recv()
    for k in range(0, comps, chunk):
        cx = cxb[pl.ds(pl.multiple_of(me * comps + k, 16), chunk), :]
        px, mx = halves(cx)
        from_east = edge_recv[0, 0, k:k + chunk].astype(F32)
        from_west = edge_recv[0, 1, k:k + chunk].astype(F32)
        for h in range(lines):
            west_part = jnp.where(small % seg == 0, pltpu.roll(from_west, (width - h) % width, 1), 0.0)
            east_part = jnp.where(small % seg == seg - 1, pltpu.roll(from_east, seg - 1 - h, 1), 0.0)
            send_f[0, h, k:k + chunk] = (outer[0, h, k:k + chunk] + px * west_part).astype(BF16)
            send_f[blocks - 1, h, k:k + chunk] = (outer[1, h, k:k + chunk] + mx * east_part).astype(BF16)

    @pl.when(inside != half - 1)
    def _():
        for h in range(lines):
            send_line(wave[6], h)
    for h in range(lines):
        send_line(wave[7], h)

    level_id = lax.broadcasted_iota(jnp.int32, (levels, width), 0)
    level_lane = lax.broadcasted_iota(jnp.int32, (levels, width), 1)
    place = level_lane % seg
    folds = seg // (2 * lines)
    depth = levels // folds
    fold_place = place[:depth]

    def fold_slots():
        for f in range(2):
            for r in range(lines):
                for q in range(folds):
                    yield f, r, slice(q * depth, (q + 1) * depth), (q * 2 + f) * lines + r

    def send_state(state, step):
        west_pack = jnp.zeros((depth, width), F32)
        east_pack = jnp.zeros((depth, width), F32)
        for f, r, cut, slot in fold_slots():
            v = state[f, r, cut]
            west_pack = jnp.where(fold_place == slot, pltpu.roll(v, slot, 1), west_pack)
            east_pack = jnp.where(fold_place == slot, pltpu.roll(v, (slot + 1 - seg) % width, 1), east_pack)
        st_edge_send[step, 0] = west_pack
        st_edge_send[step, 1] = east_pack
        copies = []
        for i, where in enumerate((near_west, near_east)):
            copies.append(remote(st_edge_send.at[step, i], st_edge_recv.at[step, i],
                                 ste_ss.at[step, i], ste_rs.at[step, i], where))
        for copy in copies:
            copy.start()
        pending.extend(copies)
        return copies

    def update(state, new, step, profile):
        rim_west = (mine_x == 0) & (spot == 0)
        rim_east = (mine_x == sect_tiles - 1) & (spot == blocks - 1)
        west_pack = jnp.where(rim_west, 0.0, st_edge_recv[step, 1])
        east_pack = jnp.where(rim_east, 0.0, st_edge_recv[step, 0])
        sides = {}
        for f, r, cut, slot in fold_slots():
            sides.setdefault((f, r), []).append((
                pltpu.roll(west_pack, (width - slot) % width, 1),
                pltpu.roll(east_pack, (width + seg - 1 - slot) % width, 1),
            ))
        for f in range(2):
            factor = -0.3 if f == 0 else 0.3
            for r in range(lines):
                v = state[f, r]
                w = jnp.where(place == 0, jnp.concatenate([x for x, _ in sides[f, r]]), pltpu.roll(v, 1, 1))
                e = jnp.where(place == seg - 1, jnp.concatenate([x for _, x in sides[f, r]]),
                              pltpu.roll(v, width - 1, 1))
                n = 0.0 if r == 0 else state[f, r - 1]
                s = 0.0 if r == lines - 1 else state[f, r + 1]
                n = pltpu.roll(jnp.where(level_lane >= width - seg, n, v), seg, 1)
                s = pltpu.roll(jnp.where(level_lane < seg, s, v), width - seg, 1)
                below = jnp.where(level_id == 0, 0.0, pltpu.roll(v, 1, 0))
                above = jnp.where(level_id == levels - 1, 0.0, pltpu.roll(v, levels - 1, 0))
                g = profile[f * levels:(f + 1) * levels, r * width:(r + 1) * width]
                new[f, r] = (v + 0.1 * (n + s + w + e - 4.0 * v)
                             + 0.1 * (above + below - 2.0 * v) + factor * g)

    loads[6].wait()
    for t in range(growth_v.shape[0] // LANES):
        column = column_of(growth_v[t * LANES:(t + 1) * LANES].reshape(1, LANES))
        grow_b[t * LANES:(t + 1) * LANES, :] = jnp.broadcast_to(0.1 * column, (LANES, width))

    def wind(state):
        out = []
        for r in range(lines):
            diff = state[0, r, 0:1, :] - state[1, r, 0:1, :]
            out.append(diff * diff)
        return out

    def fresh_part(b, wind_rows, target):
        weights = quartet_v[part(b), :]
        pair = jnp.dot(weights, cell_f[...], preferred_element_type=F32)
        quad = jnp.dot(weights, cell_s[...], preferred_element_type=F32)
        outs = []
        for r in range(lines):
            cut = slice(r * width, (r + 1) * width)
            f = cell_f[part(b), cut].astype(F32)
            top = f + 0.3 * (f * pair[:, cut] - quad[:, cut]) + grow_b[part(b), :] * wind_rows[r]
            out = (sea[r] * (top / (1.0 + 0.1 * (f * f)))).astype(BF16)
            target[part(b), cut] = out
            outs.append(out)
        return outs

    def square(b):
        f = cell_f[part(b), :].astype(F32)
        cell_s[part(b), :] = (f * f).astype(BF16)

    square(me)
    for b in order[::-1]:
        for i, dst in enumerate((cx_all, cy_all)):
            remote(dst.at[b], dst.at[b], c_send.at[i, 0], c_recv.at[i, b], block_id(b)).wait_recv()
        cxb[part(b), :] = jnp.broadcast_to(column_of(cx_all[b]), (comps, width))
        cyb[part(b), :] = jnp.broadcast_to(column_of(cy_all[b]), (comps, width))
    for b in order[::-1]:
        c = lax.div(b, lev_parts)
        core = lax.rem(b, lev_parts)
        there = st_in.at[c, pl.ds(pl.multiple_of(core * lown, 16), lown), :]
        remote(there, there, swap_ss.at[0], swap_rs.at[c, core], block_id(b)).wait_recv()
    for dc in range(1, cell_tiles):
        c = lax.rem(mine_c + dc, cell_tiles)
        remote(sea_in.at[c], sea_in.at[c], sea_ss.at[0], sea_rs.at[c], {"cells": c}).wait_recv()

    wide_lane = lax.broadcasted_iota(jnp.int32, (8, width), 1)
    sea = []
    for h in range(lines):
        low = st_in[2 * h].astype(F32)
        high = st_in[2 * h + 1].astype(F32)
        st0[0, h] = jnp.where(level_lane < mid, low, pltpu.roll(high, mid, 1))
        st0[1, h] = jnp.where(level_lane < mid, pltpu.roll(low, mid, 1), high)
        low = jnp.broadcast_to(sea_in[2 * h], (8, width))
        high = jnp.broadcast_to(sea_in[2 * h + 1], (8, width))
        sea.append(jnp.where(wide_lane < mid, low, pltpu.roll(high, mid, 1))[0:1])
    state_copies = send_state(st0, 0)

    loads[7].wait()
    loads[8].wait()
    for b in order[::-1]:
        for h in range(lines):
            cut = slice(h * width, (h + 1) * width)
            remote(cell_f.at[part(b), cut], cell_f.at[part(b), cut], f_send.at[0, 0], f_recv.at[b, h],
                   block_id(b)).wait_recv()
        square(b)

    wind_rows = wind(st0)
    first = jnp.zeros((comps, width), F32)
    last = jnp.zeros((comps, width), F32)
    for b in range(blocks):
        outs = fresh_part(b, wind_rows, e1)
        for r in range(lines):
            slot = b * lines + r
            v = outs[r].astype(F32)
            first = jnp.where(lane % seg == slot, pltpu.roll(v, slot, 1), first)
            last = jnp.where(lane % seg == slot, pltpu.roll(v, (slot + 1 - seg) % width, 1), last)
    edge_send[1, 0] = first.astype(BF16)
    edge_send[1, 1] = last.astype(BF16)
    edges = send_edges(1)

    @pl.when(inside == half - 1)
    def _():
        for i in (4, 6):
            for h in range(lines):
                send_line(wave[i], h)

    west_rim = lane % seg == 0
    east_rim = lane % seg == seg - 1
    for b in range(blocks):
        cx = cxb[part(b), :]
        cy = cyb[part(b), :]
        px, mx = halves(cx)
        py, my = halves(cy)
        keep = 1.0 - jnp.abs(cx) - jnp.abs(cy)
        field = [e1[part(b), r * width:(r + 1) * width].astype(F32) for r in range(lines)]
        for r in range(lines):
            v = field[r]
            north = pltpu.roll(jnp.where(lane >= width - seg, field[r - 1], v), seg, 1)
            south = pltpu.roll(jnp.where(lane < seg, field[(r + 1) % lines], v), width - seg, 1)
            to_west = jnp.where(west_rim, 0.0, pltpu.roll(v, 1, 1))
            to_east = jnp.where(east_rim, 0.0, pltpu.roll(v, width - 1, 1))
            inner[part(b), r * width:(r + 1) * width] = (
                v * keep + px * to_west + mx * to_east + py * north + my * south
            )

    for copy in state_copies:
        copy.wait_recv()
    update(st0, st1, 0, jnp.dot(coupler_v[...], e1[...], preferred_element_type=F32))
    state_copies = send_state(st1, 1)
    wind_rows = wind(st1)

    for copy in edges:
        copy.wait_recv()
    from_east = edge_recv[1, 0].astype(F32)
    from_west = edge_recv[1, 1].astype(F32)
    for b in range(blocks):
        px, mx = halves(cxb[part(b), :])
        for r in range(lines):
            slot = b * lines + r
            cut = slice(r * width, (r + 1) * width)
            beside = jnp.where(
                west_rim, px * pltpu.roll(from_west, (width - slot) % width, 1),
                mx * pltpu.roll(from_east, (width + seg - 1 - slot) % width, 1),
            )
            out = (inner[part(b), cut] + jnp.where(west_rim | east_rim, beside, 0.0)).astype(BF16)
            cell_f[part(b), cut] = out
            wide = out.astype(F32)
            cell_s[part(b), cut] = (wide * wide).astype(BF16)

    for d, b in enumerate(order + [me]):
        fresh_part(b, wind_rows, e2)
        if d < blocks - 1:
            copy = remote(e2.at[part(b), :], ret.at[spot], ret_ss.at[d], ret_rs.at[spot], block_id(b))
            copy.start()
            pending.append(copy)

    for copy in state_copies:
        copy.wait_recv()
    update(st1, st2, 1, jnp.dot(coupler_v[...], e2[...], preferred_element_type=F32))
    for h in range(lines):
        atm = st2[0, h]
        oce = st2[1, h]
        st_back[2 * h] = jnp.where(level_lane < mid, atm, pltpu.roll(oce, mid, 1)).astype(BF16)
        st_back[2 * h + 1] = jnp.where(level_lane < mid, pltpu.roll(atm, mid, 1), oce).astype(BF16)

    for d, b in enumerate(order):
        c = lax.div(b, lev_parts)
        core = lax.rem(b, lev_parts)
        copy = remote(st_back.at[c, pl.ds(pl.multiple_of(core * lown, 16), lown), :], fin.at[spot], back_ss.at[d],
                      back_rs.at[spot], block_id(b))
        copy.start()
        pending.append(copy)
    stores = [
        pltpu.make_async_copy(st_back.at[mine_c, my_levels, :], fin.at[spot], own_sem.at[0]),
        pltpu.make_async_copy(e2.at[part(me), :], ret.at[spot], own_sem.at[1]),
    ]
    for store in stores:
        store.start()
    for b in order[::-1]:
        t = tile_of(b)
        remote(e2.at[part(b), :], ret.at[t], ret_ss.at[0], ret_rs.at[t], block_id(b)).wait_recv()
    for b in order[::-1]:
        t = tile_of(b)
        remote(fin.at[t], fin.at[t], back_ss.at[0], back_rs.at[t], block_id(b)).wait_recv()

    for b in order:
        state_in(b).wait_send()
        for h in range(lines):
            remote(send_f.at[tile_of(b), h], send_f.at[tile_of(b), h], f_send.at[b, h], f_recv.at[0, 0],
                   block_id(b)).wait_send()
    for dc in range(1, cell_tiles):
        sea_over(lax.rem(mine_c + dc, cell_tiles)).wait_send()
    for copy in pending:
        copy.wait_send()
    for store in stores:
        store.wait()


def unpack_kernel(ret, fin, spec_out, atm_out, oce_out, atm_v, oce_v, flat, spec_v, out_sem):
    blocks, comps, cells = ret.shape
    rows, width = spec_v.shape[1:]
    lines = cells // width
    seg = width // blocks
    tile_rows = atm_v.shape[1]
    stores = []
    for h in range(lines):
        groups = swap_groups([ret[t, :, h * width:(h + 1) * width].astype(F32) for t in range(blocks)], seg)
        for g, line in enumerate(groups):
            flat[pl.ds(h * blocks + g, comps, stride=rows), :] = line
    pieces = 3 if comps % 3 == 0 else 1
    size = comps // pieces
    for p in range(pieces):
        cut = pl.ds(p * size, size)
        spec_v[cut] = flat[pl.ds(p * size * rows, size * rows), :].reshape(size, rows, width).astype(BF16)
        stores.append(pltpu.make_async_copy(spec_v.at[cut], spec_out.at[cut], out_sem.at[2 + p]))
        stores[-1].start()
    groups = swap_groups([fin[t].astype(F32) for t in range(blocks)], seg)
    for f, (target, out) in enumerate(((atm_v, atm_out), (oce_v, oce_out))):
        for r in range(tile_rows):
            target[:, r, :] = groups[f * tile_rows + r]
        stores.append(pltpu.make_async_copy(target, out, out_sem.at[f]))
        stores[-1].start()
    for store in stores:
        store.wait()


def fused(
    spectrum, courant_x, courant_y, growth, quartet, coupler, atmosphere, ocean_state, sea_mask
):
    cell_tiles = lax.axis_size("cells")
    lev_parts = lax.axis_size("lev")
    sect_tiles = lax.axis_size("sect")
    blocks = cell_tiles * lev_parts
    comps, rows, width = spectrum.shape
    total = comps * blocks
    lines = rows // blocks
    lown, tile_rows, _ = atmosphere.shape
    levels = lown * lev_parts
    cells = lines * width
    depth = levels // (width // blocks // (2 * lines))
    v = pltpu.VMEM
    dma = pltpu.SemaphoreType.DMA
    scratch = [
        v((comps, rows, width), BF16), v((1, comps), F32), v((1, comps), F32),
        v((total,), F32), v((total, total), BF16), v(coupler.shape, BF16),
        v((2, lown, tile_rows, width), F32), v(sea_mask.shape, jnp.int32),
        v((comps * rows, width), F32), v((rows, comps, width), F32),
        v((blocks, lines, comps, width), BF16), v((total, cells), BF16), v((total, cells), BF16),
        v((blocks, 1, comps), F32), v((blocks, 1, comps), F32),
        v((total, width), F32), v((total, width), F32), v((total, width), F32),
        v((NSTEP, 2, comps, width), BF16), v((NSTEP, 2, comps, width), BF16),
        v((total, cells), BF16), v((total, cells), BF16),
        v((blocks, lown, width), BF16), v((cell_tiles, levels, width), BF16),
        v((blocks, 1, width), F32), v((cell_tiles, 1, width), F32),
        v((2, lines, comps, width), F32), v((total, cells), F32),
        v((2, lines, levels, width), F32), v((2, lines, levels, width), F32),
        v((2, lines, levels, width), F32),
        v((NSTEP, 2, depth, width), F32), v((NSTEP, 2, depth, width), F32),
        v((cell_tiles, levels, width), BF16),
        dma((9,)), dma((2,)), dma((blocks, lines)), dma((blocks, lines)),
        dma((2, blocks)), dma((2, blocks)),
        dma((NSTEP, 2)), dma((NSTEP, 2)),
        dma((blocks,)), dma((cell_tiles, lev_parts)), dma((cell_tiles,)), dma((cell_tiles,)),
        dma((blocks,)), dma((blocks,)),
        dma((NSTEP, 2)), dma((NSTEP, 2)),
        dma((blocks,)), dma((blocks,)),
    ]
    anywhere = pl.BlockSpec(memory_space=pltpu.HBM)
    here = pl.BlockSpec(memory_space=pltpu.VMEM)
    column = jax.ShapeDtypeStruct(atmosphere.shape, F32)
    packed = pl.pallas_call(
        functools.partial(fused_kernel, cell_tiles, lev_parts, sect_tiles),
        out_shape=(v((blocks, comps, cells), BF16), v((blocks, lown, width), BF16)),
        in_specs=[anywhere] * 9,
        out_specs=(here,) * 2,
        scratch_shapes=scratch,
        compiler_params=pltpu.CompilerParams(
            collective_id=0, has_side_effects=True, vmem_limit_bytes=33554432
        ),
    )(*(
        pltpu.with_memory_space_constraint(x, pltpu.HBM)
        for x in (spectrum, courant_x.reshape(1, comps), courant_y.reshape(1, comps),
                  growth, quartet, coupler, atmosphere, ocean_state, sea_mask)
    ))
    return pl.pallas_call(
        unpack_kernel,
        out_shape=(jax.ShapeDtypeStruct(spectrum.shape, BF16), column, column),
        in_specs=[here] * 2,
        out_specs=(anywhere,) * 3,
        scratch_shapes=[
            v(atmosphere.shape, F32), v(atmosphere.shape, F32),
            v((comps * rows, width), F32), v(spectrum.shape, BF16), dma((5,)),
        ],
        compiler_params=pltpu.CompilerParams(vmem_limit_bytes=33554432),
    )(*packed)


def fits_fused(mesh, spectrum, coupler, atmosphere):
    lev_parts = lax.axis_size("lev")
    cells = lax.axis_size("cells")
    blocks = cells * lev_parts
    comps, rows, width = spectrum.shape
    return (
        lev_parts == 2 and cells == 4 and lax.axis_size("sect") % 2 == 0 and width == LANES
        and comps % 16 == 0 and rows == 2 * blocks and (comps * blocks) % LANES == 0
        and atmosphere.shape[0] % 16 == 0 and 2 * atmosphere.shape[1] == blocks
    )


def solution(mesh):
    in_specs = (
        P(("cells", "lev"), "groups", "sect"),
        P(("cells", "lev")),
        P(("cells", "lev")),
        P(),
        P(),
        P(),
        P("lev", ("groups", "cells"), "sect"),
        P("lev", ("groups", "cells"), "sect"),
        P(("groups", "cells"), "sect"),
    )
    out_specs = (
        P(("cells", "lev"), "groups", "sect"),
        P("lev", ("groups", "cells"), "sect"),
        P("lev", ("groups", "cells"), "sect"),
    )

    def body(*args):
        if fits_fused(mesh, args[0], args[5], args[6]):
            return fused(*args)
        return on_device(*args)

    return jax.shard_map(
        body, mesh=mesh, in_specs=in_specs, out_specs=out_specs, check_vma=False
    )
```

```python
import functools

import jax
import jax.numpy as jnp
from jax import lax
from jax.experimental import pallas as pl
from jax.experimental.pallas import tpu as pltpu
from jax.sharding import PartitionSpec as P

NSTEP = 2
LANES = 128
HELD = {6: {3: "edges", 2: "far"}}
F32 = jnp.float32
BF16 = jnp.bfloat16


def from_root(block, axis, source):
    block = jnp.where(lax.axis_index(axis) == source, block, jnp.zeros_like(block))
    return lax.psum(block, axis)


def extended_2(block, sides, width, periodic):
    for axis, dim in sides:
        count = lax.axis_size(axis)
        forward = [(i, i + 1) for i in range(count - 1)]
        if periodic:
            forward.append((count - 1, 0))
        backward = [(target, source) for source, target in forward]
        low = lax.ppermute(
            lax.slice_in_dim(block, block.shape[dim] - width, None, axis=dim), axis, forward
        )
        high = lax.ppermute(lax.slice_in_dim(block, 0, width, axis=dim), axis, backward)
        block = jnp.concatenate([low, block, high], axis=dim)
    return block


def upwind(values, courant, before, after):
    return jnp.maximum(courant, 0.0) * (values - before) + jnp.minimum(courant, 0.0) * (
        after - values
    )


def on_device(
    spectrum, courant_x, courant_y, growth, quartet, coupler, atmosphere, ocean_state, sea_mask
):
    cell_tiles = lax.axis_size("cells")
    lev_parts = lax.axis_size("lev")
    blocks = cell_tiles * lev_parts
    comps_own, rows_all, row_width = spectrum.shape
    total_comps = comps_own * blocks
    cell_rows = rows_all // blocks
    level_count = coupler.shape[0] // 2
    row_start = lax.axis_index("lev") * cell_rows
    shift_x = courant_x[:, None, None]
    shift_y = courant_y[:, None, None]
    sea_rows = (
        lax.dynamic_slice_in_dim(sea_mask, row_start, cell_rows, 0)
        .astype(jnp.float32)
        .reshape(1, cell_rows * row_width)
    )
    growth_column = growth[:, None]
    forcing_sign = jnp.array([-0.3, 0.3], jnp.float32)[:, None, None, None]
    state = jnp.stack([atmosphere, ocean_state])
    energy = spectrum
    for counter in range(NSTEP):
        surface = from_root(state[:, 0], "lev", 0)
        surface_wind = surface[0] - surface[1]
        wind_rows = lax.dynamic_slice_in_dim(
            surface_wind * surface_wind, row_start, cell_rows, 0
        ).reshape(1, cell_rows * row_width)
        padded = extended_2(energy, (("sect", 2),), 1, True)
        values = padded[:, :, 1:-1].astype(jnp.float32)
        west_side = padded[:, :, :-2].astype(jnp.float32)
        east_side = padded[:, :, 2:].astype(jnp.float32)
        moved = values - upwind(values, shift_x, west_side, east_side)
        moved = moved - upwind(
            values, shift_y, jnp.roll(values, 1, axis=1), jnp.roll(values, -1, axis=1)
        )
        advected = moved.astype(jnp.bfloat16)
        pieces = advected.reshape(1, comps_own, blocks, cell_rows, row_width)
        on_cells = lax.all_to_all(pieces, ("cells", "lev"), split_axis=2, concat_axis=0, tiled=True)
        on_cells = on_cells.reshape(total_comps, cell_rows * row_width)
        cell_values = on_cells.astype(jnp.float32)
        paired = jnp.dot(quartet, on_cells, preferred_element_type=jnp.float32)
        squared = (cell_values * cell_values).astype(jnp.bfloat16)
        quad_square = jnp.dot(quartet, squared, preferred_element_type=jnp.float32)
        fresh = (
            cell_values
            + 0.3 * (cell_values * paired - quad_square)
            + 0.1 * growth_column * wind_rows
        ) / (1.0 + 0.1 * cell_values * cell_values)
        fresh = (fresh * sea_rows).astype(jnp.bfloat16)
        profile = jnp.dot(coupler, fresh, preferred_element_type=jnp.float32).reshape(
            2, level_count, cell_rows, row_width
        )
        forcing = lax.all_to_all(profile, "lev", split_axis=1, concat_axis=2, tiled=True)
        returned = fresh.reshape(blocks, comps_own, 1, cell_rows, row_width)
        returned = lax.all_to_all(
            returned, ("cells", "lev"), split_axis=0, concat_axis=2, tiled=True
        )
        energy = returned.reshape(comps_own, rows_all, row_width)
        extended = extended_2(state, (("lev", 1), ("cells", 2), ("sect", 3)), 1, False)
        middle = extended[:, 1:-1, 1:-1, 1:-1]
        lateral = (
            extended[:, 1:-1, 2:, 1:-1]
            + extended[:, 1:-1, :-2, 1:-1]
            + extended[:, 1:-1, 1:-1, 2:]
            + extended[:, 1:-1, 1:-1, :-2]
            - 4.0 * middle
        )
        upright = extended[:, 2:, 1:-1, 1:-1] + extended[:, :-2, 1:-1, 1:-1] - 2.0 * middle
        state = middle + 0.1 * lateral + 0.1 * upright + forcing_sign * forcing
    return (energy, state[0], state[1])


def column_of(row):
    n = row.shape[1]
    down = lax.broadcasted_iota(jnp.int32, (n, n), 0)
    across = lax.broadcasted_iota(jnp.int32, (n, n), 1)
    return jnp.sum(jnp.where(down == across, row, 0.0), axis=1, keepdims=True)


def swap_groups(vectors, seg):
    count = len(vectors)
    width = vectors[0].shape[1]
    group = lax.broadcasted_iota(jnp.int32, vectors[0].shape, 1) // seg
    dist = count // 2
    vectors = list(vectors)
    while dist:
        even = (group // dist) % 2 == 0
        for i in range(count):
            if (i // dist) % 2 == 0:
                x, y = vectors[i], vectors[i + dist]
                if 2 * dist * seg == width:
                    moved = pltpu.roll(jnp.where(even, y, x), dist * seg, 1)
                    vectors[i], vectors[i + dist] = jnp.where(even, x, moved), jnp.where(even, moved, y)
                else:
                    vectors[i] = jnp.where(even, x, pltpu.roll(y, dist * seg, 1))
                    vectors[i + dist] = jnp.where(even, pltpu.roll(x, width - dist * seg, 1), y)
        dist //= 2
    return vectors


def fused_kernel(
    cell_tiles, lev_parts, sect_tiles,
    spec_hbm, cx_hbm, cy_hbm, growth_hbm, quartet_hbm, coupler_hbm, atm_hbm, oce_hbm, sea_hbm,
    ret, fin,
    spec_v, c_v, growth_v, quartet_v, coupler_v, col_in, sea_v,
    flat, rows_v, send_f, cell_f, cell_s, c_all, cxb, cyb, grow_b,
    edge_send, edge_recv, e1, e2,
    swap_send, st_in, sea_send, sea_in, outer, inner, stage_v, total_v, st0, st1, st2, st_edge_send, st_edge_recv, st_back,
    in_sem, own_sem, f_send, f_recv, c_send, c_recv,
    edge_ss, edge_rs, swap_ss, swap_rs, sea_ss, sea_rs, back_ss, back_rs, ste_ss, ste_rs,
    ret_ss, ret_rs,
):
    blocks = cell_tiles * lev_parts
    comps, rows, width = spec_v.shape
    lines = rows // blocks
    lown = col_in.shape[1]
    tile_rows = col_in.shape[2]
    levels = lown * lev_parts
    cells = lines * width
    seg = width // blocks
    mid = width // 2
    mine_c = lax.axis_index("cells")
    mine_l = lax.axis_index("lev")
    mine_x = lax.axis_index("sect")
    me = mine_c * lev_parts + mine_l
    turned = lax.rem(mine_x, 2) == 1
    side = lax.div(mine_c, cell_tiles // 2)

    def tile_of(b):
        return jnp.where(turned, blocks - 1 - b, b)

    def mirrored(b):
        return jnp.where(side == 1, blocks - 1 - b, b)

    def block_id(b):
        return {"cells": lax.div(b, lev_parts), "lev": lax.rem(b, lev_parts)}

    spot = tile_of(me)
    inside = mirrored(me)
    west = {"sect": lax.rem(mine_x + sect_tiles - 1, sect_tiles)}
    east = {"sect": lax.rem(mine_x + 1, sect_tiles)}
    near_west = {
        **block_id(jnp.where(spot == 0, me, tile_of(spot - 1))),
        "sect": jnp.where(spot == 0, west["sect"], mine_x),
    }
    near_east = {
        **block_id(jnp.where(spot == blocks - 1, me, tile_of(spot + 1))),
        "sect": jnp.where(spot == blocks - 1, east["sect"], mine_x),
    }
    half = blocks // 2
    odd = lax.rem(inside, 2)
    across = [mirrored(blocks - 1 - i + (1 - 2 * (i % 2)) * -odd) for i in range(half)]
    mate = (1 - lax.div(inside, lev_parts)) * lev_parts
    mates = [mirrored(mate + k) for k in range(lev_parts)]
    order = across + mates + [mirrored(inside + 1 - 2 * odd)]

    def part(b):
        return pl.ds(pl.multiple_of(b * comps, 16), comps)

    def remote(src, dst, ss, rs, where):
        return pltpu.make_async_remote_copy(
            src_ref=src, dst_ref=dst, send_sem=ss, recv_sem=rs,
            device_id=where, device_id_type=pl.DeviceIdType.MESH,
        )

    loads = [
        pltpu.make_async_copy(a, b, in_sem.at[i])
        for i, (a, b) in enumerate([
            (spec_hbm, spec_v), (cx_hbm, c_v.at[0]), (cy_hbm, c_v.at[1]),
            (atm_hbm, col_in.at[0]), (oce_hbm, col_in.at[1]), (sea_hbm, sea_v),
            (growth_hbm, growth_v), (coupler_hbm, coupler_v), (quartet_hbm, quartet_v),
        ])
    ]

    def whole(ref, sem):
        return remote(ref, ref, sem, sem, {"lev": 1 - mine_l})
    for load in loads:
        load.start()

    barrier = pltpu.get_barrier_semaphore()
    for d in range(1, blocks):
        pl.semaphore_signal(barrier, inc=1, device_id=block_id(lax.rem(me + d, blocks)),
                            device_id_type=pl.DeviceIdType.MESH)
    for side_id in (west, east, near_west, near_east):
        pl.semaphore_signal(barrier, inc=1, device_id=side_id,
                            device_id_type=pl.DeviceIdType.MESH)

    my_levels = pl.ds(pl.multiple_of(mine_l * lown, 16), lown)

    def state_in(b):
        return remote(swap_send.at[tile_of(b)], st_in.at[mine_c, my_levels, :], swap_ss.at[0],
                      swap_rs.at[0], block_id(b))

    def sea_over(c):
        return remote(sea_send.at[tile_of(c * lev_parts + mine_l)], sea_in.at[mine_c], sea_ss.at[0],
                      sea_rs.at[0], {"cells": c})

    loads[3].wait()
    loads[4].wait()
    loads[5].wait()
    groups = [col_in[f, :, r, :] for f in range(2) for r in range(tile_rows)]
    for t, line in enumerate(swap_groups(groups, seg)):
        swap_send[t] = line.astype(BF16)
    groups = [jnp.broadcast_to(sea_v[r:r + 1, :].astype(F32), (8, width)) for r in range(tile_rows)]
    for t, line in enumerate(swap_groups(groups + [jnp.zeros((8, width), F32)] * tile_rows, seg)):
        sea_send[t] = line[0:1]
    st_in[mine_c, my_levels, :] = swap_send[spot]
    sea_in[mine_c] = sea_send[spot]

    lane = lax.broadcasted_iota(jnp.int32, (comps, width), 1)
    loads[0].wait()
    flat[...] = spec_v[...].astype(F32).reshape(comps * rows, width)
    first = jnp.zeros((comps, width), F32)
    last = jnp.zeros((comps, width), F32)
    for r in range(rows):
        v = flat[pl.ds(r, comps, stride=rows), :]
        rows_v[r] = v
        place = (r % blocks) * seg + r // blocks
        first = jnp.where(lane == place, pltpu.roll(v, place, 1), first)
        last = jnp.where(lane == place, pltpu.roll(v, (place + 1) % width, 1), last)
    edge_send[0, 0] = first.astype(BF16)
    edge_send[0, 1] = last.astype(BF16)

    pl.semaphore_wait(barrier, blocks + 3)
    def send_edges(step):
        copies = [
            remote(edge_send.at[step, i], edge_recv.at[step, i], edge_ss.at[0], edge_rs.at[step], where)
            for i, where in enumerate((west, east) if step == 0 else (near_west, near_east))
        ]
        for copy in copies:
            copy.start()

    send_edges(0)
    wave = [mirrored(i) for i in sorted(range(blocks), key=lambda i: (abs(2 * i + 1 - blocks), -i))]

    for b in wave:
        @pl.when(b != me)
        def _():
            state_in(b).start()
    for dc in range(1, cell_tiles):
        sea_over(lax.rem(mine_c + dc, cell_tiles)).start()
    loads[1].wait()
    loads[2].wait()
    for b in order:
        remote(c_v, c_all.at[me], c_send.at[0], c_recv.at[0], block_id(b)).start()

    def halves(c):
        return jnp.maximum(c, 0.0), jnp.maximum(-c, 0.0)

    cxb[part(me), :] = jnp.broadcast_to(column_of(c_v[0]), (comps, width))
    cyb[part(me), :] = jnp.broadcast_to(column_of(c_v[1]), (comps, width))

    def send_line(b, h):
        t = tile_of(b)
        cut = slice(h * width, (h + 1) * width)

        @pl.when(b != me)
        def _():
            remote(send_f.at[t, h], cell_f.at[part(me), cut], f_send.at[0], f_recv.at[me],
                   block_id(b)).start()

        @pl.when(b == me)
        def _():
            cell_f[part(me), cut] = send_f[spot, h]

    chunk = comps
    small = lax.broadcasted_iota(jnp.int32, (chunk, width), 1)

    early = [jnp.where(inside < lev_parts, wave[i], wave[j]) for i, j in ((1, 0), (3, 1), (0, 2), (2, 3))]
    for h in range(lines):
        for k in range(0, comps, chunk):
            own = pl.ds(pl.multiple_of(me * comps + k, 16), chunk)
            cx = cxb[own, :]
            cy = cyb[own, :]
            px, mx = halves(cx)
            py, my = halves(cy)
            keep = 1.0 - jnp.abs(cx) - jnp.abs(cy)
            groups = []
            for g in range(blocks):
                row = h * blocks + g
                v = rows_v[row, k:k + chunk]
                to_west = jnp.where(small == 0, 0.0, pltpu.roll(v, 1, 1))
                to_east = jnp.where(small == width - 1, 0.0, pltpu.roll(v, width - 1, 1))
                groups.append(
                    v * keep + px * to_west + mx * to_east
                    + py * rows_v[(row + rows - 1) % rows, k:k + chunk] + my * rows_v[(row + 1) % rows, k:k + chunk]
                )
            for t, line in enumerate(swap_groups(groups, seg)):
                if 0 < t < blocks - 1:
                    send_f[t, h, k:k + chunk] = line.astype(BF16)
                else:
                    outer[min(t, 1), h, k:k + chunk] = line
        for b in early[:2]:
            send_line(b, h)
    for b in early[2:]:
        for h in range(lines):
            send_line(b, h)

    def release(now, position):
        ready = [p for p, when in HELD.get(position, {}).items() if when == now]
        if now == "start":
            late = [p for p, when in HELD.get(position, {}).items() if when != now]
            ready = [p for p in range(half) if p not in late]
        if len(ready) == half:
            for h in range(lines):
                send_line(wave[position], h)
        elif ready:
            hit = inside == ready[0]
            for p in ready[1:]:
                hit = hit | (inside == p)

            @pl.when(hit)
            def _():
                for h in range(lines):
                    send_line(wave[position], h)

    release("start", 4)
    for h in range(lines):
        send_line(wave[5], h)
    whole(edge_recv.at[0], edge_rs.at[0]).wait_recv()
    for k in range(0, comps, chunk):
        cx = cxb[pl.ds(pl.multiple_of(me * comps + k, 16), chunk), :]
        px, mx = halves(cx)
        from_east = edge_recv[0, 0, k:k + chunk].astype(F32)
        from_west = edge_recv[0, 1, k:k + chunk].astype(F32)
        for h in range(lines):
            west_part = jnp.where(small % seg == 0, pltpu.roll(from_west, (width - h) % width, 1), 0.0)
            east_part = jnp.where(small % seg == seg - 1, pltpu.roll(from_east, seg - 1 - h, 1), 0.0)
            send_f[0, h, k:k + chunk] = (outer[0, h, k:k + chunk] + px * west_part).astype(BF16)
            send_f[blocks - 1, h, k:k + chunk] = (outer[1, h, k:k + chunk] + mx * east_part).astype(BF16)
    release("start", 6)
    for h in range(lines):
        send_line(wave[7], h)

    level_id = lax.broadcasted_iota(jnp.int32, (levels, width), 0)
    level_lane = lax.broadcasted_iota(jnp.int32, (levels, width), 1)
    place = level_lane % seg
    folds = seg // (2 * lines)
    depth = levels // folds
    fold_place = place[:depth]

    def fold_slots():
        for f in range(2):
            for r in range(lines):
                for q in range(folds):
                    yield f, r, slice(q * depth, (q + 1) * depth), (q * 2 + f) * lines + r

    def send_state(state, step):
        west_pack = jnp.zeros((depth, width), F32)
        east_pack = jnp.zeros((depth, width), F32)
        for f, r, cut, slot in fold_slots():
            v = state[f, r, cut]
            west_pack = jnp.where(fold_place == slot, pltpu.roll(v, slot, 1), west_pack)
            east_pack = jnp.where(fold_place == slot, pltpu.roll(v, (slot + 1 - seg) % width, 1), east_pack)
        st_edge_send[step, 0] = west_pack
        st_edge_send[step, 1] = east_pack
        for i, where in enumerate((near_west, near_east)):
            remote(st_edge_send.at[step, i], st_edge_recv.at[step, i], ste_ss.at[0], ste_rs.at[step], where).start()

    def update(state, new, step, profile):
        rim_west = (mine_x == 0) & (spot == 0)
        rim_east = (mine_x == sect_tiles - 1) & (spot == blocks - 1)
        west_pack = jnp.where(rim_west, 0.0, st_edge_recv[step, 1])
        east_pack = jnp.where(rim_east, 0.0, st_edge_recv[step, 0])
        sides = {}
        for f, r, cut, slot in fold_slots():
            sides.setdefault((f, r), []).append((
                pltpu.roll(west_pack, (width - slot) % width, 1),
                pltpu.roll(east_pack, (width + seg - 1 - slot) % width, 1),
            ))
        for f in range(2):
            factor = -0.3 if f == 0 else 0.3
            for r in range(lines):
                v = state[f, r]
                w = jnp.where(place == 0, jnp.concatenate([x for x, _ in sides[f, r]]), pltpu.roll(v, 1, 1))
                e = jnp.where(place == seg - 1, jnp.concatenate([x for _, x in sides[f, r]]),
                              pltpu.roll(v, width - 1, 1))
                n = 0.0 if r == 0 else state[f, r - 1]
                s = 0.0 if r == lines - 1 else state[f, r + 1]
                n = pltpu.roll(jnp.where(level_lane >= width - seg, n, v), seg, 1)
                s = pltpu.roll(jnp.where(level_lane < seg, s, v), width - seg, 1)
                below = jnp.where(level_id == 0, 0.0, pltpu.roll(v, 1, 0))
                above = jnp.where(level_id == levels - 1, 0.0, pltpu.roll(v, levels - 1, 0))
                g = profile[f * levels:(f + 1) * levels, r * width:(r + 1) * width]
                new[f, r] = (v + 0.1 * (n + s + w + e - 4.0 * v)
                             + 0.1 * (above + below - 2.0 * v) + factor * g)

    loads[6].wait()
    for t in range(growth_v.shape[0] // LANES):
        column = column_of(growth_v[t * LANES:(t + 1) * LANES].reshape(1, LANES))
        grow_b[t * LANES:(t + 1) * LANES, :] = jnp.broadcast_to(0.1 * column, (LANES, width))

    def wind(state):
        out = []
        for r in range(lines):
            diff = state[0, r, 0:1, :] - state[1, r, 0:1, :]
            out.append(diff * diff)
        return out

    def fresh_part(b, wind_rows, target, pair, quad):
        outs = []
        for r in range(lines):
            cut = slice(r * width, (r + 1) * width)
            f = cell_f[part(b), cut].astype(F32)
            top = f + 0.3 * (f * pair[:, cut] - quad[:, cut]) + grow_b[part(b), :] * wind_rows[r]
            out = (sea[r] * (top / (1.0 + 0.1 * (f * f)))).astype(BF16)
            target[part(b), cut] = out
            outs.append(out)
        return outs

    others = pl.ds(0, blocks - 1)
    whole(c_all.at[others], c_recv.at[0]).wait_recv()
    for b in order:
        cxb[part(b), :] = jnp.broadcast_to(column_of(c_all[b, 0]), (comps, width))
        cyb[part(b), :] = jnp.broadcast_to(column_of(c_all[b, 1]), (comps, width))
    whole(swap_send.at[others], swap_rs.at[0]).wait_recv()
    whole(sea_send.at[pl.ds(0, cell_tiles - 1)], sea_rs.at[0]).wait_recv()

    wide_lane = lax.broadcasted_iota(jnp.int32, (8, width), 1)
    sea = []
    for h in range(lines):
        low = st_in[2 * h].astype(F32)
        high = st_in[2 * h + 1].astype(F32)
        st0[0, h] = jnp.where(level_lane < mid, low, pltpu.roll(high, mid, 1))
        st0[1, h] = jnp.where(level_lane < mid, pltpu.roll(low, mid, 1), high)
        low = jnp.broadcast_to(sea_in[2 * h], (8, width))
        high = jnp.broadcast_to(sea_in[2 * h + 1], (8, width))
        sea.append(jnp.where(wide_lane < mid, low, pltpu.roll(high, mid, 1))[0:1])
    send_state(st0, 0)

    loads[7].wait()
    loads[8].wait()

    near = half * comps
    span = stage_v.shape[2]
    spare = span - near
    for i in range(2):
        for x in range(2):
            stage_v[i, x, (1 - i) * near:(1 - i) * near + spare] = jnp.zeros((spare, cells), BF16)

    def stage(b):
        f = cell_f[part(b), :]
        wide = f.astype(F32)
        which = lax.div(b, half)
        rows_of = pl.ds(pl.multiple_of(which * spare + (b - which * half) * comps, 16), comps)
        stage_v[which, 0, rows_of, :] = f
        stage_v[which, 1, rows_of, :] = (wide * wide).astype(BF16)

    def products(rows_of, which):
        weights = quartet_v[rows_of, pl.ds(pl.multiple_of(which * (quartet_v.shape[1] - span), LANES), span)]
        return [jnp.dot(weights, stage_v[which, i], preferred_element_type=F32) for i in range(2)]

    def arrived(b):
        whole(cell_f.at[part(b), :], f_recv.at[b]).wait_recv()
        stage(b)

    stage(me)
    for b in order[half:][::-1]:
        arrived(b)
    for m in range(blocks):
        for i, x in enumerate(products(part(m), side)):
            total_v[i, part(m), :] = x
    for b in order[:half][::-1]:
        arrived(b)
    release("far", 6)

    wind_rows = wind(st0)
    first = jnp.zeros((comps, width), F32)
    last = jnp.zeros((comps, width), F32)
    for b in range(blocks):
        pair, quad = [total_v[i, part(b), :] + x
                      for i, x in enumerate(products(part(b), 1 - side))]
        outs = fresh_part(b, wind_rows, e1, pair, quad)
        for r in range(lines):
            slot = b * lines + r
            v = outs[r].astype(F32)
            first = jnp.where(lane % seg == slot, pltpu.roll(v, slot, 1), first)
            last = jnp.where(lane % seg == slot, pltpu.roll(v, (slot + 1 - seg) % width, 1), last)
    edge_send[1, 0] = first.astype(BF16)
    edge_send[1, 1] = last.astype(BF16)
    send_edges(1)
    release("edges", 6)

    west_rim = lane % seg == 0
    east_rim = lane % seg == seg - 1
    for b in range(blocks):
        cx = cxb[part(b), :]
        cy = cyb[part(b), :]
        px, mx = halves(cx)
        py, my = halves(cy)
        keep = 1.0 - jnp.abs(cx) - jnp.abs(cy)
        field = [e1[part(b), r * width:(r + 1) * width].astype(F32) for r in range(lines)]
        for r in range(lines):
            v = field[r]
            north = pltpu.roll(jnp.where(lane >= width - seg, field[r - 1], v), seg, 1)
            south = pltpu.roll(jnp.where(lane < seg, field[(r + 1) % lines], v), width - seg, 1)
            to_west = jnp.where(west_rim, 0.0, pltpu.roll(v, 1, 1))
            to_east = jnp.where(east_rim, 0.0, pltpu.roll(v, width - 1, 1))
            inner[part(b), r * width:(r + 1) * width] = (
                v * keep + px * to_west + mx * to_east + py * north + my * south
            )

    whole(st_edge_recv.at[0], ste_rs.at[0]).wait_recv()
    update(st0, st1, 0, jnp.dot(coupler_v[...], e1[...], preferred_element_type=F32))
    send_state(st1, 1)
    wind_rows = wind(st1)

    whole(edge_recv.at[1], edge_rs.at[1]).wait_recv()
    from_east = edge_recv[1, 0].astype(F32)
    from_west = edge_recv[1, 1].astype(F32)
    for b in range(blocks):
        px, mx = halves(cxb[part(b), :])
        for r in range(lines):
            slot = b * lines + r
            cut = slice(r * width, (r + 1) * width)
            beside = jnp.where(
                west_rim, px * pltpu.roll(from_west, (width - slot) % width, 1),
                mx * pltpu.roll(from_east, (width + seg - 1 - slot) % width, 1),
            )
            out = (inner[part(b), cut] + jnp.where(west_rim | east_rim, beside, 0.0)).astype(BF16)
            cell_f[part(b), cut] = out
            wide = out.astype(F32)
            cell_s[part(b), cut] = (wide * wide).astype(BF16)

    for b in order + [me]:
        weights = quartet_v[part(b), :]
        pair = jnp.dot(weights, cell_f[...], preferred_element_type=F32)
        quad = jnp.dot(weights, cell_s[...], preferred_element_type=F32)
        fresh_part(b, wind_rows, e2, pair, quad)
        if b is not me:
            remote(e2.at[part(b), :], ret.at[spot], ret_ss.at[0], ret_rs.at[0], block_id(b)).start()

    whole(st_edge_recv.at[1], ste_rs.at[1]).wait_recv()
    update(st1, st2, 1, jnp.dot(coupler_v[...], e2[...], preferred_element_type=F32))
    for h in range(lines):
        atm = st2[0, h]
        oce = st2[1, h]
        st_back[2 * h] = jnp.where(level_lane < mid, atm, pltpu.roll(oce, mid, 1)).astype(BF16)
        st_back[2 * h + 1] = jnp.where(level_lane < mid, pltpu.roll(atm, mid, 1), oce).astype(BF16)

    for b in order:
        c = lax.div(b, lev_parts)
        core = lax.rem(b, lev_parts)
        remote(st_back.at[c, pl.ds(pl.multiple_of(core * lown, 16), lown), :], fin.at[spot], back_ss.at[0],
               back_rs.at[0], block_id(b)).start()
    stores = [
        pltpu.make_async_copy(st_back.at[mine_c, my_levels, :], fin.at[spot], own_sem.at[0]),
        pltpu.make_async_copy(e2.at[part(me), :], ret.at[spot], own_sem.at[1]),
    ]
    for store in stores:
        store.start()
    whole(ret.at[others], ret_rs.at[0]).wait_recv()
    whole(fin.at[others], back_rs.at[0]).wait_recv()

    whole(send_f.at[others], f_send.at[0]).wait_send()
    whole(c_all.at[others], c_send.at[0]).wait_send()
    whole(swap_send.at[others], swap_ss.at[0]).wait_send()
    whole(sea_send.at[pl.ds(0, cell_tiles - 1)], sea_ss.at[0]).wait_send()
    whole(edge_send, edge_ss.at[0]).wait_send()
    whole(st_edge_send, ste_ss.at[0]).wait_send()
    whole(ret.at[others], ret_ss.at[0]).wait_send()
    whole(fin.at[others], back_ss.at[0]).wait_send()
    for store in stores:
        store.wait()


def unpack_kernel(ret, fin, spec_out, atm_out, oce_out, atm_v, oce_v, flat, spec_v, out_sem):
    blocks, comps, cells = ret.shape
    rows, width = spec_v.shape[1:]
    lines = cells // width
    seg = width // blocks
    tile_rows = atm_v.shape[1]
    stores = []
    for h in range(lines):
        groups = swap_groups([ret[t, :, h * width:(h + 1) * width].astype(F32) for t in range(blocks)], seg)
        for g, line in enumerate(groups):
            flat[pl.ds(h * blocks + g, comps, stride=rows), :] = line
    pieces = 3 if comps % 3 == 0 else 1
    size = comps // pieces
    for p in range(pieces):
        cut = pl.ds(p * size, size)
        spec_v[cut] = flat[pl.ds(p * size * rows, size * rows), :].reshape(size, rows, width).astype(BF16)
        stores.append(pltpu.make_async_copy(spec_v.at[cut], spec_out.at[cut], out_sem.at[2 + p]))
        stores[-1].start()
    groups = swap_groups([fin[t].astype(F32) for t in range(blocks)], seg)
    for f, (target, out) in enumerate(((atm_v, atm_out), (oce_v, oce_out))):
        for r in range(tile_rows):
            target[:, r, :] = groups[f * tile_rows + r]
        stores.append(pltpu.make_async_copy(target, out, out_sem.at[f]))
        stores[-1].start()
    for store in stores:
        store.wait()


def fused(
    spectrum, courant_x, courant_y, growth, quartet, coupler, atmosphere, ocean_state, sea_mask
):
    cell_tiles = lax.axis_size("cells")
    lev_parts = lax.axis_size("lev")
    sect_tiles = lax.axis_size("sect")
    blocks = cell_tiles * lev_parts
    comps, rows, width = spectrum.shape
    total = comps * blocks
    lines = rows // blocks
    lown, tile_rows, _ = atmosphere.shape
    levels = lown * lev_parts
    cells = lines * width
    depth = levels // (width // blocks // (2 * lines))
    v = pltpu.VMEM
    dma = pltpu.SemaphoreType.DMA
    scratch = [
        v((comps, rows, width), BF16), v((2, 1, comps), F32),
        v((total,), F32), v((total, total), BF16), v(coupler.shape, BF16),
        v((2, lown, tile_rows, width), F32), v(sea_mask.shape, jnp.int32),
        v((comps * rows, width), F32), v((rows, comps, width), F32),
        v((blocks, lines, comps, width), BF16), v((total, cells), BF16), v((total, cells), BF16),
        v((blocks, 2, 1, comps), F32),
        v((total, width), F32), v((total, width), F32), v((total, width), F32),
        v((NSTEP, 2, comps, width), BF16), v((NSTEP, 2, comps, width), BF16),
        v((total, cells), BF16), v((total, cells), BF16),
        v((blocks, lown, width), BF16), v((cell_tiles, levels, width), BF16),
        v((blocks, 1, width), F32), v((cell_tiles, 1, width), F32),
        v((2, lines, comps, width), F32), v((total, cells), F32),
        v((2, 2, -(-total // (2 * LANES)) * LANES, cells), BF16), v((2, total, cells), F32),
        v((2, lines, levels, width), F32), v((2, lines, levels, width), F32),
        v((2, lines, levels, width), F32),
        v((NSTEP, 2, depth, width), F32), v((NSTEP, 2, depth, width), F32),
        v((cell_tiles, levels, width), BF16),
        dma((9,)), dma((2,)), dma((1,)), dma((blocks,)), dma((1,)), dma((1,)),
        dma((1,)), dma((NSTEP,)),
        dma((1,)), dma((1,)), dma((1,)), dma((1,)),
        dma((1,)), dma((1,)),
        dma((1,)), dma((NSTEP,)),
        dma((1,)), dma((1,)),
    ]
    anywhere = pl.BlockSpec(memory_space=pltpu.HBM)
    here = pl.BlockSpec(memory_space=pltpu.VMEM)
    column = jax.ShapeDtypeStruct(atmosphere.shape, F32)
    packed = pl.pallas_call(
        functools.partial(fused_kernel, cell_tiles, lev_parts, sect_tiles),
        out_shape=(v((blocks, comps, cells), BF16), v((blocks, lown, width), BF16)),
        in_specs=[anywhere] * 9,
        out_specs=(here,) * 2,
        scratch_shapes=scratch,
        compiler_params=pltpu.CompilerParams(
            collective_id=0, has_side_effects=True, vmem_limit_bytes=33554432
        ),
    )(*(
        pltpu.with_memory_space_constraint(x, pltpu.HBM)
        for x in (spectrum, courant_x.reshape(1, comps), courant_y.reshape(1, comps),
                  growth, quartet, coupler, atmosphere, ocean_state, sea_mask)
    ))
    return pl.pallas_call(
        unpack_kernel,
        out_shape=(jax.ShapeDtypeStruct(spectrum.shape, BF16), column, column),
        in_specs=[here] * 2,
        out_specs=(anywhere,) * 3,
        scratch_shapes=[
            v(atmosphere.shape, F32), v(atmosphere.shape, F32),
            v((comps * rows, width), F32), v(spectrum.shape, BF16), dma((5,)),
        ],
        compiler_params=pltpu.CompilerParams(vmem_limit_bytes=33554432),
    )(*packed)


def fits_fused(mesh, spectrum, coupler, atmosphere):
    lev_parts = lax.axis_size("lev")
    cells = lax.axis_size("cells")
    blocks = cells * lev_parts
    comps, rows, width = spectrum.shape
    return (
        lev_parts == 2 and cells == 4 and lax.axis_size("sect") % 2 == 0 and width == LANES
        and comps % 16 == 0 and rows == 2 * blocks and (comps * blocks) % LANES == 0
        and atmosphere.shape[0] % 16 == 0 and 2 * atmosphere.shape[1] == blocks
    )


def solution(mesh):
    in_specs = (
        P(("cells", "lev"), "groups", "sect"),
        P(("cells", "lev")),
        P(("cells", "lev")),
        P(),
        P(),
        P(),
        P("lev", ("groups", "cells"), "sect"),
        P("lev", ("groups", "cells"), "sect"),
        P(("groups", "cells"), "sect"),
    )
    out_specs = (
        P(("cells", "lev"), "groups", "sect"),
        P("lev", ("groups", "cells"), "sect"),
        P("lev", ("groups", "cells"), "sect"),
    )

    def body(*args):
        if fits_fused(mesh, args[0], args[5], args[6]):
            return fused(*args)
        return on_device(*args)

    return jax.shard_map(
        body, mesh=mesh, in_specs=in_specs, out_specs=out_specs, check_vma=False
    )
```

```python
import functools

import jax
import jax.numpy as jnp
from jax import lax
from jax.experimental import pallas as pl
from jax.experimental.pallas import tpu as pltpu
from jax.sharding import PartitionSpec as P

NSTEP = 2
LANES = 128
HELD = {6: {3: "edges", 2: "far"}}
F32 = jnp.float32
BF16 = jnp.bfloat16


def from_root(block, axis, source):
    block = jnp.where(lax.axis_index(axis) == source, block, jnp.zeros_like(block))
    return lax.psum(block, axis)


def extended_2(block, sides, width, periodic):
    for axis, dim in sides:
        count = lax.axis_size(axis)
        forward = [(i, i + 1) for i in range(count - 1)]
        if periodic:
            forward.append((count - 1, 0))
        backward = [(target, source) for source, target in forward]
        low = lax.ppermute(
            lax.slice_in_dim(block, block.shape[dim] - width, None, axis=dim), axis, forward
        )
        high = lax.ppermute(lax.slice_in_dim(block, 0, width, axis=dim), axis, backward)
        block = jnp.concatenate([low, block, high], axis=dim)
    return block


def upwind(values, courant, before, after):
    return jnp.maximum(courant, 0.0) * (values - before) + jnp.minimum(courant, 0.0) * (
        after - values
    )


def on_device(
    spectrum, courant_x, courant_y, growth, quartet, coupler, atmosphere, ocean_state, sea_mask
):
    cell_tiles = lax.axis_size("cells")
    lev_parts = lax.axis_size("lev")
    blocks = cell_tiles * lev_parts
    comps_own, rows_all, row_width = spectrum.shape
    total_comps = comps_own * blocks
    cell_rows = rows_all // blocks
    level_count = coupler.shape[0] // 2
    row_start = lax.axis_index("lev") * cell_rows
    shift_x = courant_x[:, None, None]
    shift_y = courant_y[:, None, None]
    sea_rows = (
        lax.dynamic_slice_in_dim(sea_mask, row_start, cell_rows, 0)
        .astype(jnp.float32)
        .reshape(1, cell_rows * row_width)
    )
    growth_column = growth[:, None]
    forcing_sign = jnp.array([-0.3, 0.3], jnp.float32)[:, None, None, None]
    state = jnp.stack([atmosphere, ocean_state])
    energy = spectrum
    for counter in range(NSTEP):
        surface = from_root(state[:, 0], "lev", 0)
        surface_wind = surface[0] - surface[1]
        wind_rows = lax.dynamic_slice_in_dim(
            surface_wind * surface_wind, row_start, cell_rows, 0
        ).reshape(1, cell_rows * row_width)
        padded = extended_2(energy, (("sect", 2),), 1, True)
        values = padded[:, :, 1:-1].astype(jnp.float32)
        west_side = padded[:, :, :-2].astype(jnp.float32)
        east_side = padded[:, :, 2:].astype(jnp.float32)
        moved = values - upwind(values, shift_x, west_side, east_side)
        moved = moved - upwind(
            values, shift_y, jnp.roll(values, 1, axis=1), jnp.roll(values, -1, axis=1)
        )
        advected = moved.astype(jnp.bfloat16)
        pieces = advected.reshape(1, comps_own, blocks, cell_rows, row_width)
        on_cells = lax.all_to_all(pieces, ("cells", "lev"), split_axis=2, concat_axis=0, tiled=True)
        on_cells = on_cells.reshape(total_comps, cell_rows * row_width)
        cell_values = on_cells.astype(jnp.float32)
        paired = jnp.dot(quartet, on_cells, preferred_element_type=jnp.float32)
        squared = (cell_values * cell_values).astype(jnp.bfloat16)
        quad_square = jnp.dot(quartet, squared, preferred_element_type=jnp.float32)
        fresh = (
            cell_values
            + 0.3 * (cell_values * paired - quad_square)
            + 0.1 * growth_column * wind_rows
        ) / (1.0 + 0.1 * cell_values * cell_values)
        fresh = (fresh * sea_rows).astype(jnp.bfloat16)
        profile = jnp.dot(coupler, fresh, preferred_element_type=jnp.float32).reshape(
            2, level_count, cell_rows, row_width
        )
        forcing = lax.all_to_all(profile, "lev", split_axis=1, concat_axis=2, tiled=True)
        returned = fresh.reshape(blocks, comps_own, 1, cell_rows, row_width)
        returned = lax.all_to_all(
            returned, ("cells", "lev"), split_axis=0, concat_axis=2, tiled=True
        )
        energy = returned.reshape(comps_own, rows_all, row_width)
        extended = extended_2(state, (("lev", 1), ("cells", 2), ("sect", 3)), 1, False)
        middle = extended[:, 1:-1, 1:-1, 1:-1]
        lateral = (
            extended[:, 1:-1, 2:, 1:-1]
            + extended[:, 1:-1, :-2, 1:-1]
            + extended[:, 1:-1, 1:-1, 2:]
            + extended[:, 1:-1, 1:-1, :-2]
            - 4.0 * middle
        )
        upright = extended[:, 2:, 1:-1, 1:-1] + extended[:, :-2, 1:-1, 1:-1] - 2.0 * middle
        state = middle + 0.1 * lateral + 0.1 * upright + forcing_sign * forcing
    return (energy, state[0], state[1])


def column_of(row):
    n = row.shape[1]
    down = lax.broadcasted_iota(jnp.int32, (n, n), 0)
    across = lax.broadcasted_iota(jnp.int32, (n, n), 1)
    return jnp.sum(jnp.where(down == across, row, 0.0), axis=1, keepdims=True)


def swap_groups(vectors, seg):
    count = len(vectors)
    width = vectors[0].shape[1]
    group = lax.broadcasted_iota(jnp.int32, vectors[0].shape, 1) // seg
    dist = count // 2
    vectors = list(vectors)
    while dist:
        even = (group // dist) % 2 == 0
        for i in range(count):
            if (i // dist) % 2 == 0:
                x, y = vectors[i], vectors[i + dist]
                if 2 * dist * seg == width:
                    moved = pltpu.roll(jnp.where(even, y, x), dist * seg, 1)
                    vectors[i], vectors[i + dist] = jnp.where(even, x, moved), jnp.where(even, moved, y)
                else:
                    vectors[i] = jnp.where(even, x, pltpu.roll(y, dist * seg, 1))
                    vectors[i + dist] = jnp.where(even, pltpu.roll(x, width - dist * seg, 1), y)
        dist //= 2
    return vectors


def fused_kernel(
    cell_tiles, lev_parts, sect_tiles,
    spec_hbm, cx_hbm, cy_hbm, growth_hbm, quartet_hbm, coupler_hbm, atm_hbm, oce_hbm, sea_hbm,
    ret, fin, early,
    spec_v, c_v, growth_v, quartet_v, coupler_v, col_in, sea_v,
    flat, rows_v, send_f, cell_f, cell_s, c_all, cxb, cyb, grow_b,
    side_send, side_recv, edge_send, edge_recv, e1, e2,
    swap_send, st_in, sea_send, sea_in, outer, inner, stage_v, total_v, st0, st1, st2, st_edge_send, st_edge_recv, st_back,
    in_sem, f_send, f_recv, c_send, c_recv,
    side_ss, side_rs, edge_ss, edge_rs, swap_ss, swap_rs, sea_ss, sea_rs, back_ss, back_rs, ste_ss, ste_rs,
    ret_ss, ret_rs,
):
    blocks = cell_tiles * lev_parts
    comps, rows, width = spec_v.shape
    lines = rows // blocks
    lown = col_in.shape[1]
    tile_rows = col_in.shape[2]
    levels = lown * lev_parts
    cells = lines * width
    seg = width // blocks
    mid = width // 2
    mine_c = lax.axis_index("cells")
    mine_l = lax.axis_index("lev")
    mine_x = lax.axis_index("sect")
    me = mine_c * lev_parts + mine_l
    turned = lax.rem(mine_x, 2) == 1
    side = lax.div(mine_c, cell_tiles // 2)

    def tile_of(b):
        return jnp.where(turned, blocks - 1 - b, b)

    def mirrored(b):
        return jnp.where(side == 1, blocks - 1 - b, b)

    def block_id(b):
        return {"cells": lax.div(b, lev_parts), "lev": lax.rem(b, lev_parts)}

    spot = tile_of(me)
    inside = mirrored(me)
    west = {"sect": lax.rem(mine_x + sect_tiles - 1, sect_tiles)}
    east = {"sect": lax.rem(mine_x + 1, sect_tiles)}
    near_west = {
        **block_id(jnp.where(spot == 0, me, tile_of(spot - 1))),
        "sect": jnp.where(spot == 0, west["sect"], mine_x),
    }
    near_east = {
        **block_id(jnp.where(spot == blocks - 1, me, tile_of(spot + 1))),
        "sect": jnp.where(spot == blocks - 1, east["sect"], mine_x),
    }
    half = blocks // 2
    odd = lax.rem(inside, 2)
    across = [mirrored(blocks - 1 - i + (1 - 2 * (i % 2)) * -odd) for i in range(half)]
    mate = (1 - lax.div(inside, lev_parts)) * lev_parts
    mates = [mirrored(mate + k) for k in range(lev_parts)]
    order = across + mates + [mirrored(inside + 1 - 2 * odd)]

    def part(b):
        return pl.ds(pl.multiple_of(b * comps, 16), comps)

    def remote(src, dst, ss, rs, where):
        return pltpu.make_async_remote_copy(
            src_ref=src, dst_ref=dst, send_sem=ss, recv_sem=rs,
            device_id=where, device_id_type=pl.DeviceIdType.MESH,
        )

    loads = [
        pltpu.make_async_copy(a, b, in_sem.at[i])
        for i, (a, b) in enumerate([
            (spec_hbm, spec_v), (cx_hbm, c_v.at[0]), (cy_hbm, c_v.at[1]),
            (atm_hbm, col_in.at[0]), (oce_hbm, col_in.at[1]), (sea_hbm, sea_v),
            (growth_hbm, growth_v), (coupler_hbm, coupler_v), (quartet_hbm, quartet_v),
        ])
    ]

    def whole(ref, sem):
        return remote(ref, ref, sem, sem, {"lev": 1 - mine_l})
    for load in loads:
        load.start()

    barrier = pltpu.get_barrier_semaphore()
    for d in range(1, blocks):
        pl.semaphore_signal(barrier, inc=1, device_id=block_id(lax.rem(me + d, blocks)),
                            device_id_type=pl.DeviceIdType.MESH)
    for side_id in (west, east, near_west, near_east):
        pl.semaphore_signal(barrier, inc=1, device_id=side_id,
                            device_id_type=pl.DeviceIdType.MESH)

    my_levels = pl.ds(pl.multiple_of(mine_l * lown, 16), lown)

    def state_in(b):
        return remote(swap_send.at[tile_of(b)], st_in.at[mine_c, my_levels, :], swap_ss.at[0],
                      swap_rs.at[0], block_id(b))

    def sea_over(c):
        return remote(sea_send.at[tile_of(c * lev_parts + mine_l)], sea_in.at[mine_c], sea_ss.at[0],
                      sea_rs.at[0], {"cells": c})

    loads[3].wait()
    loads[4].wait()
    loads[5].wait()
    groups = [col_in[f, :, r, :] for f in range(2) for r in range(tile_rows)]
    for t, line in enumerate(swap_groups(groups, seg)):
        swap_send[t] = line.astype(BF16)
    groups = [jnp.broadcast_to(sea_v[r:r + 1, :].astype(F32), (8, width)) for r in range(tile_rows)]
    for t, line in enumerate(swap_groups(groups + [jnp.zeros((8, width), F32)] * tile_rows, seg)):
        sea_send[t] = line[0:1]
    st_in[mine_c, my_levels, :] = swap_send[spot]
    sea_in[mine_c] = sea_send[spot]

    pl.semaphore_wait(barrier, blocks + 3)
    wave = [mirrored(i) for i in sorted(range(blocks), key=lambda i: (abs(2 * i + 1 - blocks), -i))]

    for b in wave:
        @pl.when(b != me)
        def _():
            state_in(b).start()
    for dc in range(1, cell_tiles):
        sea_over(lax.rem(mine_c + dc, cell_tiles)).start()
    loads[1].wait()
    loads[2].wait()
    for b in order:
        remote(c_v, c_all.at[me], c_send.at[0], c_recv.at[0], block_id(b)).start()

    lane = lax.broadcasted_iota(jnp.int32, (comps, width), 1)
    loads[0].wait()
    flat[...] = spec_v[...].astype(F32).reshape(comps * rows, width)
    for r in range(rows):
        rows_v[r] = flat[pl.ds(r, comps, stride=rows), :]

    def halves(c):
        return jnp.maximum(c, 0.0), jnp.maximum(-c, 0.0)

    cxb[part(me), :] = jnp.broadcast_to(column_of(c_v[0]), (comps, width))
    cyb[part(me), :] = jnp.broadcast_to(column_of(c_v[1]), (comps, width))

    def send_line(b, h):
        t = tile_of(b)
        cut = slice(h * width, (h + 1) * width)

        @pl.when(b != me)
        def _():
            remote(send_f.at[t, h], cell_f.at[part(me), cut], f_send.at[0], f_recv.at[me],
                   block_id(b)).start()

        @pl.when(b == me)
        def _():
            cell_f[part(me), cut] = send_f[spot, h]

    chunk = comps
    small = lax.broadcasted_iota(jnp.int32, (chunk, width), 1)

    lead = [jnp.where(inside < lev_parts, wave[i], wave[j]) for i, j in ((1, 0), (3, 1), (0, 2), (2, 3))]
    for h in range(lines):
        for k in range(0, comps, chunk):
            own = pl.ds(pl.multiple_of(me * comps + k, 16), chunk)
            cx = cxb[own, :]
            cy = cyb[own, :]
            px, mx = halves(cx)
            py, my = halves(cy)
            keep = 1.0 - jnp.abs(cx) - jnp.abs(cy)
            groups = []
            for g in range(blocks):
                row = h * blocks + g
                v = rows_v[row, k:k + chunk]
                to_west = jnp.where(small == 0, 0.0, pltpu.roll(v, 1, 1))
                to_east = jnp.where(small == width - 1, 0.0, pltpu.roll(v, width - 1, 1))
                groups.append(
                    v * keep + px * to_west + mx * to_east
                    + py * rows_v[(row + rows - 1) % rows, k:k + chunk] + my * rows_v[(row + 1) % rows, k:k + chunk]
                )
            for t, line in enumerate(swap_groups(groups, seg)):
                if 0 < t < blocks - 1:
                    send_f[t, h, k:k + chunk] = line.astype(BF16)
                else:
                    outer[min(t, 1), h, k:k + chunk] = line
        for b in lead[:2]:
            send_line(b, h)
    for b in lead[2:]:
        for h in range(lines):
            send_line(b, h)

    def release(now, position):
        ready = [p for p, when in HELD.get(position, {}).items() if when == now]
        if now == "start":
            late = [p for p, when in HELD.get(position, {}).items() if when != now]
            ready = [p for p in range(half) if p not in late]
        if len(ready) == half:
            for h in range(lines):
                send_line(wave[position], h)
        elif ready:
            hit = inside == ready[0]
            for p in ready[1:]:
                hit = hit | (inside == p)

            @pl.when(hit)
            def _():
                for h in range(lines):
                    send_line(wave[position], h)

    release("start", 4)
    for h in range(lines):
        send_line(wave[5], h)

    edge = jnp.zeros((comps, width), F32)
    for r in range(rows):
        v = rows_v[r]
        slot = (r % blocks) * seg + r // blocks
        edge = jnp.where(lane == slot, pltpu.roll(v, slot, 1), edge)
        edge = jnp.where(lane == slot + lines, pltpu.roll(v, (slot + lines + 1) % width, 1), edge)
    side_send[...] = edge.astype(BF16)
    sides = (west, east) if sect_tiles > 2 else (west,)
    for i, where in enumerate(sides):
        remote(side_send, side_recv.at[i], side_ss.at[0], side_rs.at[0], where).start()
    whole(side_recv.at[pl.ds(0, len(sides))], side_rs.at[0]).wait_recv()
    for k in range(0, comps, chunk):
        cx = cxb[pl.ds(pl.multiple_of(me * comps + k, 16), chunk), :]
        px, mx = halves(cx)
        from_east = side_recv[0, k:k + chunk].astype(F32)
        from_west = side_recv[len(sides) - 1, k:k + chunk].astype(F32)
        for h in range(lines):
            west_part = jnp.where(small % seg == 0, pltpu.roll(from_west, (width - lines - h) % width, 1), 0.0)
            east_part = jnp.where(small % seg == seg - 1, pltpu.roll(from_east, seg - 1 - h, 1), 0.0)
            send_f[0, h, k:k + chunk] = (outer[0, h, k:k + chunk] + px * west_part).astype(BF16)
            send_f[blocks - 1, h, k:k + chunk] = (outer[1, h, k:k + chunk] + mx * east_part).astype(BF16)
    release("start", 6)
    for h in range(lines):
        send_line(wave[7], h)

    level_id = lax.broadcasted_iota(jnp.int32, (levels, width), 0)
    level_lane = lax.broadcasted_iota(jnp.int32, (levels, width), 1)
    place = level_lane % seg
    folds = seg // (2 * lines)
    depth = levels // folds
    fold_place = place[:depth]

    def fold_slots():
        for f in range(2):
            for r in range(lines):
                for q in range(folds):
                    yield f, r, slice(q * depth, (q + 1) * depth), (q * 2 + f) * lines + r

    def send_state(state, step):
        west_pack = jnp.zeros((depth, width), F32)
        east_pack = jnp.zeros((depth, width), F32)
        for f, r, cut, slot in fold_slots():
            v = state[f, r, cut]
            west_pack = jnp.where(fold_place == slot, pltpu.roll(v, slot, 1), west_pack)
            east_pack = jnp.where(fold_place == slot, pltpu.roll(v, (slot + 1 - seg) % width, 1), east_pack)
        st_edge_send[step, 0] = west_pack
        st_edge_send[step, 1] = east_pack
        for i, where in enumerate((near_west, near_east)):
            remote(st_edge_send.at[step, i], st_edge_recv.at[step, i], ste_ss.at[0], ste_rs.at[step], where).start()

    def update(state, new, step, profile):
        rim_west = (mine_x == 0) & (spot == 0)
        rim_east = (mine_x == sect_tiles - 1) & (spot == blocks - 1)
        west_pack = jnp.where(rim_west, 0.0, st_edge_recv[step, 1])
        east_pack = jnp.where(rim_east, 0.0, st_edge_recv[step, 0])
        sides = {}
        for f, r, cut, slot in fold_slots():
            sides.setdefault((f, r), []).append((
                pltpu.roll(west_pack, (width - slot) % width, 1),
                pltpu.roll(east_pack, (width + seg - 1 - slot) % width, 1),
            ))
        for f in range(2):
            factor = -0.3 if f == 0 else 0.3
            for r in range(lines):
                v = state[f, r]
                w = jnp.where(place == 0, jnp.concatenate([x for x, _ in sides[f, r]]), pltpu.roll(v, 1, 1))
                e = jnp.where(place == seg - 1, jnp.concatenate([x for _, x in sides[f, r]]),
                              pltpu.roll(v, width - 1, 1))
                n = 0.0 if r == 0 else state[f, r - 1]
                s = 0.0 if r == lines - 1 else state[f, r + 1]
                n = pltpu.roll(jnp.where(level_lane >= width - seg, n, v), seg, 1)
                s = pltpu.roll(jnp.where(level_lane < seg, s, v), width - seg, 1)
                below = jnp.where(level_id == 0, 0.0, pltpu.roll(v, 1, 0))
                above = jnp.where(level_id == levels - 1, 0.0, pltpu.roll(v, levels - 1, 0))
                g = profile[f * levels:(f + 1) * levels, r * width:(r + 1) * width]
                new[f, r] = (v + 0.1 * (n + s + w + e - 4.0 * v)
                             + 0.1 * (above + below - 2.0 * v) + factor * g)

    loads[6].wait()
    for t in range(growth_v.shape[0] // LANES):
        column = column_of(growth_v[t * LANES:(t + 1) * LANES].reshape(1, LANES))
        grow_b[t * LANES:(t + 1) * LANES, :] = jnp.broadcast_to(0.1 * column, (LANES, width))

    def wind(state):
        out = []
        for r in range(lines):
            diff = state[0, r, 0:1, :] - state[1, r, 0:1, :]
            out.append(diff * diff)
        return out

    def fresh_part(rows_of, wind_rows, target, pair, quad):
        outs = []
        for r in range(lines):
            cut = slice(r * width, (r + 1) * width)
            f = cell_f[rows_of, cut].astype(F32)
            top = f + 0.3 * (f * pair[:, cut] - quad[:, cut]) + grow_b[rows_of, :] * wind_rows[r]
            out = (sea[r] * (top / (1.0 + 0.1 * (f * f)))).astype(BF16)
            target[rows_of, cut] = out
            outs.append(out)
        return outs

    others = pl.ds(0, blocks - 1)
    whole(c_all.at[others], c_recv.at[0]).wait_recv()
    for b in order:
        cxb[part(b), :] = jnp.broadcast_to(column_of(c_all[b, 0]), (comps, width))
        cyb[part(b), :] = jnp.broadcast_to(column_of(c_all[b, 1]), (comps, width))
    whole(swap_send.at[others], swap_rs.at[0]).wait_recv()
    whole(sea_send.at[pl.ds(0, cell_tiles - 1)], sea_rs.at[0]).wait_recv()

    wide_lane = lax.broadcasted_iota(jnp.int32, (8, width), 1)
    sea = []
    for h in range(lines):
        low = st_in[2 * h].astype(F32)
        high = st_in[2 * h + 1].astype(F32)
        st0[0, h] = jnp.where(level_lane < mid, low, pltpu.roll(high, mid, 1))
        st0[1, h] = jnp.where(level_lane < mid, pltpu.roll(low, mid, 1), high)
        low = jnp.broadcast_to(sea_in[2 * h], (8, width))
        high = jnp.broadcast_to(sea_in[2 * h + 1], (8, width))
        sea.append(jnp.where(wide_lane < mid, low, pltpu.roll(high, mid, 1))[0:1])
    send_state(st0, 0)

    loads[7].wait()
    loads[8].wait()

    near = half * comps
    span = stage_v.shape[2]
    spare = span - near
    for i in range(2):
        for x in range(2):
            stage_v[i, x, (1 - i) * near:(1 - i) * near + spare] = jnp.zeros((spare, cells), BF16)

    def stage(b):
        f = cell_f[part(b), :]
        wide = f.astype(F32)
        which = lax.div(b, half)
        rows_of = pl.ds(pl.multiple_of(which * spare + (b - which * half) * comps, 16), comps)
        stage_v[which, 0, rows_of, :] = f
        stage_v[which, 1, rows_of, :] = (wide * wide).astype(BF16)

    def products(rows_of, which):
        weights = quartet_v[rows_of, pl.ds(pl.multiple_of(which * (quartet_v.shape[1] - span), LANES), span)]
        return [jnp.dot(weights, stage_v[which, i], preferred_element_type=F32) for i in range(2)]

    def arrived(b):
        whole(cell_f.at[part(b), :], f_recv.at[b]).wait_recv()
        stage(b)

    stage(me)
    for b in order[half:][::-1]:
        arrived(b)
    for m in range(blocks):
        for i, x in enumerate(products(part(m), side)):
            total_v[i, part(m), :] = x
    for b in order[:half][::-1]:
        arrived(b)
    release("far", 6)

    wind_rows = wind(st0)
    first = jnp.zeros((comps, width), F32)
    last = jnp.zeros((comps, width), F32)
    for b in range(blocks):
        pair, quad = [total_v[i, part(b), :] + x
                      for i, x in enumerate(products(part(b), 1 - side))]
        outs = fresh_part(part(b), wind_rows, e1, pair, quad)
        for r in range(lines):
            slot = b * lines + r
            v = outs[r].astype(F32)
            first = jnp.where(lane % seg == slot, pltpu.roll(v, slot, 1), first)
            last = jnp.where(lane % seg == slot, pltpu.roll(v, (slot + 1 - seg) % width, 1), last)
    edge_send[0] = first.astype(BF16)
    edge_send[1] = last.astype(BF16)
    for i, where in enumerate((near_west, near_east)):
        remote(edge_send.at[i], edge_recv.at[i], edge_ss.at[0], edge_rs.at[0], where).start()
    release("edges", 6)

    west_rim = lane % seg == 0
    east_rim = lane % seg == seg - 1
    for b in range(blocks):
        cx = cxb[part(b), :]
        cy = cyb[part(b), :]
        px, mx = halves(cx)
        py, my = halves(cy)
        keep = 1.0 - jnp.abs(cx) - jnp.abs(cy)
        field = [e1[part(b), r * width:(r + 1) * width].astype(F32) for r in range(lines)]
        for r in range(lines):
            v = field[r]
            north = pltpu.roll(jnp.where(lane >= width - seg, field[r - 1], v), seg, 1)
            south = pltpu.roll(jnp.where(lane < seg, field[(r + 1) % lines], v), width - seg, 1)
            to_west = jnp.where(west_rim, 0.0, pltpu.roll(v, 1, 1))
            to_east = jnp.where(east_rim, 0.0, pltpu.roll(v, width - 1, 1))
            inner[part(b), r * width:(r + 1) * width] = (
                v * keep + px * to_west + mx * to_east + py * north + my * south
            )

    whole(st_edge_recv.at[0], ste_rs.at[0]).wait_recv()
    update(st0, st1, 0, jnp.dot(coupler_v[...], e1[...], preferred_element_type=F32))
    send_state(st1, 1)
    wind_rows = wind(st1)

    whole(edge_recv, edge_rs.at[0]).wait_recv()
    from_east = edge_recv[0].astype(F32)
    from_west = edge_recv[1].astype(F32)
    for b in range(blocks):
        px, mx = halves(cxb[part(b), :])
        for r in range(lines):
            slot = b * lines + r
            cut = slice(r * width, (r + 1) * width)
            beside = jnp.where(
                west_rim, px * pltpu.roll(from_west, (width - slot) % width, 1),
                mx * pltpu.roll(from_east, (width + seg - 1 - slot) % width, 1),
            )
            out = (inner[part(b), cut] + jnp.where(west_rim | east_rim, beside, 0.0)).astype(BF16)
            cell_f[part(b), cut] = out
            wide = out.astype(F32)
            cell_s[part(b), cut] = (wide * wide).astype(BF16)

    cuts = [(0, early.shape[0]), (early.shape[0], comps - early.shape[0])]

    def send_back(b, q):
        start, size = cuts[q]
        remote(e2.at[pl.ds(pl.multiple_of(b * comps + start, 16), size), :], ret.at[spot, pl.ds(start, size), :],
               ret_ss.at[0], ret_rs.at[q], block_id(b)).start()

    for b in order + [me]:
        weights = quartet_v[part(b), :]
        pair = jnp.dot(weights, cell_f[...], preferred_element_type=F32)
        quad = jnp.dot(weights, cell_s[...], preferred_element_type=F32)
        outs = fresh_part(part(b), wind_rows, e2, pair, quad)
        if b is not me:
            send_back(b, 0)
    for r, out in enumerate(outs):
        ret[spot, :, r * width:(r + 1) * width] = out
    for b in order:
        send_back(b, 1)

    whole(st_edge_recv.at[1], ste_rs.at[1]).wait_recv()
    update(st1, st2, 1, jnp.dot(coupler_v[...], e2[...], preferred_element_type=F32))
    for h in range(lines):
        atm = st2[0, h]
        oce = st2[1, h]
        st_back[2 * h] = jnp.where(level_lane < mid, atm, pltpu.roll(oce, mid, 1)).astype(BF16)
        st_back[2 * h + 1] = jnp.where(level_lane < mid, pltpu.roll(atm, mid, 1), oce).astype(BF16)

    for b in order:
        c = lax.div(b, lev_parts)
        core = lax.rem(b, lev_parts)
        remote(st_back.at[c, pl.ds(pl.multiple_of(core * lown, 16), lown), :], fin.at[spot], back_ss.at[0],
               back_rs.at[0], block_id(b)).start()
    fin[spot] = st_back[mine_c, my_levels, :]
    for q, (start, size) in enumerate(cuts):
        whole(ret.at[others, pl.ds(start, size), :], ret_rs.at[q]).wait_recv()
        if q == 0:
            to_rows(ret, early, flat, start)
    whole(fin.at[others], back_rs.at[0]).wait_recv()

    whole(send_f.at[others], f_send.at[0]).wait_send()
    whole(c_all.at[others], c_send.at[0]).wait_send()
    whole(swap_send.at[others], swap_ss.at[0]).wait_send()
    whole(sea_send.at[pl.ds(0, cell_tiles - 1)], sea_ss.at[0]).wait_send()
    for _ in sides:
        whole(side_send, side_ss.at[0]).wait_send()
    whole(edge_send, edge_ss.at[0]).wait_send()
    whole(st_edge_send, ste_ss.at[0]).wait_send()
    whole(ret.at[others], ret_ss.at[0]).wait_send()
    whole(fin.at[others], back_ss.at[0]).wait_send()


def to_rows(ret, target, flat, start):
    blocks = ret.shape[0]
    size, rows, width = target.shape
    lines = rows // blocks
    for h in range(lines):
        groups = swap_groups([
            ret[t, start:start + size, h * width:(h + 1) * width].astype(F32) for t in range(blocks)
        ], width // blocks)
        for g, line in enumerate(groups):
            flat[pl.ds(h * blocks + g, size, stride=rows), :] = line
    target[...] = flat[pl.ds(0, size * rows), :].reshape(size, rows, width).astype(BF16)


def unpack_kernel(ret, fin, early, spec_out, atm_out, oce_out, atm_v, oce_v, flat, late, out_sem):
    blocks = ret.shape[0]
    tile_rows = atm_v.shape[1]
    start = early.shape[0]
    stores = [pltpu.make_async_copy(early, spec_out.at[pl.ds(0, start)], out_sem.at[2])]
    stores[-1].start()
    to_rows(ret, late, flat, start)
    stores.append(pltpu.make_async_copy(late, spec_out.at[pl.ds(start, late.shape[0])], out_sem.at[3]))
    stores[-1].start()
    groups = swap_groups([fin[t].astype(F32) for t in range(blocks)], fin.shape[2] // blocks)
    for f, (target, out) in enumerate(((atm_v, atm_out), (oce_v, oce_out))):
        for r in range(tile_rows):
            target[:, r, :] = groups[f * tile_rows + r]
        stores.append(pltpu.make_async_copy(target, out, out_sem.at[f]))
        stores[-1].start()
    for store in stores:
        store.wait()


def fused(
    spectrum, courant_x, courant_y, growth, quartet, coupler, atmosphere, ocean_state, sea_mask
):
    cell_tiles = lax.axis_size("cells")
    lev_parts = lax.axis_size("lev")
    sect_tiles = lax.axis_size("sect")
    blocks = cell_tiles * lev_parts
    comps, rows, width = spectrum.shape
    total = comps * blocks
    lines = rows // blocks
    lown, tile_rows, _ = atmosphere.shape
    levels = lown * lev_parts
    cells = lines * width
    first = comps // 16 * 2 // 3 * 16
    depth = levels // (width // blocks // (2 * lines))
    v = pltpu.VMEM
    dma = pltpu.SemaphoreType.DMA
    scratch = [
        v((comps, rows, width), BF16), v((2, 1, comps), F32),
        v((total,), F32), v((total, total), BF16), v(coupler.shape, BF16),
        v((2, lown, tile_rows, width), F32), v(sea_mask.shape, jnp.int32),
        v((comps * rows, width), F32), v((rows, comps, width), F32),
        v((blocks, lines, comps, width), BF16), v((total, cells), BF16), v((total, cells), BF16),
        v((blocks, 2, 1, comps), F32),
        v((total, width), F32), v((total, width), F32), v((total, width), F32),
        v((comps, width), BF16), v((2, comps, width), BF16), v((2, comps, width), BF16), v((2, comps, width), BF16),
        v((total, cells), BF16), v((total, cells), BF16),
        v((blocks, lown, width), BF16), v((cell_tiles, levels, width), BF16),
        v((blocks, 1, width), F32), v((cell_tiles, 1, width), F32),
        v((2, lines, comps, width), F32), v((total, cells), F32),
        v((2, 2, -(-total // (2 * LANES)) * LANES, cells), BF16), v((2, total, cells), F32),
        v((2, lines, levels, width), F32), v((2, lines, levels, width), F32),
        v((2, lines, levels, width), F32),
        v((NSTEP, 2, depth, width), F32), v((NSTEP, 2, depth, width), F32),
        v((cell_tiles, levels, width), BF16),
        dma((9,)), dma((1,)), dma((blocks,)), dma((1,)), dma((1,)),
        dma((1,)), dma((1,)), dma((1,)), dma((1,)),
        dma((1,)), dma((1,)), dma((1,)), dma((1,)),
        dma((1,)), dma((1,)),
        dma((1,)), dma((NSTEP,)),
        dma((1,)), dma((2,)),
    ]
    anywhere = pl.BlockSpec(memory_space=pltpu.HBM)
    here = pl.BlockSpec(memory_space=pltpu.VMEM)
    column = jax.ShapeDtypeStruct(atmosphere.shape, F32)
    packed = pl.pallas_call(
        functools.partial(fused_kernel, cell_tiles, lev_parts, sect_tiles),
        out_shape=(
            v((blocks, comps, cells), BF16), v((blocks, lown, width), BF16), v((first, rows, width), BF16),
        ),
        in_specs=[anywhere] * 9,
        out_specs=(here,) * 3,
        scratch_shapes=scratch,
        compiler_params=pltpu.CompilerParams(
            collective_id=0, has_side_effects=True, vmem_limit_bytes=33554432
        ),
    )(*(
        pltpu.with_memory_space_constraint(x, pltpu.HBM)
        for x in (spectrum, courant_x.reshape(1, comps), courant_y.reshape(1, comps),
                  growth, quartet, coupler, atmosphere, ocean_state, sea_mask)
    ))
    return pl.pallas_call(
        unpack_kernel,
        out_shape=(jax.ShapeDtypeStruct(spectrum.shape, BF16), column, column),
        in_specs=[here] * 3,
        out_specs=(anywhere,) * 3,
        scratch_shapes=[
            v(atmosphere.shape, F32), v(atmosphere.shape, F32),
            v(((comps - first) * rows, width), F32), v((comps - first, rows, width), BF16), dma((4,)),
        ],
        compiler_params=pltpu.CompilerParams(vmem_limit_bytes=33554432),
    )(*packed)


def fits_fused(mesh, spectrum, coupler, atmosphere):
    lev_parts = lax.axis_size("lev")
    cells = lax.axis_size("cells")
    blocks = cells * lev_parts
    comps, rows, width = spectrum.shape
    return (
        lev_parts == 2 and cells == 4 and lax.axis_size("sect") % 2 == 0 and width == LANES
        and comps % 16 == 0 and rows == 2 * blocks and (comps * blocks) % LANES == 0
        and atmosphere.shape[0] % 16 == 0 and 2 * atmosphere.shape[1] == blocks
    )


def solution(mesh):
    in_specs = (
        P(("cells", "lev"), "groups", "sect"),
        P(("cells", "lev")),
        P(("cells", "lev")),
        P(),
        P(),
        P(),
        P("lev", ("groups", "cells"), "sect"),
        P("lev", ("groups", "cells"), "sect"),
        P(("groups", "cells"), "sect"),
    )
    out_specs = (
        P(("cells", "lev"), "groups", "sect"),
        P("lev", ("groups", "cells"), "sect"),
        P("lev", ("groups", "cells"), "sect"),
    )

    def body(*args):
        if fits_fused(mesh, args[0], args[5], args[6]):
            return fused(*args)
        return on_device(*args)

    return jax.shard_map(
        body, mesh=mesh, in_specs=in_specs, out_specs=out_specs, check_vma=False
    )
```

```python
import functools

import jax
import jax.numpy as jnp
from jax import lax
from jax.experimental import pallas as pl
from jax.experimental.pallas import tpu as pltpu
from jax.sharding import PartitionSpec as P

NSTEP = 2
LANES = 128
HELD = {6: {3: "edges", 2: "far"}}
FIRST = (0, 4, 1, 5, 2, 3, 6)
SECOND = (0, 4, 1, 5, 2, 3, 6)
F32 = jnp.float32
BF16 = jnp.bfloat16


def from_root(block, axis, source):
    block = jnp.where(lax.axis_index(axis) == source, block, jnp.zeros_like(block))
    return lax.psum(block, axis)


def extended_2(block, sides, width, periodic):
    for axis, dim in sides:
        count = lax.axis_size(axis)
        forward = [(i, i + 1) for i in range(count - 1)]
        if periodic:
            forward.append((count - 1, 0))
        backward = [(target, source) for source, target in forward]
        low = lax.ppermute(
            lax.slice_in_dim(block, block.shape[dim] - width, None, axis=dim), axis, forward
        )
        high = lax.ppermute(lax.slice_in_dim(block, 0, width, axis=dim), axis, backward)
        block = jnp.concatenate([low, block, high], axis=dim)
    return block


def upwind(values, courant, before, after):
    return jnp.maximum(courant, 0.0) * (values - before) + jnp.minimum(courant, 0.0) * (
        after - values
    )


def on_device(
    spectrum, courant_x, courant_y, growth, quartet, coupler, atmosphere, ocean_state, sea_mask
):
    cell_tiles = lax.axis_size("cells")
    lev_parts = lax.axis_size("lev")
    blocks = cell_tiles * lev_parts
    comps_own, rows_all, row_width = spectrum.shape
    total_comps = comps_own * blocks
    cell_rows = rows_all // blocks
    level_count = coupler.shape[0] // 2
    row_start = lax.axis_index("lev") * cell_rows
    shift_x = courant_x[:, None, None]
    shift_y = courant_y[:, None, None]
    sea_rows = (
        lax.dynamic_slice_in_dim(sea_mask, row_start, cell_rows, 0)
        .astype(jnp.float32)
        .reshape(1, cell_rows * row_width)
    )
    growth_column = growth[:, None]
    forcing_sign = jnp.array([-0.3, 0.3], jnp.float32)[:, None, None, None]
    state = jnp.stack([atmosphere, ocean_state])
    energy = spectrum
    for counter in range(NSTEP):
        surface = from_root(state[:, 0], "lev", 0)
        surface_wind = surface[0] - surface[1]
        wind_rows = lax.dynamic_slice_in_dim(
            surface_wind * surface_wind, row_start, cell_rows, 0
        ).reshape(1, cell_rows * row_width)
        padded = extended_2(energy, (("sect", 2),), 1, True)
        values = padded[:, :, 1:-1].astype(jnp.float32)
        west_side = padded[:, :, :-2].astype(jnp.float32)
        east_side = padded[:, :, 2:].astype(jnp.float32)
        moved = values - upwind(values, shift_x, west_side, east_side)
        moved = moved - upwind(
            values, shift_y, jnp.roll(values, 1, axis=1), jnp.roll(values, -1, axis=1)
        )
        advected = moved.astype(jnp.bfloat16)
        pieces = advected.reshape(1, comps_own, blocks, cell_rows, row_width)
        on_cells = lax.all_to_all(pieces, ("cells", "lev"), split_axis=2, concat_axis=0, tiled=True)
        on_cells = on_cells.reshape(total_comps, cell_rows * row_width)
        cell_values = on_cells.astype(jnp.float32)
        paired = jnp.dot(quartet, on_cells, preferred_element_type=jnp.float32)
        squared = (cell_values * cell_values).astype(jnp.bfloat16)
        quad_square = jnp.dot(quartet, squared, preferred_element_type=jnp.float32)
        fresh = (
            cell_values
            + 0.3 * (cell_values * paired - quad_square)
            + 0.1 * growth_column * wind_rows
        ) / (1.0 + 0.1 * cell_values * cell_values)
        fresh = (fresh * sea_rows).astype(jnp.bfloat16)
        profile = jnp.dot(coupler, fresh, preferred_element_type=jnp.float32).reshape(
            2, level_count, cell_rows, row_width
        )
        forcing = lax.all_to_all(profile, "lev", split_axis=1, concat_axis=2, tiled=True)
        returned = fresh.reshape(blocks, comps_own, 1, cell_rows, row_width)
        returned = lax.all_to_all(
            returned, ("cells", "lev"), split_axis=0, concat_axis=2, tiled=True
        )
        energy = returned.reshape(comps_own, rows_all, row_width)
        extended = extended_2(state, (("lev", 1), ("cells", 2), ("sect", 3)), 1, False)
        middle = extended[:, 1:-1, 1:-1, 1:-1]
        lateral = (
            extended[:, 1:-1, 2:, 1:-1]
            + extended[:, 1:-1, :-2, 1:-1]
            + extended[:, 1:-1, 1:-1, 2:]
            + extended[:, 1:-1, 1:-1, :-2]
            - 4.0 * middle
        )
        upright = extended[:, 2:, 1:-1, 1:-1] + extended[:, :-2, 1:-1, 1:-1] - 2.0 * middle
        state = middle + 0.1 * lateral + 0.1 * upright + forcing_sign * forcing
    return (energy, state[0], state[1])


def column_of(row):
    n = row.shape[1]
    down = lax.broadcasted_iota(jnp.int32, (n, n), 0)
    across = lax.broadcasted_iota(jnp.int32, (n, n), 1)
    return jnp.sum(jnp.where(down == across, row, 0.0), axis=1, keepdims=True)


def swap_groups(vectors, seg):
    count = len(vectors)
    width = vectors[0].shape[1]
    group = lax.broadcasted_iota(jnp.int32, vectors[0].shape, 1) // seg
    dist = count // 2
    vectors = list(vectors)
    while dist:
        even = (group // dist) % 2 == 0
        for i in range(count):
            if (i // dist) % 2 == 0:
                x, y = vectors[i], vectors[i + dist]
                if 2 * dist * seg == width:
                    moved = pltpu.roll(jnp.where(even, y, x), dist * seg, 1)
                    vectors[i], vectors[i + dist] = jnp.where(even, x, moved), jnp.where(even, moved, y)
                else:
                    vectors[i] = jnp.where(even, x, pltpu.roll(y, dist * seg, 1))
                    vectors[i + dist] = jnp.where(even, pltpu.roll(x, width - dist * seg, 1), y)
        dist //= 2
    return vectors


def fused_kernel(
    cell_tiles, lev_parts, sect_tiles,
    spec_hbm, cx_hbm, cy_hbm, growth_hbm, quartet_hbm, coupler_hbm, atm_hbm, oce_hbm, sea_hbm,
    ret, early, atm_v, oce_v,
    spec_v, fin, c_v, growth_v, quartet_v, coupler_v, col_in, sea_v,
    flat, rows_v, send_f, cell_f, cell_s, c_all, cxb, cyb, grow_b,
    side_send, side_recv, edge_send, edge_recv, e1, e2,
    swap_send, st_in, sea_send, sea_in, outer, inner, stage_v, total_v, st0, st1, st2, st_edge_send, st_edge_recv, st_back,
    in_sem, f_send, f_recv, c_send, c_recv,
    side_ss, side_rs, edge_ss, edge_rs, swap_ss, swap_rs, sea_ss, sea_rs, back_ss, back_rs, ste_ss, ste_rs,
    ret_ss, ret_rs,
):
    blocks = cell_tiles * lev_parts
    comps, rows, width = spec_v.shape
    lines = rows // blocks
    lown = col_in.shape[1]
    tile_rows = col_in.shape[2]
    levels = lown * lev_parts
    cells = lines * width
    seg = width // blocks
    mid = width // 2
    mine_c = lax.axis_index("cells")
    mine_l = lax.axis_index("lev")
    mine_x = lax.axis_index("sect")
    me = mine_c * lev_parts + mine_l
    turned = lax.rem(mine_x, 2) == 1
    side = lax.div(mine_c, cell_tiles // 2)

    def tile_of(b):
        return jnp.where(turned, blocks - 1 - b, b)

    def mirrored(b):
        return jnp.where(side == 1, blocks - 1 - b, b)

    def block_id(b):
        return {"cells": lax.div(b, lev_parts), "lev": lax.rem(b, lev_parts)}

    spot = tile_of(me)
    inside = mirrored(me)
    west = {"sect": lax.rem(mine_x + sect_tiles - 1, sect_tiles)}
    east = {"sect": lax.rem(mine_x + 1, sect_tiles)}
    near_west = {
        **block_id(jnp.where(spot == 0, me, tile_of(spot - 1))),
        "sect": jnp.where(spot == 0, west["sect"], mine_x),
    }
    near_east = {
        **block_id(jnp.where(spot == blocks - 1, me, tile_of(spot + 1))),
        "sect": jnp.where(spot == blocks - 1, east["sect"], mine_x),
    }
    half = blocks // 2
    odd = lax.rem(inside, 2)
    across = [mirrored(blocks - 1 - i + (1 - 2 * (i % 2)) * -odd) for i in range(half)]
    mate = (1 - lax.div(inside, lev_parts)) * lev_parts
    mates = [mirrored(mate + k) for k in range(lev_parts)]
    order = across + mates + [mirrored(inside + 1 - 2 * odd)]

    def part(b):
        return pl.ds(pl.multiple_of(b * comps, 16), comps)

    def remote(src, dst, ss, rs, where):
        return pltpu.make_async_remote_copy(
            src_ref=src, dst_ref=dst, send_sem=ss, recv_sem=rs,
            device_id=where, device_id_type=pl.DeviceIdType.MESH,
        )

    loads = [
        pltpu.make_async_copy(a, b, in_sem.at[i])
        for i, (a, b) in enumerate([
            (spec_hbm, spec_v), (cx_hbm, c_v.at[0]), (cy_hbm, c_v.at[1]),
            (atm_hbm, col_in.at[0]), (oce_hbm, col_in.at[1]), (sea_hbm, sea_v),
            (growth_hbm, growth_v), (coupler_hbm, coupler_v), (quartet_hbm, quartet_v),
        ])
    ]

    def whole(ref, sem):
        return remote(ref, ref, sem, sem, {"lev": 1 - mine_l})
    for load in loads:
        load.start()

    barrier = pltpu.get_barrier_semaphore()
    for d in range(1, blocks):
        pl.semaphore_signal(barrier, inc=1, device_id=block_id(lax.rem(me + d, blocks)),
                            device_id_type=pl.DeviceIdType.MESH)
    for side_id in (west, east, near_west, near_east):
        pl.semaphore_signal(barrier, inc=1, device_id=side_id,
                            device_id_type=pl.DeviceIdType.MESH)

    my_levels = pl.ds(pl.multiple_of(mine_l * lown, 16), lown)

    def state_in(b):
        return remote(swap_send.at[tile_of(b)], st_in.at[mine_c, my_levels, :], swap_ss.at[0],
                      swap_rs.at[0], block_id(b))

    def sea_over(c):
        return remote(sea_send.at[tile_of(c * lev_parts + mine_l)], sea_in.at[mine_c], sea_ss.at[0],
                      sea_rs.at[0], {"cells": c})

    loads[3].wait()
    loads[4].wait()
    loads[5].wait()
    groups = [col_in[f, :, r, :] for f in range(2) for r in range(tile_rows)]
    for t, line in enumerate(swap_groups(groups, seg)):
        swap_send[t] = line.astype(BF16)
    groups = [jnp.broadcast_to(sea_v[r:r + 1, :].astype(F32), (8, width)) for r in range(tile_rows)]
    for t, line in enumerate(swap_groups(groups + [jnp.zeros((8, width), F32)] * tile_rows, seg)):
        sea_send[t] = line[0:1]
    st_in[mine_c, my_levels, :] = swap_send[spot]
    sea_in[mine_c] = sea_send[spot]

    pl.semaphore_wait(barrier, blocks + 3)
    wave = [mirrored(i) for i in sorted(range(blocks), key=lambda i: (abs(2 * i + 1 - blocks), -i))]

    for b in wave:
        @pl.when(b != me)
        def _():
            state_in(b).start()
    for dc in range(1, cell_tiles):
        sea_over(lax.rem(mine_c + dc, cell_tiles)).start()
    loads[1].wait()
    loads[2].wait()
    for b in order:
        remote(c_v, c_all.at[me], c_send.at[0], c_recv.at[0], block_id(b)).start()

    lane = lax.broadcasted_iota(jnp.int32, (comps, width), 1)
    loads[0].wait()
    flat[...] = spec_v[...].astype(F32).reshape(comps * rows, width)
    for r in range(rows):
        rows_v[r] = flat[pl.ds(r, comps, stride=rows), :]

    def halves(c):
        return jnp.maximum(c, 0.0), jnp.maximum(-c, 0.0)

    cxb[part(me), :] = jnp.broadcast_to(column_of(c_v[0]), (comps, width))
    cyb[part(me), :] = jnp.broadcast_to(column_of(c_v[1]), (comps, width))

    def send_line(b, h):
        t = tile_of(b)
        cut = slice(h * width, (h + 1) * width)

        @pl.when(b != me)
        def _():
            remote(send_f.at[t, h], cell_f.at[part(me), cut], f_send.at[0], f_recv.at[me],
                   block_id(b)).start()

        @pl.when(b == me)
        def _():
            cell_f[part(me), cut] = send_f[spot, h]

    chunk = comps
    small = lax.broadcasted_iota(jnp.int32, (chunk, width), 1)

    lead = [jnp.where(inside < lev_parts, wave[i], wave[j]) for i, j in ((1, 0), (3, 1), (0, 2), (2, 3))]
    for h in range(lines):
        for k in range(0, comps, chunk):
            own = pl.ds(pl.multiple_of(me * comps + k, 16), chunk)
            cx = cxb[own, :]
            cy = cyb[own, :]
            px, mx = halves(cx)
            py, my = halves(cy)
            keep = 1.0 - jnp.abs(cx) - jnp.abs(cy)
            groups = []
            for g in range(blocks):
                row = h * blocks + g
                v = rows_v[row, k:k + chunk]
                to_west = jnp.where(small == 0, 0.0, pltpu.roll(v, 1, 1))
                to_east = jnp.where(small == width - 1, 0.0, pltpu.roll(v, width - 1, 1))
                groups.append(
                    v * keep + px * to_west + mx * to_east
                    + py * rows_v[(row + rows - 1) % rows, k:k + chunk] + my * rows_v[(row + 1) % rows, k:k + chunk]
                )
            for t, line in enumerate(swap_groups(groups, seg)):
                if 0 < t < blocks - 1:
                    send_f[t, h, k:k + chunk] = line.astype(BF16)
                else:
                    outer[min(t, 1), h, k:k + chunk] = line
        for b in lead[:2]:
            send_line(b, h)
    for b in lead[2:]:
        for h in range(lines):
            send_line(b, h)

    def release(now, position):
        ready = [p for p, when in HELD.get(position, {}).items() if when == now]
        if now == "start":
            late = [p for p, when in HELD.get(position, {}).items() if when != now]
            ready = [p for p in range(half) if p not in late]
        if len(ready) == half:
            for h in range(lines):
                send_line(wave[position], h)
        elif ready:
            hit = inside == ready[0]
            for p in ready[1:]:
                hit = hit | (inside == p)

            @pl.when(hit)
            def _():
                for h in range(lines):
                    send_line(wave[position], h)

    release("start", 4)
    for h in range(lines):
        send_line(wave[5], h)

    edge = jnp.zeros((comps, width), F32)
    for r in range(rows):
        v = rows_v[r]
        slot = (r % blocks) * seg + r // blocks
        edge = jnp.where(lane == slot, pltpu.roll(v, slot, 1), edge)
        edge = jnp.where(lane == slot + lines, pltpu.roll(v, (slot + lines + 1) % width, 1), edge)
    side_send[...] = edge.astype(BF16)
    sides = (west, east) if sect_tiles > 2 else (west,)
    for i, where in enumerate(sides):
        remote(side_send, side_recv.at[i], side_ss.at[0], side_rs.at[0], where).start()
    whole(side_recv.at[pl.ds(0, len(sides))], side_rs.at[0]).wait_recv()
    for k in range(0, comps, chunk):
        cx = cxb[pl.ds(pl.multiple_of(me * comps + k, 16), chunk), :]
        px, mx = halves(cx)
        from_east = side_recv[0, k:k + chunk].astype(F32)
        from_west = side_recv[len(sides) - 1, k:k + chunk].astype(F32)
        for h in range(lines):
            west_part = jnp.where(small % seg == 0, pltpu.roll(from_west, (width - lines - h) % width, 1), 0.0)
            east_part = jnp.where(small % seg == seg - 1, pltpu.roll(from_east, seg - 1 - h, 1), 0.0)
            send_f[0, h, k:k + chunk] = (outer[0, h, k:k + chunk] + px * west_part).astype(BF16)
            send_f[blocks - 1, h, k:k + chunk] = (outer[1, h, k:k + chunk] + mx * east_part).astype(BF16)
    release("start", 6)
    for h in range(lines):
        send_line(wave[7], h)

    level_id = lax.broadcasted_iota(jnp.int32, (levels, width), 0)
    level_lane = lax.broadcasted_iota(jnp.int32, (levels, width), 1)
    place = level_lane % seg
    folds = seg // (2 * lines)
    depth = levels // folds
    fold_place = place[:depth]

    def fold_slots():
        for f in range(2):
            for r in range(lines):
                for q in range(folds):
                    yield f, r, slice(q * depth, (q + 1) * depth), (q * 2 + f) * lines + r

    def send_state(state, step):
        west_pack = jnp.zeros((depth, width), F32)
        east_pack = jnp.zeros((depth, width), F32)
        for f, r, cut, slot in fold_slots():
            v = state[f, r, cut]
            west_pack = jnp.where(fold_place == slot, pltpu.roll(v, slot, 1), west_pack)
            east_pack = jnp.where(fold_place == slot, pltpu.roll(v, (slot + 1 - seg) % width, 1), east_pack)
        st_edge_send[step, 0] = west_pack
        st_edge_send[step, 1] = east_pack
        for i, where in enumerate((near_west, near_east)):
            remote(st_edge_send.at[step, i], st_edge_recv.at[step, i], ste_ss.at[0], ste_rs.at[step], where).start()

    def update(state, new, step, profile):
        rim_west = (mine_x == 0) & (spot == 0)
        rim_east = (mine_x == sect_tiles - 1) & (spot == blocks - 1)
        west_pack = jnp.where(rim_west, 0.0, st_edge_recv[step, 1])
        east_pack = jnp.where(rim_east, 0.0, st_edge_recv[step, 0])
        sides = {}
        for f, r, cut, slot in fold_slots():
            sides.setdefault((f, r), []).append((
                pltpu.roll(west_pack, (width - slot) % width, 1),
                pltpu.roll(east_pack, (width + seg - 1 - slot) % width, 1),
            ))
        for f in range(2):
            factor = -0.3 if f == 0 else 0.3
            for r in range(lines):
                v = state[f, r]
                w = jnp.where(place == 0, jnp.concatenate([x for x, _ in sides[f, r]]), pltpu.roll(v, 1, 1))
                e = jnp.where(place == seg - 1, jnp.concatenate([x for _, x in sides[f, r]]),
                              pltpu.roll(v, width - 1, 1))
                n = 0.0 if r == 0 else state[f, r - 1]
                s = 0.0 if r == lines - 1 else state[f, r + 1]
                n = pltpu.roll(jnp.where(level_lane >= width - seg, n, v), seg, 1)
                s = pltpu.roll(jnp.where(level_lane < seg, s, v), width - seg, 1)
                below = jnp.where(level_id == 0, 0.0, pltpu.roll(v, 1, 0))
                above = jnp.where(level_id == levels - 1, 0.0, pltpu.roll(v, levels - 1, 0))
                g = profile[f * levels:(f + 1) * levels, r * width:(r + 1) * width]
                new[f, r] = (v + 0.1 * (n + s + w + e - 4.0 * v)
                             + 0.1 * (above + below - 2.0 * v) + factor * g)

    loads[6].wait()
    for t in range(growth_v.shape[0] // LANES):
        column = column_of(growth_v[t * LANES:(t + 1) * LANES].reshape(1, LANES))
        grow_b[t * LANES:(t + 1) * LANES, :] = jnp.broadcast_to(0.1 * column, (LANES, width))

    def wind(state):
        out = []
        for r in range(lines):
            diff = state[0, r, 0:1, :] - state[1, r, 0:1, :]
            out.append(diff * diff)
        return out

    def fresh_part(rows_of, wind_rows, target, pair, quad):
        outs = []
        for r in range(lines):
            cut = slice(r * width, (r + 1) * width)
            f = cell_f[rows_of, cut].astype(F32)
            top = f + 0.3 * (f * pair[:, cut] - quad[:, cut]) + grow_b[rows_of, :] * wind_rows[r]
            out = (sea[r] * (top / (1.0 + 0.1 * (f * f)))).astype(BF16)
            target[rows_of, cut] = out
            outs.append(out)
        return outs

    others = pl.ds(0, blocks - 1)
    whole(c_all.at[others], c_recv.at[0]).wait_recv()
    for b in order:
        cxb[part(b), :] = jnp.broadcast_to(column_of(c_all[b, 0]), (comps, width))
        cyb[part(b), :] = jnp.broadcast_to(column_of(c_all[b, 1]), (comps, width))
    whole(swap_send.at[others], swap_rs.at[0]).wait_recv()
    whole(sea_send.at[pl.ds(0, cell_tiles - 1)], sea_rs.at[0]).wait_recv()

    wide_lane = lax.broadcasted_iota(jnp.int32, (8, width), 1)
    sea = []
    for h in range(lines):
        low = st_in[2 * h].astype(F32)
        high = st_in[2 * h + 1].astype(F32)
        st0[0, h] = jnp.where(level_lane < mid, low, pltpu.roll(high, mid, 1))
        st0[1, h] = jnp.where(level_lane < mid, pltpu.roll(low, mid, 1), high)
        low = jnp.broadcast_to(sea_in[2 * h], (8, width))
        high = jnp.broadcast_to(sea_in[2 * h + 1], (8, width))
        sea.append(jnp.where(wide_lane < mid, low, pltpu.roll(high, mid, 1))[0:1])
    send_state(st0, 0)

    loads[7].wait()
    loads[8].wait()

    near = half * comps
    span = stage_v.shape[2]
    spare = span - near
    for i in range(2):
        for x in range(2):
            stage_v[i, x, (1 - i) * near:(1 - i) * near + spare] = jnp.zeros((spare, cells), BF16)

    def stage(b):
        f = cell_f[part(b), :]
        wide = f.astype(F32)
        which = lax.div(b, half)
        rows_of = pl.ds(pl.multiple_of(which * spare + (b - which * half) * comps, 16), comps)
        stage_v[which, 0, rows_of, :] = f
        stage_v[which, 1, rows_of, :] = (wide * wide).astype(BF16)

    def products(rows_of, which):
        weights = quartet_v[rows_of, pl.ds(pl.multiple_of(which * (quartet_v.shape[1] - span), LANES), span)]
        return [jnp.dot(weights, stage_v[which, i], preferred_element_type=F32) for i in range(2)]

    def arrived(b):
        whole(cell_f.at[part(b), :], f_recv.at[b]).wait_recv()
        stage(b)

    stage(me)
    for b in order[half:][::-1]:
        arrived(b)
    for m in range(blocks):
        for i, x in enumerate(products(part(m), side)):
            total_v[i, part(m), :] = x
    for b in order[:half][::-1]:
        arrived(b)
    release("far", 6)

    wind_rows = wind(st0)
    first = jnp.zeros((comps, width), F32)
    last = jnp.zeros((comps, width), F32)
    for b in range(blocks):
        pair, quad = [total_v[i, part(b), :] + x
                      for i, x in enumerate(products(part(b), 1 - side))]
        outs = fresh_part(part(b), wind_rows, e1, pair, quad)
        for r in range(lines):
            slot = b * lines + r
            v = outs[r].astype(F32)
            first = jnp.where(lane % seg == slot, pltpu.roll(v, slot, 1), first)
            last = jnp.where(lane % seg == slot, pltpu.roll(v, (slot + 1 - seg) % width, 1), last)
    edge_send[0] = first.astype(BF16)
    edge_send[1] = last.astype(BF16)
    for i, where in enumerate((near_west, near_east)):
        remote(edge_send.at[i], edge_recv.at[i], edge_ss.at[0], edge_rs.at[0], where).start()
    release("edges", 6)

    west_rim = lane % seg == 0
    east_rim = lane % seg == seg - 1
    for b in range(blocks):
        cx = cxb[part(b), :]
        cy = cyb[part(b), :]
        px, mx = halves(cx)
        py, my = halves(cy)
        keep = 1.0 - jnp.abs(cx) - jnp.abs(cy)
        field = [e1[part(b), r * width:(r + 1) * width].astype(F32) for r in range(lines)]
        for r in range(lines):
            v = field[r]
            north = pltpu.roll(jnp.where(lane >= width - seg, field[r - 1], v), seg, 1)
            south = pltpu.roll(jnp.where(lane < seg, field[(r + 1) % lines], v), width - seg, 1)
            to_west = jnp.where(west_rim, 0.0, pltpu.roll(v, 1, 1))
            to_east = jnp.where(east_rim, 0.0, pltpu.roll(v, width - 1, 1))
            inner[part(b), r * width:(r + 1) * width] = (
                v * keep + px * to_west + mx * to_east + py * north + my * south
            )

    whole(st_edge_recv.at[0], ste_rs.at[0]).wait_recv()
    update(st0, st1, 0, jnp.dot(coupler_v[...], e1[...], preferred_element_type=F32))
    send_state(st1, 1)
    wind_rows = wind(st1)

    whole(edge_recv, edge_rs.at[0]).wait_recv()
    from_east = edge_recv[0].astype(F32)
    from_west = edge_recv[1].astype(F32)
    for b in range(blocks):
        px, mx = halves(cxb[part(b), :])
        for r in range(lines):
            slot = b * lines + r
            cut = slice(r * width, (r + 1) * width)
            beside = jnp.where(
                west_rim, px * pltpu.roll(from_west, (width - slot) % width, 1),
                mx * pltpu.roll(from_east, (width + seg - 1 - slot) % width, 1),
            )
            out = (inner[part(b), cut] + jnp.where(west_rim | east_rim, beside, 0.0)).astype(BF16)
            cell_f[part(b), cut] = out
            wide = out.astype(F32)
            cell_s[part(b), cut] = (wide * wide).astype(BF16)

    cuts = [(0, early.shape[0]), (early.shape[0], comps - early.shape[0])]

    def send_back(b, q):
        start, size = cuts[q]
        remote(e2.at[pl.ds(pl.multiple_of(b * comps + start, 16), size), :], ret.at[spot, pl.ds(start, size), :],
               ret_ss.at[0], ret_rs.at[q], block_id(b)).start()

    for b in [order[i] for i in FIRST] + [me]:
        weights = quartet_v[part(b), :]
        pair = jnp.dot(weights, cell_f[...], preferred_element_type=F32)
        quad = jnp.dot(weights, cell_s[...], preferred_element_type=F32)
        outs = fresh_part(part(b), wind_rows, e2, pair, quad)
        if b is not me:
            send_back(b, 0)
    for r, out in enumerate(outs):
        ret[spot, :, r * width:(r + 1) * width] = out
    whole(st_edge_recv.at[1], ste_rs.at[1]).wait_recv()
    update(st1, st2, 1, jnp.dot(coupler_v[...], e2[...], preferred_element_type=F32))
    for h in range(lines):
        atm = st2[0, h]
        oce = st2[1, h]
        st_back[2 * h] = jnp.where(level_lane < mid, atm, pltpu.roll(oce, mid, 1)).astype(BF16)
        st_back[2 * h + 1] = jnp.where(level_lane < mid, pltpu.roll(atm, mid, 1), oce).astype(BF16)

    for b in order:
        c = lax.div(b, lev_parts)
        core = lax.rem(b, lev_parts)
        remote(st_back.at[c, pl.ds(pl.multiple_of(core * lown, 16), lown), :], fin.at[spot], back_ss.at[0],
               back_rs.at[0], block_id(b)).start()
    fin[spot] = st_back[mine_c, my_levels, :]
    for b in [order[i] for i in SECOND]:
        send_back(b, 1)
    whole(ret.at[others, pl.ds(0, cuts[0][1]), :], ret_rs.at[0]).wait_recv()
    to_rows(ret, early, flat, 0)
    whole(fin.at[others], back_rs.at[0]).wait_recv()
    groups = swap_groups([fin[t].astype(F32) for t in range(blocks)], seg)
    for f, target in enumerate((atm_v, oce_v)):
        for r in range(tile_rows):
            target[:, r, :] = groups[f * tile_rows + r]
    whole(ret.at[others, pl.ds(*cuts[1]), :], ret_rs.at[1]).wait_recv()

    whole(send_f.at[others], f_send.at[0]).wait_send()
    whole(c_all.at[others], c_send.at[0]).wait_send()
    whole(swap_send.at[others], swap_ss.at[0]).wait_send()
    whole(sea_send.at[pl.ds(0, cell_tiles - 1)], sea_ss.at[0]).wait_send()
    for _ in sides:
        whole(side_send, side_ss.at[0]).wait_send()
    whole(edge_send, edge_ss.at[0]).wait_send()
    whole(st_edge_send, ste_ss.at[0]).wait_send()
    whole(ret.at[others], ret_ss.at[0]).wait_send()
    whole(fin.at[others], back_ss.at[0]).wait_send()


def to_rows(ret, target, flat, start):
    blocks = ret.shape[0]
    size, rows, width = target.shape
    lines = rows // blocks
    for h in range(lines):
        groups = swap_groups([
            ret[t, start:start + size, h * width:(h + 1) * width].astype(F32) for t in range(blocks)
        ], width // blocks)
        for g, line in enumerate(groups):
            flat[pl.ds(h * blocks + g, size, stride=rows), :] = line
    target[...] = flat[pl.ds(0, size * rows), :].reshape(size, rows, width).astype(BF16)


def unpack_kernel(ret, early, atm_v, oce_v, spec_out, atm_out, oce_out, flat, late, out_sem):
    start = early.shape[0]
    stores = [
        pltpu.make_async_copy(x, y, out_sem.at[i])
        for i, (x, y) in enumerate(((early, spec_out.at[pl.ds(0, start)]), (atm_v, atm_out), (oce_v, oce_out)))
    ]
    for store in stores:
        store.start()
    to_rows(ret, late, flat, start)
    stores.append(pltpu.make_async_copy(late, spec_out.at[pl.ds(start, late.shape[0])], out_sem.at[3]))
    stores[-1].start()
    for store in stores:
        store.wait()


def fused(
    spectrum, courant_x, courant_y, growth, quartet, coupler, atmosphere, ocean_state, sea_mask
):
    cell_tiles = lax.axis_size("cells")
    lev_parts = lax.axis_size("lev")
    sect_tiles = lax.axis_size("sect")
    blocks = cell_tiles * lev_parts
    comps, rows, width = spectrum.shape
    total = comps * blocks
    lines = rows // blocks
    lown, tile_rows, _ = atmosphere.shape
    levels = lown * lev_parts
    cells = lines * width
    first = comps // 16 * 2 // 3 * 16
    depth = levels // (width // blocks // (2 * lines))
    v = pltpu.VMEM
    dma = pltpu.SemaphoreType.DMA
    scratch = [
        v((comps, rows, width), BF16), v((blocks, lown, width), BF16), v((2, 1, comps), F32),
        v((total,), F32), v((total, total), BF16), v(coupler.shape, BF16),
        v((2, lown, tile_rows, width), F32), v(sea_mask.shape, jnp.int32),
        v((comps * rows, width), F32), v((rows, comps, width), F32),
        v((blocks, lines, comps, width), BF16), v((total, cells), BF16), v((total, cells), BF16),
        v((blocks, 2, 1, comps), F32),
        v((total, width), F32), v((total, width), F32), v((total, width), F32),
        v((comps, width), BF16), v((2, comps, width), BF16), v((2, comps, width), BF16), v((2, comps, width), BF16),
        v((total, cells), BF16), v((total, cells), BF16),
        v((blocks, lown, width), BF16), v((cell_tiles, levels, width), BF16),
        v((blocks, 1, width), F32), v((cell_tiles, 1, width), F32),
        v((2, lines, comps, width), F32), v((total, cells), F32),
        v((2, 2, -(-total // (2 * LANES)) * LANES, cells), BF16), v((2, total, cells), F32),
        v((2, lines, levels, width), F32), v((2, lines, levels, width), F32),
        v((2, lines, levels, width), F32),
        v((NSTEP, 2, depth, width), F32), v((NSTEP, 2, depth, width), F32),
        v((cell_tiles, levels, width), BF16),
        dma((9,)), dma((1,)), dma((blocks,)), dma((1,)), dma((1,)),
        dma((1,)), dma((1,)), dma((1,)), dma((1,)),
        dma((1,)), dma((1,)), dma((1,)), dma((1,)),
        dma((1,)), dma((1,)),
        dma((1,)), dma((NSTEP,)),
        dma((1,)), dma((2,)),
    ]
    anywhere = pl.BlockSpec(memory_space=pltpu.HBM)
    here = pl.BlockSpec(memory_space=pltpu.VMEM)
    column = jax.ShapeDtypeStruct(atmosphere.shape, F32)
    packed = pl.pallas_call(
        functools.partial(fused_kernel, cell_tiles, lev_parts, sect_tiles),
        out_shape=(
            v((blocks, comps, cells), BF16), v((first, rows, width), BF16),
            v(atmosphere.shape, F32), v(atmosphere.shape, F32),
        ),
        in_specs=[anywhere] * 9,
        out_specs=(here,) * 4,
        scratch_shapes=scratch,
        compiler_params=pltpu.CompilerParams(
            collective_id=0, has_side_effects=True, vmem_limit_bytes=33554432
        ),
    )(*(
        pltpu.with_memory_space_constraint(x, pltpu.HBM)
        for x in (spectrum, courant_x.reshape(1, comps), courant_y.reshape(1, comps),
                  growth, quartet, coupler, atmosphere, ocean_state, sea_mask)
    ))
    return pl.pallas_call(
        unpack_kernel,
        out_shape=(jax.ShapeDtypeStruct(spectrum.shape, BF16), column, column),
        in_specs=[here] * 4,
        out_specs=(anywhere,) * 3,
        scratch_shapes=[
            v(((comps - first) * rows, width), F32), v((comps - first, rows, width), BF16), dma((4,)),
        ],
        compiler_params=pltpu.CompilerParams(vmem_limit_bytes=33554432),
    )(*packed)


def fits_fused(mesh, spectrum, coupler, atmosphere):
    lev_parts = lax.axis_size("lev")
    cells = lax.axis_size("cells")
    blocks = cells * lev_parts
    comps, rows, width = spectrum.shape
    return (
        lev_parts == 2 and cells == 4 and lax.axis_size("sect") % 2 == 0 and width == LANES
        and comps % 16 == 0 and rows == 2 * blocks and (comps * blocks) % LANES == 0
        and atmosphere.shape[0] % 16 == 0 and 2 * atmosphere.shape[1] == blocks
    )


def solution(mesh):
    in_specs = (
        P(("cells", "lev"), "groups", "sect"),
        P(("cells", "lev")),
        P(("cells", "lev")),
        P(),
        P(),
        P(),
        P("lev", ("groups", "cells"), "sect"),
        P("lev", ("groups", "cells"), "sect"),
        P(("groups", "cells"), "sect"),
    )
    out_specs = (
        P(("cells", "lev"), "groups", "sect"),
        P("lev", ("groups", "cells"), "sect"),
        P("lev", ("groups", "cells"), "sect"),
    )

    def body(*args):
        if fits_fused(mesh, args[0], args[5], args[6]):
            return fused(*args)
        return on_device(*args)

    return jax.shard_map(
        body, mesh=mesh, in_specs=in_specs, out_specs=out_specs, check_vma=False
    )
```

```python
import functools

import jax
import jax.numpy as jnp
from jax import lax
from jax.experimental import pallas as pl
from jax.experimental.pallas import tpu as pltpu
from jax.sharding import PartitionSpec as P

NSTEP = 2
LANES = 128
HELD = {6: {3: "edges", 2: "far"}}
FIRST = (2, 4, 0, 5, 1, 3, 6)
SECOND = (0, 4, 1, 5, 2, 3, 6)
F32 = jnp.float32
BF16 = jnp.bfloat16


def from_root(block, axis, source):
    block = jnp.where(lax.axis_index(axis) == source, block, jnp.zeros_like(block))
    return lax.psum(block, axis)


def extended_2(block, sides, width, periodic):
    for axis, dim in sides:
        count = lax.axis_size(axis)
        forward = [(i, i + 1) for i in range(count - 1)]
        if periodic:
            forward.append((count - 1, 0))
        backward = [(target, source) for source, target in forward]
        low = lax.ppermute(
            lax.slice_in_dim(block, block.shape[dim] - width, None, axis=dim), axis, forward
        )
        high = lax.ppermute(lax.slice_in_dim(block, 0, width, axis=dim), axis, backward)
        block = jnp.concatenate([low, block, high], axis=dim)
    return block


def upwind(values, courant, before, after):
    return jnp.maximum(courant, 0.0) * (values - before) + jnp.minimum(courant, 0.0) * (
        after - values
    )


def on_device(
    spectrum, courant_x, courant_y, growth, quartet, coupler, atmosphere, ocean_state, sea_mask
):
    cell_tiles = lax.axis_size("cells")
    lev_parts = lax.axis_size("lev")
    blocks = cell_tiles * lev_parts
    comps_own, rows_all, row_width = spectrum.shape
    total_comps = comps_own * blocks
    cell_rows = rows_all // blocks
    level_count = coupler.shape[0] // 2
    row_start = lax.axis_index("lev") * cell_rows
    shift_x = courant_x[:, None, None]
    shift_y = courant_y[:, None, None]
    sea_rows = (
        lax.dynamic_slice_in_dim(sea_mask, row_start, cell_rows, 0)
        .astype(jnp.float32)
        .reshape(1, cell_rows * row_width)
    )
    growth_column = growth[:, None]
    forcing_sign = jnp.array([-0.3, 0.3], jnp.float32)[:, None, None, None]
    state = jnp.stack([atmosphere, ocean_state])
    energy = spectrum
    for counter in range(NSTEP):
        surface = from_root(state[:, 0], "lev", 0)
        surface_wind = surface[0] - surface[1]
        wind_rows = lax.dynamic_slice_in_dim(
            surface_wind * surface_wind, row_start, cell_rows, 0
        ).reshape(1, cell_rows * row_width)
        padded = extended_2(energy, (("sect", 2),), 1, True)
        values = padded[:, :, 1:-1].astype(jnp.float32)
        west_side = padded[:, :, :-2].astype(jnp.float32)
        east_side = padded[:, :, 2:].astype(jnp.float32)
        moved = values - upwind(values, shift_x, west_side, east_side)
        moved = moved - upwind(
            values, shift_y, jnp.roll(values, 1, axis=1), jnp.roll(values, -1, axis=1)
        )
        advected = moved.astype(jnp.bfloat16)
        pieces = advected.reshape(1, comps_own, blocks, cell_rows, row_width)
        on_cells = lax.all_to_all(pieces, ("cells", "lev"), split_axis=2, concat_axis=0, tiled=True)
        on_cells = on_cells.reshape(total_comps, cell_rows * row_width)
        cell_values = on_cells.astype(jnp.float32)
        paired = jnp.dot(quartet, on_cells, preferred_element_type=jnp.float32)
        squared = (cell_values * cell_values).astype(jnp.bfloat16)
        quad_square = jnp.dot(quartet, squared, preferred_element_type=jnp.float32)
        fresh = (
            cell_values
            + 0.3 * (cell_values * paired - quad_square)
            + 0.1 * growth_column * wind_rows
        ) / (1.0 + 0.1 * cell_values * cell_values)
        fresh = (fresh * sea_rows).astype(jnp.bfloat16)
        profile = jnp.dot(coupler, fresh, preferred_element_type=jnp.float32).reshape(
            2, level_count, cell_rows, row_width
        )
        forcing = lax.all_to_all(profile, "lev", split_axis=1, concat_axis=2, tiled=True)
        returned = fresh.reshape(blocks, comps_own, 1, cell_rows, row_width)
        returned = lax.all_to_all(
            returned, ("cells", "lev"), split_axis=0, concat_axis=2, tiled=True
        )
        energy = returned.reshape(comps_own, rows_all, row_width)
        extended = extended_2(state, (("lev", 1), ("cells", 2), ("sect", 3)), 1, False)
        middle = extended[:, 1:-1, 1:-1, 1:-1]
        lateral = (
            extended[:, 1:-1, 2:, 1:-1]
            + extended[:, 1:-1, :-2, 1:-1]
            + extended[:, 1:-1, 1:-1, 2:]
            + extended[:, 1:-1, 1:-1, :-2]
            - 4.0 * middle
        )
        upright = extended[:, 2:, 1:-1, 1:-1] + extended[:, :-2, 1:-1, 1:-1] - 2.0 * middle
        state = middle + 0.1 * lateral + 0.1 * upright + forcing_sign * forcing
    return (energy, state[0], state[1])


def column_of(row):
    n = row.shape[1]
    down = lax.broadcasted_iota(jnp.int32, (n, n), 0)
    across = lax.broadcasted_iota(jnp.int32, (n, n), 1)
    return jnp.sum(jnp.where(down == across, row, 0.0), axis=1, keepdims=True)


def swap_groups(vectors, seg):
    count = len(vectors)
    width = vectors[0].shape[1]
    group = lax.broadcasted_iota(jnp.int32, vectors[0].shape, 1) // seg
    dist = count // 2
    vectors = list(vectors)
    while dist:
        even = (group // dist) % 2 == 0
        for i in range(count):
            if (i // dist) % 2 == 0:
                x, y = vectors[i], vectors[i + dist]
                if 2 * dist * seg == width:
                    moved = pltpu.roll(jnp.where(even, y, x), dist * seg, 1)
                    vectors[i], vectors[i + dist] = jnp.where(even, x, moved), jnp.where(even, moved, y)
                else:
                    vectors[i] = jnp.where(even, x, pltpu.roll(y, dist * seg, 1))
                    vectors[i + dist] = jnp.where(even, pltpu.roll(x, width - dist * seg, 1), y)
        dist //= 2
    return vectors


def fused_kernel(
    cell_tiles, lev_parts, sect_tiles,
    spec_hbm, cx_hbm, cy_hbm, growth_hbm, quartet_hbm, coupler_hbm, atm_hbm, oce_hbm, sea_hbm,
    ret, early, atm_v, oce_v,
    spec_v, fin, c_v, growth_v, quartet_v, coupler_v, col_in, sea_v,
    flat, rows_v, send_f, cell_f, cell_s, c_all, cxb, cyb, grow_b,
    side_send, side_recv, edge_send, edge_recv, e1, e2,
    swap_send, st_in, sea_send, sea_in, outer, inner, stage_v, total_v, st0, st1, st2, st_edge_send, st_edge_recv, st_back,
    in_sem, f_send, f_recv, c_send, c_recv,
    side_ss, side_rs, edge_ss, edge_rs, swap_ss, swap_rs, sea_ss, sea_rs, back_ss, back_rs, ste_ss, ste_rs,
    ret_ss, ret_rs,
):
    blocks = cell_tiles * lev_parts
    comps, rows, width = spec_v.shape
    lines = rows // blocks
    lown = col_in.shape[1]
    tile_rows = col_in.shape[2]
    levels = lown * lev_parts
    cells = lines * width
    seg = width // blocks
    mid = width // 2
    mine_c = lax.axis_index("cells")
    mine_l = lax.axis_index("lev")
    mine_x = lax.axis_index("sect")
    me = mine_c * lev_parts + mine_l
    turned = lax.rem(mine_x, 2) == 1
    side = lax.div(mine_c, cell_tiles // 2)

    def tile_of(b):
        return jnp.where(turned, blocks - 1 - b, b)

    def mirrored(b):
        return jnp.where(side == 1, blocks - 1 - b, b)

    def block_id(b):
        return {"cells": lax.div(b, lev_parts), "lev": lax.rem(b, lev_parts)}

    spot = tile_of(me)
    inside = mirrored(me)
    west = {"sect": lax.rem(mine_x + sect_tiles - 1, sect_tiles)}
    east = {"sect": lax.rem(mine_x + 1, sect_tiles)}
    near_west = {
        **block_id(jnp.where(spot == 0, me, tile_of(spot - 1))),
        "sect": jnp.where(spot == 0, west["sect"], mine_x),
    }
    near_east = {
        **block_id(jnp.where(spot == blocks - 1, me, tile_of(spot + 1))),
        "sect": jnp.where(spot == blocks - 1, east["sect"], mine_x),
    }
    half = blocks // 2
    odd = lax.rem(inside, 2)
    across = [mirrored(blocks - 1 - i + (1 - 2 * (i % 2)) * -odd) for i in range(half)]
    mate = (1 - lax.div(inside, lev_parts)) * lev_parts
    mates = [mirrored(mate + k) for k in range(lev_parts)]
    order = across + mates + [mirrored(inside + 1 - 2 * odd)]

    def part(b):
        return pl.ds(pl.multiple_of(b * comps, 16), comps)

    def remote(src, dst, ss, rs, where):
        return pltpu.make_async_remote_copy(
            src_ref=src, dst_ref=dst, send_sem=ss, recv_sem=rs,
            device_id=where, device_id_type=pl.DeviceIdType.MESH,
        )

    loads = [
        pltpu.make_async_copy(a, b, in_sem.at[i])
        for i, (a, b) in enumerate([
            (spec_hbm, spec_v), (cx_hbm, c_v.at[0]), (cy_hbm, c_v.at[1]),
            (atm_hbm, col_in.at[0]), (oce_hbm, col_in.at[1]), (sea_hbm, sea_v),
            (growth_hbm, growth_v), (coupler_hbm, coupler_v), (quartet_hbm, quartet_v),
        ])
    ]

    def whole(ref, sem):
        return remote(ref, ref, sem, sem, {"lev": 1 - mine_l})
    for load in loads:
        load.start()

    barrier = pltpu.get_barrier_semaphore()
    for d in range(1, blocks):
        pl.semaphore_signal(barrier, inc=1, device_id=block_id(lax.rem(me + d, blocks)),
                            device_id_type=pl.DeviceIdType.MESH)
    for side_id in (west, east, near_west, near_east):
        pl.semaphore_signal(barrier, inc=1, device_id=side_id,
                            device_id_type=pl.DeviceIdType.MESH)

    my_levels = pl.ds(pl.multiple_of(mine_l * lown, 16), lown)

    def state_in(b):
        return remote(swap_send.at[tile_of(b)], st_in.at[mine_c, my_levels, :], swap_ss.at[0],
                      swap_rs.at[0], block_id(b))

    def sea_over(c):
        return remote(sea_send.at[tile_of(c * lev_parts + mine_l)], sea_in.at[mine_c], sea_ss.at[0],
                      sea_rs.at[0], {"cells": c})

    loads[3].wait()
    loads[4].wait()
    loads[5].wait()
    groups = [col_in[f, :, r, :] for f in range(2) for r in range(tile_rows)]
    for t, line in enumerate(swap_groups(groups, seg)):
        swap_send[t] = line.astype(BF16)
    groups = [jnp.broadcast_to(sea_v[r:r + 1, :].astype(F32), (8, width)) for r in range(tile_rows)]
    for t, line in enumerate(swap_groups(groups + [jnp.zeros((8, width), F32)] * tile_rows, seg)):
        sea_send[t] = line[0:1]
    st_in[mine_c, my_levels, :] = swap_send[spot]
    sea_in[mine_c] = sea_send[spot]

    pl.semaphore_wait(barrier, blocks + 3)
    wave = [mirrored(i) for i in sorted(range(blocks), key=lambda i: (abs(2 * i + 1 - blocks), -i))]

    for b in wave:
        @pl.when(b != me)
        def _():
            state_in(b).start()
    for dc in range(1, cell_tiles):
        sea_over(lax.rem(mine_c + dc, cell_tiles)).start()
    loads[1].wait()
    loads[2].wait()
    for b in order:
        remote(c_v, c_all.at[me], c_send.at[0], c_recv.at[0], block_id(b)).start()

    lane = lax.broadcasted_iota(jnp.int32, (comps, width), 1)
    loads[0].wait()
    flat[...] = spec_v[...].astype(F32).reshape(comps * rows, width)
    for r in range(rows):
        rows_v[r] = flat[pl.ds(r, comps, stride=rows), :]

    def halves(c):
        return jnp.maximum(c, 0.0), jnp.maximum(-c, 0.0)

    cxb[part(me), :] = jnp.broadcast_to(column_of(c_v[0]), (comps, width))
    cyb[part(me), :] = jnp.broadcast_to(column_of(c_v[1]), (comps, width))

    def send_line(b, h):
        t = tile_of(b)
        cut = slice(h * width, (h + 1) * width)

        @pl.when(b != me)
        def _():
            remote(send_f.at[t, h], cell_f.at[part(me), cut], f_send.at[0], f_recv.at[me],
                   block_id(b)).start()

        @pl.when(b == me)
        def _():
            cell_f[part(me), cut] = send_f[spot, h]

    chunk = comps
    small = lax.broadcasted_iota(jnp.int32, (chunk, width), 1)

    lead = [jnp.where(inside < lev_parts, wave[i], wave[j]) for i, j in ((1, 0), (3, 1), (0, 2), (2, 3))]
    for h in range(lines):
        for k in range(0, comps, chunk):
            own = pl.ds(pl.multiple_of(me * comps + k, 16), chunk)
            cx = cxb[own, :]
            cy = cyb[own, :]
            px, mx = halves(cx)
            py, my = halves(cy)
            keep = 1.0 - jnp.abs(cx) - jnp.abs(cy)
            groups = []
            for g in range(blocks):
                row = h * blocks + g
                v = rows_v[row, k:k + chunk]
                to_west = jnp.where(small == 0, 0.0, pltpu.roll(v, 1, 1))
                to_east = jnp.where(small == width - 1, 0.0, pltpu.roll(v, width - 1, 1))
                groups.append(
                    v * keep + px * to_west + mx * to_east
                    + py * rows_v[(row + rows - 1) % rows, k:k + chunk] + my * rows_v[(row + 1) % rows, k:k + chunk]
                )
            for t, line in enumerate(swap_groups(groups, seg)):
                if 0 < t < blocks - 1:
                    send_f[t, h, k:k + chunk] = line.astype(BF16)
                else:
                    outer[min(t, 1), h, k:k + chunk] = line
        for b in lead[:2]:
            send_line(b, h)
    for b in lead[2:]:
        for h in range(lines):
            send_line(b, h)

    def release(now, position):
        ready = [p for p, when in HELD.get(position, {}).items() if when == now]
        if now == "start":
            late = [p for p, when in HELD.get(position, {}).items() if when != now]
            ready = [p for p in range(half) if p not in late]
        if len(ready) == half:
            for h in range(lines):
                send_line(wave[position], h)
        elif ready:
            hit = inside == ready[0]
            for p in ready[1:]:
                hit = hit | (inside == p)

            @pl.when(hit)
            def _():
                for h in range(lines):
                    send_line(wave[position], h)

    release("start", 4)
    for h in range(lines):
        send_line(wave[5], h)

    edge = jnp.zeros((comps, width), F32)
    for r in range(rows):
        v = rows_v[r]
        slot = (r % blocks) * seg + r // blocks
        edge = jnp.where(lane == slot, pltpu.roll(v, slot, 1), edge)
        edge = jnp.where(lane == slot + lines, pltpu.roll(v, (slot + lines + 1) % width, 1), edge)
    side_send[...] = edge.astype(BF16)
    sides = (west, east) if sect_tiles > 2 else (west,)
    for i, where in enumerate(sides):
        remote(side_send, side_recv.at[i], side_ss.at[0], side_rs.at[0], where).start()
    whole(side_recv.at[pl.ds(0, len(sides))], side_rs.at[0]).wait_recv()
    for k in range(0, comps, chunk):
        cx = cxb[pl.ds(pl.multiple_of(me * comps + k, 16), chunk), :]
        px, mx = halves(cx)
        from_east = side_recv[0, k:k + chunk].astype(F32)
        from_west = side_recv[len(sides) - 1, k:k + chunk].astype(F32)
        for h in range(lines):
            west_part = jnp.where(small % seg == 0, pltpu.roll(from_west, (width - lines - h) % width, 1), 0.0)
            east_part = jnp.where(small % seg == seg - 1, pltpu.roll(from_east, seg - 1 - h, 1), 0.0)
            send_f[0, h, k:k + chunk] = (outer[0, h, k:k + chunk] + px * west_part).astype(BF16)
            send_f[blocks - 1, h, k:k + chunk] = (outer[1, h, k:k + chunk] + mx * east_part).astype(BF16)
    release("start", 6)
    for h in range(lines):
        send_line(wave[7], h)

    level_id = lax.broadcasted_iota(jnp.int32, (levels, width), 0)
    level_lane = lax.broadcasted_iota(jnp.int32, (levels, width), 1)
    place = level_lane % seg
    folds = seg // (2 * lines)
    depth = levels // folds
    fold_place = place[:depth]

    def fold_slots():
        for f in range(2):
            for r in range(lines):
                for q in range(folds):
                    yield f, r, slice(q * depth, (q + 1) * depth), (q * 2 + f) * lines + r

    def send_state(state, step):
        west_pack = jnp.zeros((depth, width), F32)
        east_pack = jnp.zeros((depth, width), F32)
        for f, r, cut, slot in fold_slots():
            v = state[f, r, cut]
            west_pack = jnp.where(fold_place == slot, pltpu.roll(v, slot, 1), west_pack)
            east_pack = jnp.where(fold_place == slot, pltpu.roll(v, (slot + 1 - seg) % width, 1), east_pack)
        st_edge_send[step, 0] = west_pack
        st_edge_send[step, 1] = east_pack
        for i, where in enumerate((near_west, near_east)):
            remote(st_edge_send.at[step, i], st_edge_recv.at[step, i], ste_ss.at[0], ste_rs.at[step], where).start()

    def update(state, new, step, profile):
        rim_west = (mine_x == 0) & (spot == 0)
        rim_east = (mine_x == sect_tiles - 1) & (spot == blocks - 1)
        west_pack = jnp.where(rim_west, 0.0, st_edge_recv[step, 1])
        east_pack = jnp.where(rim_east, 0.0, st_edge_recv[step, 0])
        sides = {}
        for f, r, cut, slot in fold_slots():
            sides.setdefault((f, r), []).append((
                pltpu.roll(west_pack, (width - slot) % width, 1),
                pltpu.roll(east_pack, (width + seg - 1 - slot) % width, 1),
            ))
        for f in range(2):
            factor = -0.3 if f == 0 else 0.3
            for r in range(lines):
                v = state[f, r]
                w = jnp.where(place == 0, jnp.concatenate([x for x, _ in sides[f, r]]), pltpu.roll(v, 1, 1))
                e = jnp.where(place == seg - 1, jnp.concatenate([x for _, x in sides[f, r]]),
                              pltpu.roll(v, width - 1, 1))
                n = 0.0 if r == 0 else state[f, r - 1]
                s = 0.0 if r == lines - 1 else state[f, r + 1]
                n = pltpu.roll(jnp.where(level_lane >= width - seg, n, v), seg, 1)
                s = pltpu.roll(jnp.where(level_lane < seg, s, v), width - seg, 1)
                below = jnp.where(level_id == 0, 0.0, pltpu.roll(v, 1, 0))
                above = jnp.where(level_id == levels - 1, 0.0, pltpu.roll(v, levels - 1, 0))
                g = profile[f * levels:(f + 1) * levels, r * width:(r + 1) * width]
                new[f, r] = (v + 0.1 * (n + s + w + e - 4.0 * v)
                             + 0.1 * (above + below - 2.0 * v) + factor * g)

    loads[6].wait()
    for t in range(growth_v.shape[0] // LANES):
        column = column_of(growth_v[t * LANES:(t + 1) * LANES].reshape(1, LANES))
        grow_b[t * LANES:(t + 1) * LANES, :] = jnp.broadcast_to(0.1 * column, (LANES, width))

    def wind(state):
        out = []
        for r in range(lines):
            diff = state[0, r, 0:1, :] - state[1, r, 0:1, :]
            out.append(diff * diff)
        return out

    def fresh_part(rows_of, wind_rows, target, pair, quad):
        outs = []
        for r in range(lines):
            cut = slice(r * width, (r + 1) * width)
            f = cell_f[rows_of, cut].astype(F32)
            top = f + 0.3 * (f * pair[:, cut] - quad[:, cut]) + grow_b[rows_of, :] * wind_rows[r]
            out = (sea[r] * (top / (1.0 + 0.1 * (f * f)))).astype(BF16)
            target[rows_of, cut] = out
            outs.append(out)
        return outs

    others = pl.ds(0, blocks - 1)
    whole(c_all.at[others], c_recv.at[0]).wait_recv()
    for b in order:
        cxb[part(b), :] = jnp.broadcast_to(column_of(c_all[b, 0]), (comps, width))
        cyb[part(b), :] = jnp.broadcast_to(column_of(c_all[b, 1]), (comps, width))
    whole(swap_send.at[others], swap_rs.at[0]).wait_recv()
    whole(sea_send.at[pl.ds(0, cell_tiles - 1)], sea_rs.at[0]).wait_recv()

    wide_lane = lax.broadcasted_iota(jnp.int32, (8, width), 1)
    sea = []
    for h in range(lines):
        low = st_in[2 * h].astype(F32)
        high = st_in[2 * h + 1].astype(F32)
        st0[0, h] = jnp.where(level_lane < mid, low, pltpu.roll(high, mid, 1))
        st0[1, h] = jnp.where(level_lane < mid, pltpu.roll(low, mid, 1), high)
        low = jnp.broadcast_to(sea_in[2 * h], (8, width))
        high = jnp.broadcast_to(sea_in[2 * h + 1], (8, width))
        sea.append(jnp.where(wide_lane < mid, low, pltpu.roll(high, mid, 1))[0:1])
    send_state(st0, 0)

    loads[7].wait()
    loads[8].wait()

    near = half * comps
    span = stage_v.shape[2]
    spare = span - near
    for i in range(2):
        for x in range(2):
            stage_v[i, x, (1 - i) * near:(1 - i) * near + spare] = jnp.zeros((spare, cells), BF16)

    def stage(b):
        f = cell_f[part(b), :]
        wide = f.astype(F32)
        which = lax.div(b, half)
        rows_of = pl.ds(pl.multiple_of(which * spare + (b - which * half) * comps, 16), comps)
        stage_v[which, 0, rows_of, :] = f
        stage_v[which, 1, rows_of, :] = (wide * wide).astype(BF16)

    def products(rows_of, which):
        weights = quartet_v[rows_of, pl.ds(pl.multiple_of(which * (quartet_v.shape[1] - span), LANES), span)]
        return [jnp.dot(weights, stage_v[which, i], preferred_element_type=F32) for i in range(2)]

    def arrived(b):
        whole(cell_f.at[part(b), :], f_recv.at[b]).wait_recv()
        stage(b)

    stage(me)
    for b in order[half:][::-1]:
        arrived(b)
    for m in range(blocks):
        for i, x in enumerate(products(part(m), side)):
            total_v[i, part(m), :] = x
    for b in order[:half][::-1]:
        arrived(b)
    release("far", 6)

    wind_rows = wind(st0)
    first = jnp.zeros((comps, width), F32)
    last = jnp.zeros((comps, width), F32)
    for b in range(blocks):
        pair, quad = [total_v[i, part(b), :] + x
                      for i, x in enumerate(products(part(b), 1 - side))]
        outs = fresh_part(part(b), wind_rows, e1, pair, quad)
        for r in range(lines):
            slot = b * lines + r
            v = pltpu.roll(outs[r].astype(F32), slot, 1)
            first = jnp.where(lane % seg == slot, v, first)
            last = jnp.where(lane % seg == (slot + seg - 1) % seg, v, last)
    edge_send[0] = first.astype(BF16)
    edge_send[1] = last.astype(BF16)
    for i, where in enumerate((near_west, near_east)):
        remote(edge_send.at[i], edge_recv.at[i], edge_ss.at[0], edge_rs.at[0], where).start()
    release("edges", 6)

    west_rim = lane % seg == 0
    east_rim = lane % seg == seg - 1
    for b in range(blocks):
        cx = cxb[part(b), :]
        cy = cyb[part(b), :]
        px, mx = halves(cx)
        py, my = halves(cy)
        keep = 1.0 - jnp.abs(cx) - jnp.abs(cy)
        field = [e1[part(b), r * width:(r + 1) * width].astype(F32) for r in range(lines)]
        for r in range(lines):
            v = field[r]
            north = pltpu.roll(jnp.where(lane >= width - seg, field[r - 1], v), seg, 1)
            south = pltpu.roll(jnp.where(lane < seg, field[(r + 1) % lines], v), width - seg, 1)
            to_west = jnp.where(west_rim, 0.0, pltpu.roll(v, 1, 1))
            to_east = jnp.where(east_rim, 0.0, pltpu.roll(v, width - 1, 1))
            inner[part(b), r * width:(r + 1) * width] = (
                v * keep + px * to_west + mx * to_east + py * north + my * south
            )

    whole(st_edge_recv.at[0], ste_rs.at[0]).wait_recv()
    update(st0, st1, 0, jnp.dot(coupler_v[...], e1[...], preferred_element_type=F32))
    send_state(st1, 1)
    wind_rows = wind(st1)

    whole(edge_recv, edge_rs.at[0]).wait_recv()
    from_east = edge_recv[0].astype(F32)
    from_west = edge_recv[1].astype(F32)
    for b in range(blocks):
        px, mx = halves(cxb[part(b), :])
        for r in range(lines):
            slot = b * lines + r
            cut = slice(r * width, (r + 1) * width)
            beside = jnp.where(
                west_rim, px * pltpu.roll(from_west, (width - slot - seg + 1) % width, 1),
                mx * pltpu.roll(from_east, (width + seg - 1 - slot) % width, 1),
            )
            out = (inner[part(b), cut] + jnp.where(west_rim | east_rim, beside, 0.0)).astype(BF16)
            cell_f[part(b), cut] = out
            wide = out.astype(F32)
            cell_s[part(b), cut] = (wide * wide).astype(BF16)

    cuts = [(0, early.shape[0]), (early.shape[0], comps - early.shape[0])]

    def send_back(b, q):
        start, size = cuts[q]
        remote(e2.at[pl.ds(pl.multiple_of(b * comps + start, 16), size), :], ret.at[spot, pl.ds(start, size), :],
               ret_ss.at[0], ret_rs.at[q], block_id(b)).start()

    for b in [order[i] for i in FIRST] + [me]:
        weights = quartet_v[part(b), :]
        pair = jnp.dot(weights, cell_f[...], preferred_element_type=F32)
        quad = jnp.dot(weights, cell_s[...], preferred_element_type=F32)
        outs = fresh_part(part(b), wind_rows, e2, pair, quad)
        if b is not me:
            send_back(b, 0)
    for r, out in enumerate(outs):
        ret[spot, :, r * width:(r + 1) * width] = out
    whole(st_edge_recv.at[1], ste_rs.at[1]).wait_recv()
    update(st1, st2, 1, jnp.dot(coupler_v[...], e2[...], preferred_element_type=F32))
    for h in range(lines):
        atm = st2[0, h]
        oce = st2[1, h]
        st_back[2 * h] = jnp.where(level_lane < mid, atm, pltpu.roll(oce, mid, 1)).astype(BF16)
        st_back[2 * h + 1] = jnp.where(level_lane < mid, pltpu.roll(atm, mid, 1), oce).astype(BF16)

    for b in order:
        c = lax.div(b, lev_parts)
        core = lax.rem(b, lev_parts)
        remote(st_back.at[c, pl.ds(pl.multiple_of(core * lown, 16), lown), :], fin.at[spot], back_ss.at[0],
               back_rs.at[0], block_id(b)).start()
    fin[spot] = st_back[mine_c, my_levels, :]
    for b in [order[i] for i in SECOND]:
        send_back(b, 1)
    whole(ret.at[others, pl.ds(0, cuts[0][1]), :], ret_rs.at[0]).wait_recv()
    to_rows(ret, early, flat, 0)
    whole(fin.at[others], back_rs.at[0]).wait_recv()
    groups = swap_groups([fin[t].astype(F32) for t in range(blocks)], seg)
    for f, target in enumerate((atm_v, oce_v)):
        for r in range(tile_rows):
            target[:, r, :] = groups[f * tile_rows + r]
    whole(ret.at[others, pl.ds(*cuts[1]), :], ret_rs.at[1]).wait_recv()

    whole(send_f.at[others], f_send.at[0]).wait_send()
    whole(c_all.at[others], c_send.at[0]).wait_send()
    whole(swap_send.at[others], swap_ss.at[0]).wait_send()
    whole(sea_send.at[pl.ds(0, cell_tiles - 1)], sea_ss.at[0]).wait_send()
    for _ in sides:
        whole(side_send, side_ss.at[0]).wait_send()
    whole(edge_send, edge_ss.at[0]).wait_send()
    whole(st_edge_send, ste_ss.at[0]).wait_send()
    whole(ret.at[others], ret_ss.at[0]).wait_send()
    whole(fin.at[others], back_ss.at[0]).wait_send()


def to_rows(ret, target, flat, start):
    blocks = ret.shape[0]
    size, rows, width = target.shape
    lines = rows // blocks
    for h in range(lines):
        groups = swap_groups([
            ret[t, start:start + size, h * width:(h + 1) * width].astype(F32) for t in range(blocks)
        ], width // blocks)
        for g, line in enumerate(groups):
            flat[pl.ds(h * blocks + g, size, stride=rows), :] = line
    target[...] = flat[pl.ds(0, size * rows), :].reshape(size, rows, width).astype(BF16)


def unpack_kernel(ret, early, atm_v, oce_v, spec_out, atm_out, oce_out, flat, late, out_sem):
    start = early.shape[0]
    stores = [
        pltpu.make_async_copy(x, y, out_sem.at[i])
        for i, (x, y) in enumerate(((early, spec_out.at[pl.ds(0, start)]), (atm_v, atm_out), (oce_v, oce_out)))
    ]
    for store in stores:
        store.start()
    to_rows(ret, late, flat, start)
    stores.append(pltpu.make_async_copy(late, spec_out.at[pl.ds(start, late.shape[0])], out_sem.at[3]))
    stores[-1].start()
    for store in stores:
        store.wait()


def fused(
    spectrum, courant_x, courant_y, growth, quartet, coupler, atmosphere, ocean_state, sea_mask
):
    cell_tiles = lax.axis_size("cells")
    lev_parts = lax.axis_size("lev")
    sect_tiles = lax.axis_size("sect")
    blocks = cell_tiles * lev_parts
    comps, rows, width = spectrum.shape
    total = comps * blocks
    lines = rows // blocks
    lown, tile_rows, _ = atmosphere.shape
    levels = lown * lev_parts
    cells = lines * width
    first = comps // 16 * 2 // 3 * 16
    depth = levels // (width // blocks // (2 * lines))
    v = pltpu.VMEM
    dma = pltpu.SemaphoreType.DMA
    scratch = [
        v((comps, rows, width), BF16), v((blocks, lown, width), BF16), v((2, 1, comps), F32),
        v((total,), F32), v((total, total), BF16), v(coupler.shape, BF16),
        v((2, lown, tile_rows, width), F32), v(sea_mask.shape, jnp.int32),
        v((comps * rows, width), F32), v((rows, comps, width), F32),
        v((blocks, lines, comps, width), BF16), v((total, cells), BF16), v((total, cells), BF16),
        v((blocks, 2, 1, comps), F32),
        v((total, width), F32), v((total, width), F32), v((total, width), F32),
        v((comps, width), BF16), v((2, comps, width), BF16), v((2, comps, width), BF16), v((2, comps, width), BF16),
        v((total, cells), BF16), v((total, cells), BF16),
        v((blocks, lown, width), BF16), v((cell_tiles, levels, width), BF16),
        v((blocks, 1, width), F32), v((cell_tiles, 1, width), F32),
        v((2, lines, comps, width), F32), v((total, cells), F32),
        v((2, 2, -(-total // (2 * LANES)) * LANES, cells), BF16), v((2, total, cells), F32),
        v((2, lines, levels, width), F32), v((2, lines, levels, width), F32),
        v((2, lines, levels, width), F32),
        v((NSTEP, 2, depth, width), F32), v((NSTEP, 2, depth, width), F32),
        v((cell_tiles, levels, width), BF16),
        dma((9,)), dma((1,)), dma((blocks,)), dma((1,)), dma((1,)),
        dma((1,)), dma((1,)), dma((1,)), dma((1,)),
        dma((1,)), dma((1,)), dma((1,)), dma((1,)),
        dma((1,)), dma((1,)),
        dma((1,)), dma((NSTEP,)),
        dma((1,)), dma((2,)),
    ]
    anywhere = pl.BlockSpec(memory_space=pltpu.HBM)
    here = pl.BlockSpec(memory_space=pltpu.VMEM)
    column = jax.ShapeDtypeStruct(atmosphere.shape, F32)
    packed = pl.pallas_call(
        functools.partial(fused_kernel, cell_tiles, lev_parts, sect_tiles),
        out_shape=(
            v((blocks, comps, cells), BF16), v((first, rows, width), BF16),
            v(atmosphere.shape, F32), v(atmosphere.shape, F32),
        ),
        in_specs=[anywhere] * 9,
        out_specs=(here,) * 4,
        scratch_shapes=scratch,
        compiler_params=pltpu.CompilerParams(
            collective_id=0, has_side_effects=True, vmem_limit_bytes=33554432
        ),
    )(*(
        pltpu.with_memory_space_constraint(x, pltpu.HBM)
        for x in (spectrum, courant_x.reshape(1, comps), courant_y.reshape(1, comps),
                  growth, quartet, coupler, atmosphere, ocean_state, sea_mask)
    ))
    return pl.pallas_call(
        unpack_kernel,
        out_shape=(jax.ShapeDtypeStruct(spectrum.shape, BF16), column, column),
        in_specs=[here] * 4,
        out_specs=(anywhere,) * 3,
        scratch_shapes=[
            v(((comps - first) * rows, width), F32), v((comps - first, rows, width), BF16), dma((4,)),
        ],
        compiler_params=pltpu.CompilerParams(vmem_limit_bytes=33554432),
    )(*packed)


def fits_fused(mesh, spectrum, coupler, atmosphere):
    lev_parts = lax.axis_size("lev")
    cells = lax.axis_size("cells")
    blocks = cells * lev_parts
    comps, rows, width = spectrum.shape
    return (
        lev_parts == 2 and cells == 4 and lax.axis_size("sect") % 2 == 0 and width == LANES
        and comps % 16 == 0 and rows == 2 * blocks and (comps * blocks) % LANES == 0
        and atmosphere.shape[0] % 16 == 0 and 2 * atmosphere.shape[1] == blocks
    )


def solution(mesh):
    in_specs = (
        P(("cells", "lev"), "groups", "sect"),
        P(("cells", "lev")),
        P(("cells", "lev")),
        P(),
        P(),
        P(),
        P("lev", ("groups", "cells"), "sect"),
        P("lev", ("groups", "cells"), "sect"),
        P(("groups", "cells"), "sect"),
    )
    out_specs = (
        P(("cells", "lev"), "groups", "sect"),
        P("lev", ("groups", "cells"), "sect"),
        P("lev", ("groups", "cells"), "sect"),
    )

    def body(*args):
        if fits_fused(mesh, args[0], args[5], args[6]):
            return fused(*args)
        return on_device(*args)

    return jax.shard_map(
        body, mesh=mesh, in_specs=in_specs, out_specs=out_specs, check_vma=False
    )
```
